128 devices in a mesh: node: 32 (over z, x, core), freq: 4 (over y).
Axes of the slice: x: 4, y: 4, z: 4, core: 2. Of those that a mesh axis runs over, the one named last changes fastest.
Arguments:
- receiver_gathers: float32 [256, 393216], P('node', 'freq'), may hold values from -6 to 6
- fourier_estimate: float32 [256, 2, 256, 384], P(('node', 'freq')), may hold values from -6 to 6
- random_projector: float32 [384, 48], replicated, may hold values from -0.3125 to 0.3125
- release_sample: int32 [384], P('freq'), may hold values from 0 to 393215, as said below
Outputs:
- deblended: float32 [256, 2, 256, 384], P(('node', 'freq'))
- misfit_signal: float32 [256, 393216], P('node', 'freq')
The draws below stay inside these ranges and needn't reach their ends.
Inputs may be any that keep to these rules, and one draw needn't show every extreme that they name: `release_sample`: shot s fires at a sample of [s * 1024, (s + 1) * 1024).
All inputs are finite; a program needn't handle non-finite values.
Results may differ from the reference program's by a relative error of at most 0.0003.
Values sent between devices are 32-bit elements; how exact they have to be, the bound alone decides.
No kernel may reach another device: no remote copies, remote signals or barrier semaphores. Data moves between devices by JAX's collectives and lax.ppermute only.
A program may use at most 128 MiB of HBM per device.

```python
import math
from functools import partial
import jax
import jax.numpy as jnp
from jax import lax

SOURCE_COUNT = 384
RECEIVER_COUNT = 256
LISTEN_SPAN = 4096
SOURCE_SPACING = 1024
RANK = 48
FREQS = 256
LENGTH = 393216


def draw_release_sample(key, part):
    random_dither = jax.random.randint(jax.random.fold_in(key, 17), (SOURCE_COUNT,), 0, SOURCE_SPACING, dtype=jnp.int32)
    return jnp.arange(SOURCE_COUNT, dtype=jnp.int32) * SOURCE_SPACING + random_dither


def level_of(key, dims, pieces, low, top_value):
    factor_of = 1.0
    for dim, blocks in pieces:
        steps = jax.random.uniform(jax.random.fold_in(jax.random.fold_in(key, 6), dim), (blocks,), jnp.float32, low / len(pieces), top_value / len(pieces))
        factor_of = factor_of * jnp.repeat(jnp.exp(steps), dims[dim] // blocks).reshape((-1,) + (1,) * (len(dims) - 1 - dim))
    return factor_of


def centred(own_key, dims, width, most, shards=(), held_as=jnp.bfloat16):
    entries = jax.random.normal(own_key, dims, jnp.float32) * width
    if len(shards) > 0:
        entries = level_of(own_key, dims, shards, -0.22, 0.18) * entries
    return jnp.clip(entries, min=-most, max=most).astype(held_as)


def setup_inputs(seed: int = 0) -> dict:
    splits = jax.random.split(jax.random.key(seed), 5)
    receiver_gathers = centred(splits[0], (RECEIVER_COUNT, LENGTH), 1.0, 6.0, ((0, 32), (1, 4)), jnp.float32)
    fourier_estimate = centred(splits[1], (FREQS, 2, RECEIVER_COUNT, SOURCE_COUNT), 1.0, 6.0, ((0, 128),), jnp.float32)
    random_projector = centred(splits[2], (SOURCE_COUNT, RANK), SOURCE_COUNT ** -0.5, 0.3125, (), jnp.float32)
    release_sample = draw_release_sample(jax.random.fold_in(splits[4], 71), 0)
    return {"receiver_gathers": receiver_gathers, "fourier_estimate": fourier_estimate, "random_projector": random_projector, "release_sample": release_sample}


relaxation = 0.25
ridge_scale = 0.001
highest = lax.Precision.HIGHEST

def dft_table(bin_count, length):
    spectral_columns = lax.iota(jnp.int32, bin_count) + 1
    sample_times = lax.iota(jnp.int32, length)
    phases = spectral_columns[:, None] * sample_times[None, :] % LISTEN_SPAN
    phase_angles = 2.0 * math.pi / LISTEN_SPAN * phases.astype(jnp.float32)
    inverse_root = 1.0 / math.sqrt(LISTEN_SPAN)
    return jnp.stack([jnp.cos(phase_angles) * inverse_root, -jnp.sin(phase_angles) * inverse_root], axis=1)

def inner_product(former, latter):
    return lax.dot_general(former, latter, (((1,), (1,)), ((), ())), precision=highest)

def outer_product(former, latter):
    return lax.dot_general(former, latter, (((0,), (0,)), ((), ())), precision=highest)

def reduce_rank(matrix, random_projector):
    real_part = matrix[0]
    imag_part = matrix[1]
    rank_count = random_projector.shape[1]
    proj_real = lax.dot_general(random_projector, real_part, (((0,), (1,)), ((), ())), precision=highest)
    proj_imag = lax.dot_general(random_projector, imag_part, (((0,), (1,)), ((), ())), precision=highest)
    gram_real = inner_product(proj_real, proj_real) + inner_product(proj_imag, proj_imag)
    gram_imag = inner_product(proj_real, proj_imag) - inner_product(proj_imag, proj_real)
    coef_real = jnp.dot(proj_real, real_part, precision=highest) + jnp.dot(proj_imag, imag_part, precision=highest)
    coef_imag = jnp.dot(proj_real, imag_part, precision=highest) - jnp.dot(proj_imag, real_part, precision=highest)
    system = jnp.concatenate([jnp.concatenate([gram_real, -gram_imag], 1), jnp.concatenate([gram_imag, gram_real], 1)], 0)
    ridge_shift = ridge_scale * jnp.trace(gram_real) / rank_count
    system = system + ridge_shift * jnp.eye(2 * rank_count, dtype=system.dtype)
    factor = jnp.linalg.cholesky(system)
    right_side = jnp.concatenate([coef_real, coef_imag], 0)
    halfway = lax.linalg.triangular_solve(factor, right_side, left_side=True, lower=True)
    solved = lax.linalg.triangular_solve(factor, halfway, left_side=True, lower=True, transpose_a=True)
    solution_real = solved[:rank_count]
    solution_imag = solved[rank_count:]
    low_real = outer_product(proj_real, solution_real) - outer_product(proj_imag, solution_imag)
    low_imag = outer_product(proj_real, solution_imag) + outer_product(proj_imag, solution_real)
    return jnp.stack([low_real, low_imag])

def reference(receiver_gathers, fourier_estimate, random_projector, release_sample):
    dft_rows = dft_table(FREQS, LISTEN_SPAN).reshape(2 * FREQS, LISTEN_SPAN)
    zero_extended = jnp.zeros((RECEIVER_COUNT, SOURCE_COUNT * SOURCE_SPACING + LISTEN_SPAN), jnp.float32)

    def place(record, source_label):
        source_start_moment = release_sample[source_label].astype(jnp.int32)
        coeffs = lax.dynamic_index_in_dim(fourier_estimate, source_label, 3, keepdims=False).reshape(2 * FREQS, RECEIVER_COUNT)
        window = 2.0 * lax.dot_general(coeffs, dft_rows, (((0,), (0,)), ((), ())), precision=highest)
        before = lax.dynamic_slice(record, (jnp.int32(0), source_start_moment), (RECEIVER_COUNT, LISTEN_SPAN))
        record = lax.dynamic_update_slice(record, before + window, (jnp.int32(0), source_start_moment))
        return (record, None)
    mixed_signal, unused = lax.scan(place, zero_extended, jnp.arange(SOURCE_COUNT, dtype=jnp.int32))
    misfit_signal = receiver_gathers - mixed_signal[:, :SOURCE_COUNT * SOURCE_SPACING]
    extended = jnp.concatenate([misfit_signal, jnp.zeros((RECEIVER_COUNT, LISTEN_SPAN), jnp.float32)], 1)

    def window_cut(source_label):
        source_start_moment = release_sample[source_label].astype(jnp.int32)
        window_piece = lax.dynamic_slice(extended, (jnp.int32(0), source_start_moment), (RECEIVER_COUNT, LISTEN_SPAN))
        return lax.dot_general(dft_rows, window_piece, (((1,), (1,)), ((), ())), precision=highest)
    adjoint_operator = lax.map(window_cut, jnp.arange(SOURCE_COUNT, dtype=jnp.int32))
    adjoint_operator = jnp.transpose(adjoint_operator.reshape(SOURCE_COUNT, FREQS, 2, RECEIVER_COUNT), (1, 2, 3, 0))
    updated = fourier_estimate + relaxation * adjoint_operator
    deblended = lax.map(partial(reduce_rank, random_projector=random_projector), updated)
    return (deblended, misfit_signal)
```

```python
import functools
import math

import jax
import jax.numpy as jnp
from jax import lax
from jax.experimental import pallas as pl
from jax.experimental.pallas import tpu as pltpu
from jax.sharding import PartitionSpec as P

SPAN = 4096
FRAME = 1024
RANK = 48
HALO = 4
SHOTS = 96
NODES = 8
EXT = SHOTS + 2 * HALO
FRAMES = SHOTS + HALO
GROUP = 128
RELAX = 0.25
RIDGE = 0.001
highest = lax.Precision.HIGHEST
f32 = jnp.float32
bf16 = jnp.bfloat16


def split(x):
    hi = x.astype(bf16)
    lo = (x - hi.astype(f32)).astype(bf16)
    return hi, lo


def pack_kernel(x_ref, o_ref):
    groups, count = x_ref.shape[0], x_ref.shape[1]
    x = x_ref[...].reshape(groups * count * NODES, 4 * SHOTS)
    lane = lax.broadcasted_iota(jnp.int32, (groups * count * NODES, 128), 1)
    for q in range(4):
        y = pltpu.roll(x, (HALO - SHOTS * q) % (4 * SHOTS), axis=1)[:, :128]
        if q == 0:
            y = jnp.where(lane < HALO, 0.0, y)
        if q == 3:
            y = jnp.where(lane >= HALO + SHOTS, 0.0, y)
        y = y.reshape(groups, count, NODES, 128)
        for g in range(groups):
            o_ref[:, q, g] = y[g]


def pack(x):
    step = 8
    return pl.pallas_call(
        pack_kernel,
        grid=(32 // step,),
        in_specs=[pl.BlockSpec((4, step, NODES, 4 * SHOTS), lambda i: (0, i, 0, 0))],
        out_specs=pl.BlockSpec((step, 4, 4, NODES, 128), lambda i: (i, 0, 0, 0, 0)),
        out_shape=jax.ShapeDtypeStruct((32, 4, 4, NODES, 128), f32),
        name="pack",
    )(x)


def signal_kernel(
    d_ref, last_ref, recv_ref, cos_ref, sin_ref, fh_ref, fl_ref, ah_ref, al_ref, head_ref, gath_ref,
    mis_ref, send_ref,
    c_ref, g_ref, q_ref, dr_ref, lh_ref, ll_ref, mh_ref, ml_ref, sp_ref, in_sem, out_sem,
):
    rows_ext = EXT * NODES
    rows_frames = FRAMES * NODES
    rows_local = SHOTS * NODES

    @pl.loop(0, SHOTS)
    def _(f):
        pltpu.make_async_copy(
            gath_ref.at[:, pl.ds(pl.multiple_of(f * FRAME, FRAME), FRAME)],
            g_ref.at[pl.ds(pl.multiple_of(f * NODES, NODES), NODES), :],
            in_sem,
        ).start()

    for f in range(HALO):
        g_ref[rows_local + f * NODES : rows_local + (f + 1) * NODES, :] = head_ref[
            :, f * FRAME : (f + 1) * FRAME
        ]

    @pl.loop(0, EXT)
    def _(s):
        dr_ref[pl.ds(pl.multiple_of(s * NODES, NODES), NODES), :] = jnp.full((NODES, 128), d_ref[s], jnp.int32)

    @pl.loop(0, NODES)
    def _(n):
        for j in range(2):
            re = recv_ref[pl.ds(2 * j * NODES + n, GROUP, stride=32), :].T[:EXT]
            im = recv_ref[pl.ds((2 * j + 1) * NODES + n, GROUP, stride=32), :].T[:EXT]
            co = cos_ref[:, j * 128 : (j + 1) * 128]
            si = sin_ref[:, j * 128 : (j + 1) * 128]
            c_ref[pl.ds(2 * j * rows_ext + n, EXT, stride=NODES), :] = 2.0 * (re * co + im * si)
            c_ref[pl.ds((2 * j + 1) * rows_ext + n, EXT, stride=NODES), :] = 2.0 * (im * co - re * si)

    step = 80
    parity = 1.0 - 2.0 * (lax.broadcasted_iota(jnp.int32, (step, 128), 1) & 1).astype(f32)

    @pl.loop(0, rows_frames // step)
    def _(i):
        base = pl.multiple_of(i * step, NODES)

        def shot(m, a):
            return c_ref[pl.ds(pl.multiple_of(a * rows_ext + base + (HALO - m) * NODES, NODES), step), :]

        parts = [
            (shot(0, 0) - shot(2, 0)) - parity * (shot(1, 1) - shot(3, 1)),
            (shot(0, 1) - shot(2, 1)) + parity * (shot(1, 0) - shot(3, 0)),
            (shot(0, 2) + shot(2, 2)) - parity * (shot(1, 2) + shot(3, 2)),
            (shot(0, 3) + shot(2, 3)) - parity * (shot(1, 3) + shot(3, 3)),
        ]
        for a in range(4):
            hi, lo = split(parts[a])
            lh_ref[pl.ds(base, step), a * 128 : (a + 1) * 128] = hi
            ll_ref[pl.ds(base, step), a * 128 : (a + 1) * 128] = lo

    @pl.loop(0, rows_ext // 64)
    def _(i):
        base = pl.multiple_of(i * 64, 64)
        target = pl.multiple_of(rows_frames + base, 32)
        for a in range(4):
            hi, lo = split(c_ref[pl.ds(pl.multiple_of(a * rows_ext + base, 64), 64), :])
            lh_ref[pl.ds(target, 64), a * 128 : (a + 1) * 128] = hi
            ll_ref[pl.ds(target, 64), a * 128 : (a + 1) * 128] = lo

    def product(hi, lo, th, tl):
        out = jnp.dot(hi, th, preferred_element_type=f32)
        out += jnp.dot(lo, th, preferred_element_type=f32)
        return out + jnp.dot(hi, tl, preferred_element_type=f32)

    width = 256
    half = rows_ext // 2

    @pl.loop(0, 2 * (FRAME // width))
    def _(i):
        m = i // (FRAME // width)
        c = i % (FRAME // width)
        col = pl.multiple_of(c * width, width)
        row = pl.multiple_of(rows_frames + m * half, 16)
        out = product(
            lh_ref[pl.ds(row, half), :], ll_ref[pl.ds(row, half), :],
            fh_ref[:, pl.ds(col, width)], fl_ref[:, pl.ds(col, width)],
        )
        dest = pl.multiple_of(m * half, 16)
        lane = lax.broadcasted_iota(jnp.int32, (half, 128), 1)
        shift = dr_ref[pl.ds(dest, half), :] - col
        for k in range(width // 128):
            q_ref[pl.ds(dest, half), pl.ds(pl.multiple_of(col + k * 128, 128), 128)] = jnp.where(
                lane + k * 128 < shift, out[:, k * 128 : (k + 1) * 128], 0.0
            )

    pltpu.make_async_copy(g_ref.at[pl.ds(0, rows_local), :], g_ref.at[pl.ds(0, rows_local), :], in_sem).wait()
    half_f = rows_frames // 2

    @pl.loop(0, 2 * (FRAME // width))
    def _(i):
        m = i // (FRAME // width)
        c = i % (FRAME // width)
        col = pl.multiple_of(c * width, width)
        row = pl.multiple_of(m * half_f, 16)
        out = product(
            lh_ref[pl.ds(row, half_f), :], ll_ref[pl.ds(row, half_f), :],
            fh_ref[:, pl.ds(col, width)], fl_ref[:, pl.ds(col, width)],
        )
        cols = pl.ds(col, width)
        lead = pl.multiple_of(row + HALO * NODES, 16)
        g_ref[pl.ds(row, half_f), cols] = (
            g_ref[pl.ds(row, half_f), cols] - out + q_ref[pl.ds(lead, half_f), cols] - q_ref[pl.ds(row, half_f), cols]
        )

    @pl.when(last_ref[0] > 0)
    def _():
        g_ref[rows_local:rows_frames, :] = jnp.zeros((HALO * NODES, FRAME), f32)

    @pl.loop(0, SHOTS)
    def _(f):
        pltpu.make_async_copy(
            g_ref.at[pl.ds(pl.multiple_of(f * NODES, NODES), NODES), :],
            mis_ref.at[:, pl.ds(pl.multiple_of(f * FRAME, FRAME), FRAME)],
            out_sem,
        ).start()

    @pl.loop(0, rows_frames // 32)
    def _(i):
        base = pl.multiple_of(i * 32, 32)
        hi, lo = split(g_ref[pl.ds(base, 32), :])
        mh_ref[pl.ds(base, 32), :] = hi
        ml_ref[pl.ds(base, 32), :] = lo

    @pl.loop(0, rows_local // 32)
    def _(i):
        base = pl.multiple_of(i * 32, 32)
        lead = pl.multiple_of(base + HALO * NODES, 32)
        target = pl.multiple_of(rows_frames + base, 32)
        shift = dr_ref[pl.ds(lead, 32), :]
        lane = lax.broadcasted_iota(jnp.int32, (32, 128), 1)
        for k in range(FRAME // 128):
            cols = slice(k * 128, (k + 1) * 128)
            diff = jnp.where(lane + k * 128 < shift, g_ref[pl.ds(lead, 32), cols] - g_ref[pl.ds(base, 32), cols], 0.0)
            hi, lo = split(diff)
            mh_ref[pl.ds(target, 32), cols] = hi
            ml_ref[pl.ds(target, 32), cols] = lo

    total = rows_frames + rows_local
    quarter = total // 7

    @pl.loop(0, 7 * 2)
    def _(i):
        row = pl.multiple_of((i // 2) * quarter, 32)
        col = pl.multiple_of((i % 2) * 256, 256)
        out = product(
            mh_ref[pl.ds(row, quarter), :], ml_ref[pl.ds(row, quarter), :],
            ah_ref[:, pl.ds(col, 256)], al_ref[:, pl.ds(col, 256)],
        )
        for k in range(2):
            place = pl.multiple_of(((i % 2) * 2 + k) * total + row, 32)
            sp_ref[pl.ds(place, quarter), :] = out[:, k * 128 : (k + 1) * 128]

    sign = 1.0 - 2.0 * (lax.broadcasted_iota(jnp.int32, (SHOTS, 128), 1) & 1).astype(f32)

    @pl.loop(0, NODES)
    def _(n):
        def frame(m, a):
            return sp_ref[pl.ds(a * total + m * NODES + n, SHOTS, stride=NODES), :]

        def edge(a):
            return sp_ref[pl.ds(a * total + rows_frames + n, SHOTS, stride=NODES), :]

        parts = [
            (frame(0, 0) - frame(2, 0)) + sign * (frame(1, 1) - frame(3, 1)) + edge(0),
            (frame(0, 1) - frame(2, 1)) - sign * (frame(1, 0) - frame(3, 0)) + edge(1),
            (frame(0, 2) + frame(2, 2)) - sign * (frame(1, 2) + frame(3, 2)) + edge(2),
            (frame(0, 3) + frame(2, 3)) - sign * (frame(1, 3) + frame(3, 3)) + edge(3),
        ]
        outs = []
        for j in range(2):
            co = RELAX * cos_ref[HALO : HALO + SHOTS, j * 128 : (j + 1) * 128]
            si = RELAX * sin_ref[HALO : HALO + SHOTS, j * 128 : (j + 1) * 128]
            re, im = parts[2 * j], parts[2 * j + 1]
            outs += [re * co - im * si, im * co + re * si]
        for a in range(3):
            block = jnp.concatenate([outs[a], outs[3][32 * a : 32 * a + 32]], 0).T
            send_ref[pl.ds(a * NODES + n, GROUP, stride=24), :] = block

    pltpu.make_async_copy(g_ref.at[pl.ds(0, rows_local), :], g_ref.at[pl.ds(0, rows_local), :], out_sem).wait()


def signal(dither, last, recv, cos_t, sin_t, tables, head, gathers):
    vmem = pl.BlockSpec(memory_space=pltpu.VMEM)
    smem = pl.BlockSpec(memory_space=pltpu.SMEM)
    hbm = pl.BlockSpec(memory_space=pltpu.HBM)
    rows_ext, rows_frames, rows_local = EXT * NODES, FRAMES * NODES, SHOTS * NODES
    return pl.pallas_call(
        signal_kernel,
        in_specs=[smem, smem, vmem, vmem, vmem, vmem, vmem, vmem, vmem, vmem, hbm],
        out_specs=[hbm, vmem],
        out_shape=[
            jax.ShapeDtypeStruct((NODES, SHOTS * FRAME), f32),
            jax.ShapeDtypeStruct((GROUP * 24, 128), f32),
        ],
        scratch_shapes=[
            pltpu.VMEM((4 * rows_ext, 128), f32),
            pltpu.VMEM((rows_frames, FRAME), f32),
            pltpu.VMEM((rows_ext, FRAME), f32),
            pltpu.VMEM((rows_ext, 128), jnp.int32),
            pltpu.VMEM((rows_frames + rows_ext, 512), bf16),
            pltpu.VMEM((rows_frames + rows_ext, 512), bf16),
            pltpu.VMEM((rows_frames + rows_local, FRAME), bf16),
            pltpu.VMEM((rows_frames + rows_local, FRAME), bf16),
            pltpu.VMEM((4 * (rows_frames + rows_local), 128), f32),
            pltpu.SemaphoreType.DMA,
            pltpu.SemaphoreType.DMA,
        ],
        compiler_params=pltpu.CompilerParams(vmem_limit_bytes=56 << 20),
        name="signal",
    )(dither, last, recv, cos_t, sin_t, *tables, head, gathers)


def rank_kernel(recv_ref, est_ref, wr_ref, wi_ref, out_ref, a_ref, y_ref, c_ref, s_ref):
    lane = lax.broadcasted_iota(jnp.int32, (NODES, 128), 1)
    chunk = lane // 32

    @pl.loop(0, 32)
    def _(p):
        rows = pl.ds(pl.multiple_of(p * NODES, NODES), NODES)
        extras = []
        for a in range(3):
            t = []
            for q in range(4):
                tile = recv_ref[pl.ds(pl.multiple_of((p * 4 + q) * 24 + a * NODES, NODES), NODES), :]
                t.append(pltpu.roll(tile, (96 * q) % 128, axis=1) if q else tile)
            v = [
                jnp.where(lane < 96, t[0], t[1]),
                jnp.where(lane < 64, t[1], t[2]),
                jnp.where(lane < 32, t[2], t[3]),
            ]
            for i in range(3):
                cols = slice(i * 128, (i + 1) * 128)
                a_ref[a, rows, cols] = est_ref[a, rows, cols] + v[i]
            e = jnp.where(chunk == 0, t[3], jnp.where(chunk == 1, t[2], jnp.where(chunk == 2, t[1], t[0])))
            extras.append(pltpu.roll(e, 32 * (a + 1), axis=1))
        for i in range(3):
            cols = slice(i * 128, (i + 1) * 128)
            x = extras[(4 * i) % 3]
            for k in range(1, 4):
                x = jnp.where(chunk == k, extras[(4 * i + k) % 3], x)
            a_ref[3, rows, cols] = est_ref[3, rows, cols] + x

    dot = functools.partial(jnp.dot, precision=highest, preferred_element_type=f32)

    def dot_t(x, y):
        return lax.dot_general(x, y, (((0,), (0,)), ((), ())), precision=highest, preferred_element_type=f32)

    def dot_nt(x, y):
        return lax.dot_general(x, y, (((1,), (1,)), ((), ())), precision=highest, preferred_element_type=f32)

    lane_r = lax.broadcasted_iota(jnp.int32, (64, 128), 1)
    row_r = lax.broadcasted_iota(jnp.int32, (64, 128), 0)
    flip = jnp.where(lane_r < 64, 1.0, -1.0).astype(f32)
    diagonal = (lane_r == row_r) & (row_r < RANK)
    systems = []
    for j in range(2):
        re, im = a_ref[2 * j], a_ref[2 * j + 1]
        y = dot(re, wr_ref[...]) + dot(im, wi_ref[...])
        y_ref[j] = y
        ya = y[:, :128]
        g = dot_t(ya, ya)
        g = g[:64] + flip * pltpu.roll(g[64:], 64, axis=1)
        trace = jnp.sum(jnp.where(diagonal, g, 0.0))
        g = jnp.where(diagonal, g + RIDGE * trace / RANK, g)
        eye = jnp.where(diagonal, 1.0, 0.0).astype(f32)
        systems.append([g[: RANK], eye[: RANK]])
        dr = dot_t(ya, re)
        di = dot_t(ya, im)
        c_ref[j, :64] = dr[:64] + di[64:]
        c_ref[j, 64:] = di[:64] - dr[64:]

    neg = jnp.where(lax.broadcasted_iota(jnp.int32, (1, 128), 1) < 64, -1.0, 1.0).astype(f32)
    row_i = lax.broadcasted_iota(jnp.int32, (RANK, 128), 0)
    for k in range(RANK - 1):
        start = ((k + 1) // 8) * 8
        for j in range(2):
            g, w = systems[j]
            gk, wk = g[k : k + 1], w[k : k + 1]
            inv = 1.0 / gk[:, k : k + 1]
            gk, wk = gk * inv, wk * inv
            gs, ws = neg * pltpu.roll(gk, 64, axis=1), neg * pltpu.roll(wk, 64, axis=1)
            below = g[start:]
            live = row_i[start:] > k
            cr = jnp.where(live, below[:, k : k + 1], 0.0)
            ci = jnp.where(live, below[:, 64 + k : 65 + k], 0.0)
            low_g = below - (cr * gk + ci * gs)
            low_w = w[start:] - (cr * wk + ci * ws)
            if start:
                low_g = jnp.concatenate([g[:start], low_g], 0)
                low_w = jnp.concatenate([w[:start], low_w], 0)
            systems[j] = [low_g, low_w]

    for j in range(2):
        g, w = systems[j]
        d = jnp.sum(jnp.where(diagonal[:RANK], g, 0.0), axis=1, keepdims=True)
        w = w * lax.rsqrt(d)
        w = jnp.concatenate([w, jnp.zeros((16, 128), f32)], 0)
        zero = jnp.zeros((64, 128), f32)
        left = jnp.concatenate([flip * w, pltpu.roll(w, 64, axis=1)], 0)
        v = dot(left, c_ref[j])
        big = jnp.concatenate(
            [
                jnp.concatenate([w, zero], 1), jnp.concatenate([zero, w], 1),
                jnp.concatenate([zero, -w], 1), jnp.concatenate([w, zero], 1),
            ], 0,
        )
        z = dot_nt(y_ref[j], big)
        out_ref[2 * j] = dot(z[:, :128], v)
        out_ref[2 * j + 1] = dot(z[:, 128:], v)


def rank_reduce(recv, est, wr, wi):
    vmem = pl.BlockSpec(memory_space=pltpu.VMEM)
    return pl.pallas_call(
        rank_kernel,
        in_specs=[vmem] * 4,
        out_specs=vmem,
        out_shape=jax.ShapeDtypeStruct((4, 256, 384), f32),
        scratch_shapes=[
            pltpu.VMEM((4, 256, 384), f32),
            pltpu.VMEM((2, 256, 256), f32),
            pltpu.VMEM((2, 128, 384), f32),
            pltpu.VMEM((8, 128), f32),
        ],
        compiler_params=pltpu.CompilerParams(vmem_limit_bytes=56 << 20),
        name="rank",
    )(recv, est, wr, wi)


def table(rows_first):
    shape = (512, FRAME) if rows_first else (FRAME, 512)
    row = lax.broadcasted_iota(jnp.int32, shape, 0 if rows_first else 1)
    time = lax.broadcasted_iota(jnp.int32, shape, 1 if rows_first else 0)
    block = row // 128
    k = 2 * (row % 128) + block // 2 + 1
    phase = (k * time + (block % 2) * (SPAN // 4)) % SPAN
    value = jnp.cos(2.0 * math.pi / SPAN * phase.astype(f32)) / math.sqrt(SPAN)
    hi = lax.reduce_precision(value, 8, 7)
    return hi.astype(bf16), (value - hi).astype(bf16)


def shards(receiver_gathers, fourier_estimate, random_projector, release_sample):
    q = lax.axis_index("freq")
    est = fourier_estimate.reshape(4, 32, NODES, 4 * SHOTS)
    send = pack(est).reshape(GROUP, 32, 128)
    recv = lax.all_to_all(send, ("node", "freq"), split_axis=0, concat_axis=0, tiled=True)

    up = [(0, 1), (1, 2), (2, 3)]
    down = [(1, 0), (2, 1), (3, 2)]
    head = lax.ppermute(receiver_gathers[:, : HALO * FRAME], "freq", down)
    release_before = lax.ppermute(release_sample[SHOTS - HALO :], "freq", up)
    release_after = lax.ppermute(release_sample[:HALO], "freq", down)
    dither = jnp.concatenate([release_before, release_sample, release_after]) % FRAME
    src = lax.iota(jnp.int32, 256)
    k = 2 * (src % 128) + src // 128 + 1
    angle = 2.0 * math.pi / SPAN * (k[None, :] * dither[:, None] % SPAN).astype(f32)
    cos_t, sin_t = jnp.cos(angle), jnp.sin(angle)
    tables = table(True) + table(False)
    last = (q == 3).astype(jnp.int32).reshape(1)
    misfit, back = signal(dither, last, recv.reshape(GROUP * 32, 128), cos_t, sin_t, tables, head, receiver_gathers)

    arrived = lax.all_to_all(
        back.reshape(GROUP, 24, 128), ("node", "freq"), split_axis=0, concat_axis=0, tiled=True
    )
    omega = jnp.pad(random_projector, ((0, 0), (0, 16)))
    zero = jnp.zeros_like(omega)
    wr = jnp.concatenate([omega, zero, zero, omega], 1)
    wi = jnp.concatenate([zero, omega, -omega, zero], 1)
    low = rank_reduce(arrived.reshape(GROUP * 24, 128), fourier_estimate.reshape(4, 256, 384), wr, wi)
    return low.reshape(2, 2, 256, 384), misfit


def solution(mesh):
    return jax.shard_map(
        shards,
        mesh=mesh,
        in_specs=(P("node", "freq"), P(("node", "freq"), None, None, None), P(), P("freq")),
        out_specs=(P(("node", "freq"), None, None, None), P("node", "freq")),
        check_vma=False,
    )
```

```python
import functools
import math

import jax
import jax.numpy as jnp
from jax import lax
from jax.experimental import pallas as pl
from jax.experimental.pallas import tpu as pltpu
from jax.sharding import PartitionSpec as P


SPAN = 4096
FRAME = 1024
RANK = 48
HALO = 4
SHOTS = 96
NODES = 8
EXT = SHOTS + 2 * HALO
FRAMES = SHOTS + HALO
GROUP = 128
ROWS = 26
ORDER = (0, 2, 1, 3)
RELAX = 0.25
RIDGE = 0.001
highest = lax.Precision.HIGHEST
f32 = jnp.float32
bf16 = jnp.bfloat16


def split(x):
    hi = x.astype(bf16)
    lo = (x - hi.astype(f32)).astype(bf16)
    return hi, lo


def pack_kernel(x_ref, o_ref):
    count = x_ref.shape[1]
    lane = lax.broadcasted_iota(jnp.int32, (NODES, 128), 1)
    node = lax.broadcasted_iota(jnp.int32, (NODES, 128), 0)
    slot = lane // 32
    own = slot == node % 4

    def turn(v, by):
        return pltpu.roll(v, by % 128, axis=1) if by % 128 else v

    @pl.loop(0, count)
    def _(p):
        x = [[x_ref[a, p, :, i * 128 : (i + 1) * 128] for i in range(3)] for a in range(4)]
        edges = jnp.zeros((NODES, 128), f32)
        for k in range(3):
            for a in range(4):
                moved = turn(x[a][k], 32 * k + 8 * a - (92 - 32 * k))
                edges = jnp.where((slot == k) & ((lane // 8) % 4 == a), moved, edges)
        turned = [turn(edges, 32 * r) for r in range(4)]

        def spread(k):
            v = turned[(0 - k) % 4]
            for m in range(1, 4):
                v = jnp.where(slot == m, turned[(m - k) % 4], v)
            return jnp.where(own, v, 0.0)

        spreads = [spread(k) for k in range(3)]
        zero = jnp.zeros((NODES, 128), f32)
        for q in range(4):
            base = (p * 4 + q) * ROWS
            for a in range(3):
                if q == 0:
                    main = x[a][0]
                elif q == 3:
                    main = turn(x[a][2], 96)
                else:
                    main = jnp.where(lane < 32 * q, turn(x[a][q - 1], 32 * q), turn(x[a][q], 32 * q))
                m = 3 * q + a
                rest = turn(x[3][m // 4], 32 * (3 - m % 4))
                o_ref[pl.ds(base + NODES * a, NODES), :] = jnp.where(lane < SHOTS, main, rest)
            before = spreads[q - 1] if q > 0 else zero
            after = spreads[q] if q < 3 else zero
            halo = jnp.where(lane % 8 < 4, before, after)
            halo = halo + pltpu.roll(halo, 1, axis=0)
            halo = halo + pltpu.roll(halo, 2, axis=0)
            o_ref[pl.ds(base + 24, 1), :] = halo[3:4]
            o_ref[pl.ds(base + 25, 1), :] = halo[7:8]


def pack(x):
    step = 8
    return pl.pallas_call(
        pack_kernel,
        grid=(32 // step,),
        in_specs=[pl.BlockSpec((4, step, NODES, 4 * SHOTS), lambda i: (0, i, 0, 0))],
        out_specs=pl.BlockSpec((step * 4 * ROWS, 128), lambda i: (i, 0)),
        out_shape=jax.ShapeDtypeStruct((GROUP * ROWS, 128), f32),
        compiler_params=pltpu.CompilerParams(vmem_limit_bytes=56 << 20),
        name="pack",
    )(x)


def product(hi, lo, th, tl):
    return jnp.dot(
        jnp.concatenate([hi, lo, hi], 1), jnp.concatenate([th, th, tl], 0), preferred_element_type=f32
    )


def signal_kernel(
    d_ref, last_ref, recv_ref, cos_ref, sin_ref, fh_hbm, fl_hbm, ah_hbm, al_hbm, head_ref, gath_ref,
    mis_ref, send_hbm,
    c_ref, g_ref, q_ref, h_ref, lh_ref, ll_ref, mh_ref, ml_ref, sp_ref, w_ref, send_ref,
    fh_ref, fl_ref, ah_ref, al_ref, in_sem, head_sem, out_sem, send_sem, table_sem,
):
    rows_ext = EXT * NODES
    rows_frames = FRAMES * NODES
    rows_local = SHOTS * NODES
    local = SHOTS * FRAME
    loads = [
        pltpu.make_async_copy(src, dst, table_sem.at[i])
        for i, (src, dst) in enumerate(
            [(fh_hbm, fh_ref), (fl_hbm, fl_ref), (ah_hbm, ah_ref), (al_hbm, al_ref)]
        )
    ]
    loads[0].start()
    loads[1].start()
    fetch = pltpu.make_async_copy(gath_ref, g_ref.at[:, pl.ds(0, local)], in_sem)
    fetch.start()
    fetch_head = pltpu.make_async_copy(head_ref, g_ref.at[:, pl.ds(local, HALO * FRAME)], head_sem)
    fetch_head.start()
    loads[2].start()
    loads[3].start()

    for i in range(2):
        h_ref[i * 128 : (i + 1) * 128, :] = recv_ref[pl.ds(24 + i, GROUP, stride=ROWS), :].T

    @pl.loop(0, NODES)
    def _(n):
        blocks = [recv_ref[pl.ds(a * NODES + n, GROUP, stride=ROWS), :].T for a in range(3)]
        planes = [b[:SHOTS] for b in blocks] + [jnp.concatenate([b[SHOTS:] for b in blocks], 0)]
        halo = pl.multiple_of(n * 32, 32)
        pieces = [
            (HALO, SHOTS, planes),
            (0, HALO, [h_ref[pl.ds(halo + 8 * a, HALO), :] for a in range(4)]),
            (HALO + SHOTS, HALO, [h_ref[pl.ds(halo + 8 * a + HALO, HALO), :] for a in range(4)]),
        ]
        for first, size, values in pieces:
            for j in range(2):
                re, im = values[2 * j], values[2 * j + 1]
                co = cos_ref[first : first + size, j * 128 : (j + 1) * 128]
                si = sin_ref[first : first + size, j * 128 : (j + 1) * 128]
                place = 2 * j * rows_ext + first * NODES + n
                c_ref[pl.ds(place, size, stride=NODES), :] = 2.0 * (re * co + im * si)
                c_ref[pl.ds(place + rows_ext, size, stride=NODES), :] = 2.0 * (im * co - re * si)

    step = 80
    parity = 1.0 - 2.0 * (lax.broadcasted_iota(jnp.int32, (step, 128), 1) & 1).astype(f32)

    @pl.loop(0, rows_frames // step)
    def _(i):
        base = pl.multiple_of(i * step, NODES)

        def shot(m, a):
            return c_ref[pl.ds(pl.multiple_of(a * rows_ext + base + (HALO - m) * NODES, NODES), step), :]

        parts = [
            (shot(0, 0) - shot(2, 0)) - parity * (shot(1, 1) - shot(3, 1)),
            (shot(0, 1) - shot(2, 1)) + parity * (shot(1, 0) - shot(3, 0)),
            (shot(0, 2) + shot(2, 2)) - parity * (shot(1, 2) + shot(3, 2)),
            (shot(0, 3) + shot(2, 3)) - parity * (shot(1, 3) + shot(3, 3)),
        ]
        for a in range(4):
            hi, lo = split(parts[a])
            lh_ref[pl.ds(base, step), ORDER[a] * 128 : (ORDER[a] + 1) * 128] = hi
            ll_ref[pl.ds(base, step), ORDER[a] * 128 : (ORDER[a] + 1) * 128] = lo

    @pl.loop(0, rows_ext // 64)
    def _(i):
        base = pl.multiple_of(i * 64, 64)
        target = pl.multiple_of(rows_frames + base, 32)
        for a in range(4):
            hi, lo = split(c_ref[pl.ds(pl.multiple_of(a * rows_ext + base, 64), 64), :])
            lh_ref[pl.ds(target, 64), ORDER[a] * 128 : (ORDER[a] + 1) * 128] = hi
            ll_ref[pl.ds(target, 64), ORDER[a] * 128 : (ORDER[a] + 1) * 128] = lo

    width = 256
    lane = lax.broadcasted_iota(jnp.int32, (NODES, width), 1)
    mirror = 127 - lax.broadcasted_iota(jnp.int32, (NODES, 128), 1)

    def reverse(x):
        tiles = [x[:, i : i + 128] for i in range(0, x.shape[1], 128)]
        return jnp.concatenate([jnp.take_along_axis(t, mirror, axis=1) for t in tiles[::-1]], 1)

    def pair(row, size, c):
        cols = pl.ds(pl.multiple_of(c * width, width), width)
        rows = pl.ds(row, size)
        return (
            product(lh_ref[rows, :256], ll_ref[rows, :256], fh_ref[0, :, cols], fl_ref[0, :, cols]),
            product(lh_ref[rows, 256:], ll_ref[rows, 256:], fh_ref[1, :, cols], fl_ref[1, :, cols]),
        )

    def columns(c):
        return pl.multiple_of(512 + c * width, width), pl.multiple_of(256 - c * width, width)

    loads[0].wait()
    loads[1].wait()
    half_ext = rows_ext // 2

    @pl.loop(0, 4)
    def _(i):
        m, c = i // 2, i % 2
        even, odd = pair(pl.multiple_of(rows_frames + m * half_ext, 16), half_ext, c)
        upper, lower = columns(c)
        for s in range(EXT // 2):
            rows = slice(s * NODES, (s + 1) * NODES)
            place = pl.ds(pl.multiple_of(m * half_ext + s * NODES, NODES), NODES)
            d = d_ref[m * (EXT // 2) + s]
            q_ref[place, pl.ds(upper, width)] = jnp.where(lane < d - upper, even[rows] + odd[rows], 0.0)
            q_ref[place, pl.ds(lower, width)] = jnp.where(lane < d - lower, reverse(even[rows] - odd[rows]), 0.0)

    fetch.wait()
    fetch_head.wait()
    half_frames = rows_frames // 2

    @pl.loop(0, 4)
    def _(i):
        m, c = i // 2, i % 2
        even, odd = pair(pl.multiple_of(m * half_frames, 16), half_frames, c)
        upper, lower = columns(c)
        for f in range(FRAMES // 2):
            rows = slice(f * NODES, (f + 1) * NODES)
            first = m * half_frames + f * NODES
            now = pl.ds(pl.multiple_of(first, NODES), NODES)
            ahead = pl.ds(pl.multiple_of(first + HALO * NODES, NODES), NODES)
            start = (m * (FRAMES // 2) + f) * FRAME
            for col, out in ((upper, even[rows] + odd[rows]), (lower, reverse(even[rows] - odd[rows]))):
                cols = pl.ds(col, width)
                place = pl.ds(pl.multiple_of(start + col, width), width)
                g_ref[:, place] = g_ref[:, place] - out + (q_ref[ahead, cols] - q_ref[now, cols])

    @pl.when(last_ref[0] > 0)
    def _():
        g_ref[:, local:] = jnp.zeros((NODES, HALO * FRAME), f32)

    store = pltpu.make_async_copy(g_ref.at[:, pl.ds(0, local)], mis_ref, out_sem)
    store.start()

    wide = lax.broadcasted_iota(jnp.int32, (NODES, FRAME), 1)

    def put(row, first, second):
        folded = []
        for x in (first, second):
            back = reverse(x[:, :512])
            folded.append(jnp.concatenate([x[:, 512:] + back, x[:, 512:] - back], 1))
        hi, lo = split(jnp.concatenate(folded, 0))
        mh_ref[pl.ds(row, 16), :] = hi
        ml_ref[pl.ds(row, 16), :] = lo

    @pl.loop(0, FRAMES // 4)
    def _(i):
        now = [g_ref[:, pl.ds(pl.multiple_of((i * 4 + f) * FRAME, FRAME), FRAME)] for f in range(4)]
        base = pl.multiple_of(i * 32, 32)
        for f in range(0, 4, 2):
            put(base + f * NODES, now[f], now[f + 1])

        @pl.when(i < SHOTS // 4)
        def _():
            target = pl.multiple_of(rows_frames + base, 32)
            diffs = []
            for f in range(4):
                later = g_ref[:, pl.ds(pl.multiple_of((i * 4 + f + HALO) * FRAME, FRAME), FRAME)]
                diffs.append(jnp.where(wide < d_ref[i * 4 + f + HALO], later - now[f], 0.0))
            for f in range(0, 4, 2):
                put(target + f * NODES, diffs[f], diffs[f + 1])

    loads[2].wait()
    loads[3].wait()
    total = rows_frames + rows_local
    half = total // 2

    @pl.loop(0, 2)
    def _(i):
        row = pl.multiple_of(i * half, 16)
        rows = pl.ds(row, half)
        for part in range(2):
            cols = slice(part * 512, (part + 1) * 512)
            out = product(mh_ref[rows, cols], ml_ref[rows, cols], ah_ref[part], al_ref[part])
            for k in range(2):
                place = pl.multiple_of((2 * k + part) * total + row, 16)
                sp_ref[pl.ds(place, half), :] = out[:, k * 128 : (k + 1) * 128]

    band = 48
    sign = 1.0 - 2.0 * (lax.broadcasted_iota(jnp.int32, (band, 128), 1) & 1).astype(f32)

    @pl.loop(0, rows_local // band)
    def _(i):
        base = pl.multiple_of(i * band, NODES)

        def frame(m, a):
            return sp_ref[pl.ds(pl.multiple_of(a * total + base + m * NODES, NODES), band), :]

        def edge(a):
            return sp_ref[pl.ds(pl.multiple_of(a * total + rows_frames + base, NODES), band), :]

        parts = [
            (frame(0, 0) - frame(2, 0)) + sign * (frame(1, 1) - frame(3, 1)) + edge(0),
            (frame(0, 1) - frame(2, 1)) - sign * (frame(1, 0) - frame(3, 0)) + edge(1),
            (frame(0, 2) + frame(2, 2)) - sign * (frame(1, 2) + frame(3, 2)) + edge(2),
            (frame(0, 3) + frame(2, 3)) - sign * (frame(1, 3) + frame(3, 3)) + edge(3),
        ]
        for a in range(4):
            w_ref[pl.ds(pl.multiple_of(a * rows_local + base, NODES), band), :] = parts[a]

    @pl.loop(0, NODES)
    def _(n):
        parts = [w_ref[pl.ds(a * rows_local + n, SHOTS, stride=NODES), :] for a in range(4)]
        outs = []
        for j in range(2):
            co = RELAX * cos_ref[HALO : HALO + SHOTS, j * 128 : (j + 1) * 128]
            si = RELAX * sin_ref[HALO : HALO + SHOTS, j * 128 : (j + 1) * 128]
            re, im = parts[2 * j], parts[2 * j + 1]
            outs += [re * co - im * si, im * co + re * si]
        for a in range(3):
            block = jnp.concatenate([outs[a], outs[3][32 * a : 32 * a + 32]], 0).T
            send_ref[pl.ds(a * NODES + n, GROUP, stride=24), :] = block

    send = pltpu.make_async_copy(send_ref, send_hbm, send_sem)
    send.start()
    store.wait()
    send.wait()


def signal(dither, last, recv, cos_t, sin_t, tables, head, gathers):
    vmem = pl.BlockSpec(memory_space=pltpu.VMEM)
    smem = pl.BlockSpec(memory_space=pltpu.SMEM)
    hbm = pl.BlockSpec(memory_space=pltpu.HBM)
    rows_ext, rows_frames, rows_local = EXT * NODES, FRAMES * NODES, SHOTS * NODES
    return pl.pallas_call(
        signal_kernel,
        in_specs=[smem, smem, vmem, vmem, vmem, hbm, hbm, hbm, hbm, hbm, hbm],
        out_specs=[hbm, hbm],
        out_shape=[
            jax.ShapeDtypeStruct((NODES, SHOTS * FRAME), f32),
            jax.ShapeDtypeStruct((GROUP * 24, 128), f32),
        ],
        scratch_shapes=[
            pltpu.VMEM((4 * rows_ext, 128), f32),
            pltpu.VMEM((NODES, FRAMES * FRAME), f32),
            pltpu.VMEM((rows_ext, FRAME), f32),
            pltpu.VMEM((256, 128), f32),
            pltpu.VMEM((rows_frames + rows_ext, 512), bf16),
            pltpu.VMEM((rows_frames + rows_ext, 512), bf16),
            pltpu.VMEM((rows_frames + rows_local, FRAME), bf16),
            pltpu.VMEM((rows_frames + rows_local, FRAME), bf16),
            pltpu.VMEM((4 * (rows_frames + rows_local), 128), f32),
            pltpu.VMEM((4 * rows_local, 128), f32),
            pltpu.VMEM((GROUP * 24, 128), f32),
            pltpu.VMEM((2, 256, 512), bf16),
            pltpu.VMEM((2, 256, 512), bf16),
            pltpu.VMEM((2, 512, 256), bf16),
            pltpu.VMEM((2, 512, 256), bf16),
            pltpu.SemaphoreType.DMA,
            pltpu.SemaphoreType.DMA,
            pltpu.SemaphoreType.DMA,
            pltpu.SemaphoreType.DMA,
            pltpu.SemaphoreType.DMA((4,)),
        ],
        compiler_params=pltpu.CompilerParams(vmem_limit_bytes=40 << 20),
        name="signal",
    )(dither, last, recv, cos_t, sin_t, *tables, head, gathers)


def rank_kernel(recv_ref, est_hbm, w_ref, out_hbm, ah_ref, al_ref, est_ref, out_ref, in_sem, out_sem):
    chunks = 4
    size = 256 // chunks
    loads = [
        pltpu.make_async_copy(
            est_hbm.at[:, pl.ds(i * size, size), :], est_ref.at[:, pl.ds(i * size, size), :], in_sem.at[i]
        )
        for i in range(chunks)
    ]
    for load in loads:
        load.start()
    lane = lax.broadcasted_iota(jnp.int32, (NODES, 128), 1)
    chunk = lane // 32

    def planes(p):
        rows = pl.ds(pl.multiple_of(p * NODES, NODES), NODES)
        values, extras = [], []
        for a in range(3):
            t = []
            for q in range(4):
                tile = recv_ref[pl.ds(pl.multiple_of((p * 4 + q) * 24 + a * NODES, NODES), NODES), :]
                t.append(pltpu.roll(tile, (96 * q) % 128, axis=1) if q else tile)
            values.append([
                jnp.where(lane < 96, t[0], t[1]),
                jnp.where(lane < 64, t[1], t[2]),
                jnp.where(lane < 32, t[2], t[3]),
            ])
            e = jnp.where(chunk == 0, t[3], jnp.where(chunk == 1, t[2], jnp.where(chunk == 2, t[1], t[0])))
            extras.append(pltpu.roll(e, 32 * (a + 1), axis=1) if a < 3 else e)
        values.append([])
        for i in range(3):
            x = extras[(4 * i) % 3]
            for k in range(1, 4):
                x = jnp.where(chunk == k, extras[(4 * i + k) % 3], x)
            values[3].append(x)
        return [
            [est_ref[a, rows, i * 128 : (i + 1) * 128] + values[a][i] for i in range(3)] for a in range(4)
        ]

    def unpack(p):
        upper, lower = planes(2 * p), planes(2 * p + 1)
        rows = pl.ds(pl.multiple_of(p * 16, 16), 16)
        for a in range(4):
            for i in range(3):
                hi, lo = split(jnp.concatenate([upper[a][i], lower[a][i]], 0))
                cols = slice((a % 2) * 384 + i * 128, (a % 2) * 384 + (i + 1) * 128)
                ah_ref[a // 2, rows, cols] = hi
                al_ref[a // 2, rows, cols] = lo

    for i in range(chunks):
        loads[i].wait()
        pl.loop(i * (16 // chunks), (i + 1) * (16 // chunks))(unpack)

    dot = functools.partial(jnp.dot, preferred_element_type=f32)
    lane_r = lax.broadcasted_iota(jnp.int32, (64, 128), 1)
    row_r = lax.broadcasted_iota(jnp.int32, (64, 128), 0)
    flip = jnp.where(lane_r < 64, 1.0, -1.0).astype(f32)
    diagonal = (lane_r == row_r) & (row_r < RANK)
    systems = []
    rights = []
    basis = []
    for j in range(2):
        yy = dot(ah_ref[j], w_ref[...])
        y = yy[:, :128] + yy[:, 128:] + dot(al_ref[j], w_ref[:, :128])
        basis.append(split(y))
        yt = y.T
        g = jnp.dot(yt, y, precision=highest, preferred_element_type=f32)
        g = g[:64] + flip * pltpu.roll(g[64:], 64, axis=1)
        trace = jnp.sum(jnp.where(diagonal, g, 0.0))
        g = jnp.where(diagonal, g + RIDGE * trace / RANK, g)
        eye = jnp.where(diagonal, 1.0, 0.0).astype(f32)
        systems.append([g[:RANK], eye[:RANK]])
        yh, yl = split(yt)
        c = dot(jnp.concatenate([yh, yl], 0), ah_ref[j])
        c = c[:128] + c[128:] + dot(yh, al_ref[j])
        rights.append(jnp.concatenate([c[:64, :384] + c[64:, 384:], c[:64, 384:] - c[64:, :384]], 0))

    neg = jnp.where(lax.broadcasted_iota(jnp.int32, (1, 128), 1) < 64, -1.0, 1.0).astype(f32)
    row_i = lax.broadcasted_iota(jnp.int32, (RANK, 128), 0)
    for k in range(RANK - 1):
        start = ((k + 1) // 8) * 8
        for j in range(2):
            g, w = systems[j]
            gk, wk = g[k : k + 1], w[k : k + 1]
            inv = 1.0 / gk[:, k : k + 1]
            gk, wk = gk * inv, wk * inv
            gs, ws = neg * pltpu.roll(gk, 64, axis=1), neg * pltpu.roll(wk, 64, axis=1)
            below = g[start:]
            live = row_i[start:] > k
            cr = jnp.where(live, below[:, k : k + 1], 0.0)
            ci = jnp.where(live, below[:, 64 + k : 65 + k], 0.0)
            low_g = below - (cr * gk + ci * gs)
            low_w = w[start:] - (cr * wk + ci * ws)
            if start:
                low_g = jnp.concatenate([g[:start], low_g], 0)
                low_w = jnp.concatenate([w[:start], low_w], 0)
            systems[j] = [low_g, low_w]

    def two(left, right):
        lh, ll = split(left)
        rh, rl = split(right)
        return dot(jnp.concatenate([lh, ll], 1), jnp.concatenate([rh, rh], 0)) + dot(lh, rl)

    stores = []
    for j in range(2):
        g, w = systems[j]
        d = jnp.sum(jnp.where(diagonal[:RANK], g, 0.0), axis=1, keepdims=True)
        w = w * lax.rsqrt(d)
        w = jnp.concatenate([w, jnp.zeros((16, 128), f32)], 0)
        left = jnp.concatenate([flip * w, pltpu.roll(w, 64, axis=1)], 0)
        x = two(left.T, two(left, rights[j]))
        x = jnp.concatenate(
            [jnp.concatenate([x[:64], -x[64:]], 0), jnp.concatenate([x[64:], x[:64]], 0)], 1
        )
        xh, xl = split(x)
        yh, yl = basis[j]
        low = dot(jnp.concatenate([yh, yl], 1), jnp.concatenate([xh, xh], 0)) + dot(yh, xl)
        out_ref[2 * j] = low[:, :384]
        out_ref[2 * j + 1] = low[:, 384:]
        stores.append(
            pltpu.make_async_copy(out_ref.at[pl.ds(2 * j, 2)], out_hbm.at[pl.ds(2 * j, 2)], out_sem.at[j])
        )
        stores[-1].start()
    for store in stores:
        store.wait()


def rank_reduce(recv, est, w):
    vmem = pl.BlockSpec(memory_space=pltpu.VMEM)
    hbm = pl.BlockSpec(memory_space=pltpu.HBM)
    return pl.pallas_call(
        rank_kernel,
        in_specs=[vmem, hbm, vmem],
        out_specs=hbm,
        out_shape=jax.ShapeDtypeStruct((4, 256, 384), f32),
        scratch_shapes=[
            pltpu.VMEM((2, 256, 768), bf16),
            pltpu.VMEM((2, 256, 768), bf16),
            pltpu.VMEM((4, 256, 384), f32),
            pltpu.VMEM((4, 256, 384), f32),
            pltpu.SemaphoreType.DMA((4,)),
            pltpu.SemaphoreType.DMA((2,)),
        ],
        compiler_params=pltpu.CompilerParams(vmem_limit_bytes=20 << 20),
        name="rank",
    )(recv, est, w)


def table(rows_first):
    shape = (2, 256, FRAME // 2) if rows_first else (2, FRAME // 2, 256)
    part = lax.broadcasted_iota(jnp.int32, shape, 0)
    row = lax.broadcasted_iota(jnp.int32, shape, 1 if rows_first else 2)
    time = lax.broadcasted_iota(jnp.int32, shape, 2 if rows_first else 1)
    k = 2 * (row % 128) + row // 128 + 1
    phase = (k * (2 * time + 1) + part * (SPAN // 2)) % (2 * SPAN)
    value = jnp.cos(math.pi / SPAN * phase.astype(f32)) / math.sqrt(SPAN)
    hi = lax.reduce_precision(value, 8, 7)
    return hi.astype(bf16), (value - hi).astype(bf16)


def shards(receiver_gathers, fourier_estimate, random_projector, release_sample):
    q = lax.axis_index("freq")
    est = fourier_estimate.reshape(4, 32, NODES, 4 * SHOTS)
    send = pack(est).reshape(GROUP, ROWS // 2, 2, 128)
    recv = lax.all_to_all(send, ("node", "freq"), split_axis=0, concat_axis=0, tiled=True)

    up = [(0, 1), (1, 2), (2, 3)]
    down = [(1, 0), (2, 1), (3, 2)]
    head = lax.ppermute(receiver_gathers[:, : HALO * FRAME], "freq", down)
    release_before = lax.ppermute(release_sample[SHOTS - HALO :], "freq", up)
    release_after = lax.ppermute(release_sample[:HALO], "freq", down)
    dither = jnp.concatenate([release_before, release_sample, release_after]) % FRAME
    src = lax.iota(jnp.int32, 256)
    k = 2 * (src % 128) + src // 128 + 1
    angle = math.pi / SPAN * (k[None, :] * (2 * dither - FRAME + 1)[:, None] % (2 * SPAN)).astype(f32)
    cos_t, sin_t = jnp.cos(angle), jnp.sin(angle)
    tables = table(True) + table(False)
    last = (q == 3).astype(jnp.int32).reshape(1)
    misfit, back = signal(dither, last, recv.reshape(GROUP * ROWS, 128), cos_t, sin_t, tables, head, receiver_gathers)

    arrived = lax.all_to_all(
        back.reshape(GROUP, 24, 128), ("node", "freq"), split_axis=0, concat_axis=0, tiled=True
    )
    omega = jnp.pad(random_projector, ((0, 0), (0, 16)))
    zero = jnp.zeros_like(omega)
    w = jnp.concatenate([jnp.concatenate([omega, zero], 1), jnp.concatenate([zero, omega], 1)], 0)
    hi = lax.reduce_precision(w, 8, 7)
    w = jnp.concatenate([hi.astype(bf16), (w - hi).astype(bf16)], 1)
    low = rank_reduce(arrived.reshape(GROUP * 24, 128), fourier_estimate.reshape(4, 256, 384), w)
    return low.reshape(2, 2, 256, 384), misfit


def solution(mesh):
    return jax.shard_map(
        shards,
        mesh=mesh,
        in_specs=(P("node", "freq"), P(("node", "freq"), None, None, None), P(), P("freq")),
        out_specs=(P(("node", "freq"), None, None, None), P("node", "freq")),
        check_vma=False,
    )
```

```python
import functools
import math

import jax
import jax.numpy as jnp
from jax import lax
from jax.experimental import pallas as pl
from jax.experimental.pallas import tpu as pltpu
from jax.sharding import PartitionSpec as P


SPAN = 4096
FRAME = 1024
RANK = 48
HALO = 4
SHOTS = 96
NODES = 8
EXT = SHOTS + 2 * HALO
FRAMES = SHOTS + HALO
GROUP = 128
ROWS = 26
ORDER = (0, 2, 1, 3)
RELAX = 0.25
RIDGE = 0.001
highest = lax.Precision.HIGHEST
f32 = jnp.float32
bf16 = jnp.bfloat16


def keep(x):
    return pltpu.with_memory_space_constraint(x, pltpu.HBM)


def aligned(x, n):
    return x if isinstance(x, int) else pl.multiple_of(x, n)


def split(x):
    hi = x.astype(bf16)
    lo = (x - hi.astype(f32)).astype(bf16)
    return hi, lo


def pack_kernel(x_hbm, o_hbm, x_ref, o_ref, in_sem, out_sem):
    chunks = 4
    count = 32 // chunks
    size = count * 4 * ROWS

    def load(i):
        part = pl.ds(i * count, count)
        return pltpu.make_async_copy(x_hbm.at[:, part], x_ref.at[:, part], in_sem.at[i])

    def store(i):
        part = pl.ds(aligned(i * size, 8), size)
        return pltpu.make_async_copy(o_ref.at[part], o_hbm.at[part], out_sem.at[i])

    for i in range(chunks):
        load(i).start()
    lane = lax.broadcasted_iota(jnp.int32, (NODES, 128), 1)
    node = lax.broadcasted_iota(jnp.int32, (NODES, 128), 0)
    slot = lane // 32
    own = slot == node % 4

    def turn(v, by):
        return pltpu.roll(v, by % 128, axis=1) if by % 128 else v

    def one(p, start):
        x = [[x_ref[a, p, :, i * 128 : (i + 1) * 128] for i in range(3)] for a in range(4)]
        edges = jnp.zeros((NODES, 128), f32)
        for k in range(3):
            for a in range(4):
                moved = turn(x[a][k], 32 * k + 8 * a - (92 - 32 * k))
                edges = jnp.where((slot == k) & ((lane // 8) % 4 == a), moved, edges)
        turned = [turn(edges, 32 * r) for r in range(4)]

        def spread(k):
            v = turned[(0 - k) % 4]
            for m in range(1, 4):
                v = jnp.where(slot == m, turned[(m - k) % 4], v)
            return jnp.where(own, v, 0.0)

        spreads = [spread(k) for k in range(3)]
        zero = jnp.zeros((NODES, 128), f32)
        for q in range(4):
            base = start + q * ROWS
            for a in range(3):
                if q == 0:
                    main = x[a][0]
                elif q == 3:
                    main = turn(x[a][2], 96)
                else:
                    main = jnp.where(lane < 32 * q, turn(x[a][q - 1], 32 * q), turn(x[a][q], 32 * q))
                m = 3 * q + a
                rest = turn(x[3][m // 4], 32 * (3 - m % 4))
                o_ref[pl.ds(base + NODES * a, NODES), :] = jnp.where(lane < SHOTS, main, rest)
            before = spreads[q - 1] if q > 0 else zero
            after = spreads[q] if q < 3 else zero
            halo = jnp.where(lane % 8 < 4, before, after)
            halo = halo + pltpu.roll(halo, 1, axis=0)
            halo = halo + pltpu.roll(halo, 2, axis=0)
            o_ref[pl.ds(base + 24, 1), :] = halo[3:4]
            o_ref[pl.ds(base + 25, 1), :] = halo[7:8]

    @pl.loop(0, chunks)
    def _(step):
        load(step).wait()
        for p in range(count):
            one(step * count + p, aligned(step * size, 8) + p * 4 * ROWS)
        store(step).start()

    for i in range(chunks):
        store(i).wait()


def pack(x):
    hbm = pl.BlockSpec(memory_space=pltpu.HBM)
    return pl.pallas_call(
        pack_kernel,
        in_specs=[hbm],
        out_specs=hbm,
        out_shape=pltpu.HBM((GROUP * ROWS, 128), f32),
        scratch_shapes=[
            pltpu.VMEM((4, 32, NODES, 4 * SHOTS), f32),
            pltpu.VMEM((GROUP * ROWS, 128), f32),
            pltpu.SemaphoreType.DMA((4,)),
            pltpu.SemaphoreType.DMA((4,)),
        ],
        name="pack",
    )(keep(x))


def product(hi, lo, th, tl):
    return jnp.dot(
        jnp.concatenate([hi, lo, hi], 1), jnp.concatenate([th, th, tl], 0), preferred_element_type=f32
    )


def signal_kernel(
    d_ref, last_ref, recv_ref, cos_ref, sin_ref, fh_hbm, fl_hbm, ah_hbm, al_hbm, head_ref, gath_ref,
    mis_ref, send_hbm,
    c_ref, g_ref, q_ref, h_ref, lh_ref, ll_ref, mh_ref, ml_ref, sp_ref, w_ref, send_ref,
    fh_ref, fl_ref, ah_ref, al_ref, in_sem, head_sem, out_sem, send_sem, table_sem,
):
    rows_ext = EXT * NODES
    rows_frames = FRAMES * NODES
    rows_local = SHOTS * NODES
    local = SHOTS * FRAME
    loads = [
        pltpu.make_async_copy(src, dst, table_sem.at[i])
        for i, (src, dst) in enumerate(
            [(fh_hbm, fh_ref), (fl_hbm, fl_ref), (ah_hbm, ah_ref), (al_hbm, al_ref)]
        )
    ]
    loads[0].start()
    loads[1].start()
    fetch = pltpu.make_async_copy(gath_ref, g_ref.at[:, pl.ds(0, local)], in_sem)
    fetch.start()
    fetch_head = pltpu.make_async_copy(head_ref.at[:, pl.ds(0, HALO * FRAME)], g_ref.at[:, pl.ds(local, HALO * FRAME)], head_sem)
    fetch_head.start()
    loads[2].start()
    loads[3].start()

    for i in range(2):
        h_ref[i * 128 : (i + 1) * 128, :] = recv_ref[pl.ds(24 + i, GROUP, stride=ROWS), :].T

    @pl.loop(0, NODES)
    def _(n):
        blocks = [recv_ref[pl.ds(a * NODES + n, GROUP, stride=ROWS), :].T for a in range(3)]
        planes = [b[:SHOTS] for b in blocks] + [jnp.concatenate([b[SHOTS:] for b in blocks], 0)]
        halo = aligned(n * 32, 32)
        pieces = [
            (HALO, SHOTS, planes),
            (0, HALO, [h_ref[pl.ds(halo + 8 * a, HALO), :] for a in range(4)]),
            (HALO + SHOTS, HALO, [h_ref[pl.ds(halo + 8 * a + HALO, HALO), :] for a in range(4)]),
        ]
        for first, size, values in pieces:
            for j in range(2):
                re, im = values[2 * j], values[2 * j + 1]
                co = cos_ref[first : first + size, j * 128 : (j + 1) * 128]
                si = sin_ref[first : first + size, j * 128 : (j + 1) * 128]
                place = 2 * j * rows_ext + first * NODES + n
                c_ref[pl.ds(place, size, stride=NODES), :] = 2.0 * (re * co + im * si)
                c_ref[pl.ds(place + rows_ext, size, stride=NODES), :] = 2.0 * (im * co - re * si)

    step = 80
    parity = 1.0 - 2.0 * (lax.broadcasted_iota(jnp.int32, (step, 128), 1) & 1).astype(f32)

    @pl.loop(0, rows_frames // step)
    def _(i):
        base = aligned(i * step, NODES)

        def shot(m, a):
            return c_ref[pl.ds(aligned(a * rows_ext + base + (HALO - m) * NODES, NODES), step), :]

        parts = [
            (shot(0, 0) - shot(2, 0)) - parity * (shot(1, 1) - shot(3, 1)),
            (shot(0, 1) - shot(2, 1)) + parity * (shot(1, 0) - shot(3, 0)),
            (shot(0, 2) + shot(2, 2)) - parity * (shot(1, 2) + shot(3, 2)),
            (shot(0, 3) + shot(2, 3)) - parity * (shot(1, 3) + shot(3, 3)),
        ]
        for a in range(4):
            hi, lo = split(parts[a])
            lh_ref[pl.ds(base, step), ORDER[a] * 128 : (ORDER[a] + 1) * 128] = hi
            ll_ref[pl.ds(base, step), ORDER[a] * 128 : (ORDER[a] + 1) * 128] = lo

    @pl.loop(0, rows_ext // 64)
    def _(i):
        base = aligned(i * 64, 64)
        target = aligned(rows_frames + base, 32)
        for a in range(4):
            hi, lo = split(c_ref[pl.ds(aligned(a * rows_ext + base, 64), 64), :])
            lh_ref[pl.ds(target, 64), ORDER[a] * 128 : (ORDER[a] + 1) * 128] = hi
            ll_ref[pl.ds(target, 64), ORDER[a] * 128 : (ORDER[a] + 1) * 128] = lo

    width = 256
    lane = lax.broadcasted_iota(jnp.int32, (NODES, width), 1)
    mirror = 127 - lax.broadcasted_iota(jnp.int32, (NODES, 128), 1)

    def reverse(x):
        tiles = [x[:, i : i + 128] for i in range(0, x.shape[1], 128)]
        return jnp.concatenate([jnp.take_along_axis(t, mirror, axis=1) for t in tiles[::-1]], 1)

    def pair(row, size, c):
        cols = pl.ds(aligned(c * width, width), width)
        rows = pl.ds(row, size)
        return (
            product(lh_ref[rows, :256], ll_ref[rows, :256], fh_ref[0, :, cols], fl_ref[0, :, cols]),
            product(lh_ref[rows, 256:], ll_ref[rows, 256:], fh_ref[1, :, cols], fl_ref[1, :, cols]),
        )

    def columns(c):
        return aligned(512 + c * width, width), aligned(256 - c * width, width)

    loads[0].wait()
    loads[1].wait()
    half_ext = rows_ext // 2

    for i in range(4):
        m, c = i // 2, i % 2
        even, odd = pair(aligned(rows_frames + m * half_ext, 16), half_ext, c)
        upper, lower = columns(c)
        for s in range(EXT // 2):
            rows = slice(s * NODES, (s + 1) * NODES)
            place = pl.ds(aligned(m * half_ext + s * NODES, NODES), NODES)
            d = d_ref[m * (EXT // 2) + s]
            q_ref[place, pl.ds(upper, width)] = jnp.where(lane < d - upper, even[rows] + odd[rows], 0.0)
            q_ref[place, pl.ds(lower, width)] = jnp.where(lane < d - lower, reverse(even[rows] - odd[rows]), 0.0)

    fetch.wait()
    fetch_head.wait()
    half_frames = rows_frames // 2

    for i in range(4):
        m, c = i // 2, i % 2
        even, odd = pair(aligned(m * half_frames, 16), half_frames, c)
        upper, lower = columns(c)
        for f in range(FRAMES // 2):
            rows = slice(f * NODES, (f + 1) * NODES)
            first = m * half_frames + f * NODES
            now = pl.ds(aligned(first, NODES), NODES)
            ahead = pl.ds(aligned(first + HALO * NODES, NODES), NODES)
            start = (m * (FRAMES // 2) + f) * FRAME
            for col, out in ((upper, even[rows] + odd[rows]), (lower, reverse(even[rows] - odd[rows]))):
                cols = pl.ds(col, width)
                place = pl.ds(aligned(start + col, width), width)
                g_ref[:, place] = g_ref[:, place] - out + (q_ref[ahead, cols] - q_ref[now, cols])

    store = pltpu.make_async_copy(g_ref.at[:, pl.ds(0, local)], mis_ref, out_sem)
    store.start()

    wide = lax.broadcasted_iota(jnp.int32, (NODES, FRAME), 1)

    def put(row, first, second):
        folded = []
        for x in (first, second):
            back = reverse(x[:, :512])
            folded.append(jnp.concatenate([x[:, 512:] + back, x[:, 512:] - back], 1))
        hi, lo = split(jnp.concatenate(folded, 0))
        mh_ref[pl.ds(row, 16), :] = hi
        ml_ref[pl.ds(row, 16), :] = lo

    def frame_at(f):
        return g_ref[:, pl.ds(aligned(f * FRAME, FRAME), FRAME)]

    inside = last_ref[0] == 0

    def residual(f):
        x = frame_at(f)
        return x if f < SHOTS else jnp.where(inside, x, 0.0)

    total = rows_frames + rows_local
    half = total // 2

    def adjoint(i):
        rows = slice(i * half, (i + 1) * half)
        for part in range(2):
            cols = slice(part * 512, (part + 1) * 512)
            out = product(mh_ref[rows, cols], ml_ref[rows, cols], ah_ref[part], al_ref[part])
            for k in range(2):
                place = (2 * k + part) * total + i * half
                sp_ref[place : place + half, :] = out[:, k * 128 : (k + 1) * 128]

    def edge_of(f):
        return jnp.where(wide < d_ref[f + HALO], residual(f + HALO) - residual(f), 0.0)

    for f in range(0, FRAMES, 2):
        put(f * NODES, residual(f), residual(f + 1))
    loads[2].wait()
    loads[3].wait()
    adjoint(0)
    for f in range(0, SHOTS, 2):
        put(rows_frames + f * NODES, edge_of(f), edge_of(f + 1))
    adjoint(1)

    band = 48
    sign = 1.0 - 2.0 * (lax.broadcasted_iota(jnp.int32, (band, 128), 1) & 1).astype(f32)

    @pl.loop(0, rows_local // band)
    def _(i):
        base = aligned(i * band, NODES)

        def frame(m, a):
            return sp_ref[pl.ds(aligned(a * total + base + m * NODES, NODES), band), :]

        def edge(a):
            return sp_ref[pl.ds(aligned(a * total + rows_frames + base, NODES), band), :]

        parts = [
            (frame(0, 0) - frame(2, 0)) + sign * (frame(1, 1) - frame(3, 1)) + edge(0),
            (frame(0, 1) - frame(2, 1)) - sign * (frame(1, 0) - frame(3, 0)) + edge(1),
            (frame(0, 2) + frame(2, 2)) - sign * (frame(1, 2) + frame(3, 2)) + edge(2),
            (frame(0, 3) + frame(2, 3)) - sign * (frame(1, 3) + frame(3, 3)) + edge(3),
        ]
        for a in range(4):
            w_ref[pl.ds(aligned(a * rows_local + base, NODES), band), :] = parts[a]

    def emit(n):
        parts = [w_ref[pl.ds(a * rows_local + n, SHOTS, stride=NODES), :] for a in range(4)]
        outs = []
        for j in range(2):
            co = RELAX * cos_ref[HALO : HALO + SHOTS, j * 128 : (j + 1) * 128]
            si = RELAX * sin_ref[HALO : HALO + SHOTS, j * 128 : (j + 1) * 128]
            re, im = parts[2 * j], parts[2 * j + 1]
            outs += [re * co - im * si, im * co + re * si]
        for a in range(3):
            block = jnp.concatenate([outs[a], outs[3][32 * a : 32 * a + 32]], 0).T
            send_ref[pl.ds(a * NODES + n, GROUP, stride=24), :] = block

    @pl.loop(0, NODES // 2)
    def _(n):
        emit(2 * n)
        emit(2 * n + 1)

    send = pltpu.make_async_copy(send_ref, send_hbm, send_sem)
    send.start()
    store.wait()
    send.wait()


def signal(dither, last, recv, cos_t, sin_t, tables, head, gathers):
    vmem = pl.BlockSpec(memory_space=pltpu.VMEM)
    smem = pl.BlockSpec(memory_space=pltpu.SMEM)
    hbm = pl.BlockSpec(memory_space=pltpu.HBM)
    rows_ext, rows_frames, rows_local = EXT * NODES, FRAMES * NODES, SHOTS * NODES
    return pl.pallas_call(
        signal_kernel,
        in_specs=[smem, smem, vmem, vmem, vmem, hbm, hbm, hbm, hbm, hbm, hbm],
        out_specs=[hbm, hbm],
        out_shape=[
            pltpu.HBM((NODES, SHOTS * FRAME), f32),
            pltpu.HBM((GROUP * 24, 128), f32),
        ],
        scratch_shapes=[
            pltpu.VMEM((4 * rows_ext, 128), f32),
            pltpu.VMEM((NODES, FRAMES * FRAME), f32),
            pltpu.VMEM((rows_ext, FRAME), f32),
            pltpu.VMEM((256, 128), f32),
            pltpu.VMEM((rows_frames + rows_ext, 512), bf16),
            pltpu.VMEM((rows_frames + rows_ext, 512), bf16),
            pltpu.VMEM((rows_frames + rows_local, FRAME), bf16),
            pltpu.VMEM((rows_frames + rows_local, FRAME), bf16),
            pltpu.VMEM((4 * (rows_frames + rows_local), 128), f32),
            pltpu.VMEM((4 * rows_local, 128), f32),
            pltpu.VMEM((GROUP * 24, 128), f32),
            pltpu.VMEM((2, 256, 512), bf16),
            pltpu.VMEM((2, 256, 512), bf16),
            pltpu.VMEM((2, 512, 256), bf16),
            pltpu.VMEM((2, 512, 256), bf16),
            pltpu.SemaphoreType.DMA,
            pltpu.SemaphoreType.DMA,
            pltpu.SemaphoreType.DMA,
            pltpu.SemaphoreType.DMA,
            pltpu.SemaphoreType.DMA((4,)),
        ],
        compiler_params=pltpu.CompilerParams(vmem_limit_bytes=40 << 20),
        name="signal",
    )(dither, last, recv, cos_t, sin_t, *[keep(t) for t in tables], keep(head), keep(gathers))


def rank_kernel(
    recv_ref, est_hbm, w_hbm, out_hbm, ah_ref, al_ref, est_ref, out_ref, w_ref, in_sem, out_sem, w_sem
):
    chunks = 4
    size = 256 // chunks
    loads = [
        pltpu.make_async_copy(
            est_hbm.at[:, pl.ds(i * size, size), :], est_ref.at[:, pl.ds(i * size, size), :], in_sem.at[i]
        )
        for i in range(chunks)
    ]
    for load in loads:
        load.start()
    load_w = pltpu.make_async_copy(w_hbm, w_ref, w_sem)
    load_w.start()
    lane = lax.broadcasted_iota(jnp.int32, (NODES, 128), 1)
    chunk = lane // 32

    def planes(p):
        rows = pl.ds(aligned(p * NODES, NODES), NODES)
        values, extras = [], []
        for a in range(3):
            t = []
            for q in range(4):
                tile = recv_ref[pl.ds(aligned((p * 4 + q) * 24 + a * NODES, NODES), NODES), :]
                t.append(pltpu.roll(tile, (96 * q) % 128, axis=1) if q else tile)
            values.append([
                jnp.where(lane < 96, t[0], t[1]),
                jnp.where(lane < 64, t[1], t[2]),
                jnp.where(lane < 32, t[2], t[3]),
            ])
            e = jnp.where(chunk == 0, t[3], jnp.where(chunk == 1, t[2], jnp.where(chunk == 2, t[1], t[0])))
            extras.append(pltpu.roll(e, 32 * (a + 1), axis=1) if a < 3 else e)
        values.append([])
        for i in range(3):
            x = extras[(4 * i) % 3]
            for k in range(1, 4):
                x = jnp.where(chunk == k, extras[(4 * i + k) % 3], x)
            values[3].append(x)
        return [
            [est_ref[a, rows, i * 128 : (i + 1) * 128] + values[a][i] for i in range(3)] for a in range(4)
        ]

    def unpack(p):
        upper, lower = planes(2 * p), planes(2 * p + 1)
        rows = pl.ds(aligned(p * 16, 16), 16)
        for a in range(4):
            for i in range(3):
                hi, lo = split(jnp.concatenate([upper[a][i], lower[a][i]], 0))
                cols = slice((a % 2) * 384 + i * 128, (a % 2) * 384 + (i + 1) * 128)
                ah_ref[a // 2, rows, cols] = hi
                al_ref[a // 2, rows, cols] = lo

    for i in range(chunks):
        loads[i].wait()

        @pl.loop(0, 2)
        def _(p, i=i):
            unpack(i * 4 + p * 2)
            unpack(i * 4 + p * 2 + 1)

    load_w.wait()

    dot = functools.partial(jnp.dot, preferred_element_type=f32)
    lane_r = lax.broadcasted_iota(jnp.int32, (64, 128), 1)
    row_r = lax.broadcasted_iota(jnp.int32, (64, 128), 0)
    flip = jnp.where(lane_r < 64, 1.0, -1.0).astype(f32)
    diagonal = (lane_r == row_r) & (row_r < RANK)
    systems = []
    rights = []
    basis = []
    for j in range(2):
        yy = dot(ah_ref[j], w_ref[...])
        y = yy[:, :128] + yy[:, 128:] + dot(al_ref[j], w_ref[:, :128])
        basis.append(split(y))
        yt = y.T
        g = jnp.dot(yt, y, precision=highest, preferred_element_type=f32)
        g = g[:64] + flip * pltpu.roll(g[64:], 64, axis=1)
        trace = jnp.sum(jnp.where(diagonal, g, 0.0))
        g = jnp.where(diagonal, g + RIDGE * trace / RANK, g)
        eye = jnp.where(diagonal, 1.0, 0.0).astype(f32)
        systems.append([g[:RANK], eye[:RANK]])
        yh, yl = split(yt)
        c = dot(jnp.concatenate([yh, yl], 0), ah_ref[j])
        c = c[:128] + c[128:] + dot(yh, al_ref[j])
        rights.append(jnp.concatenate([c[:64, :384] + c[64:, 384:], c[:64, 384:] - c[64:, :384]], 0))

    neg = jnp.where(lax.broadcasted_iota(jnp.int32, (NODES, 128), 1) < 64, -1.0, 1.0).astype(f32)
    row_i = lax.broadcasted_iota(jnp.int32, (NODES, 128), 0)
    groups = RANK // NODES
    state = [
        ([g[i * NODES : (i + 1) * NODES] for i in range(groups)], [w[i * NODES : (i + 1) * NODES] for i in range(groups)])
        for g, w in systems
    ]

    def row(x, k):
        return jnp.broadcast_to(x[k % NODES : k % NODES + 1], (NODES, 128))

    def column(x, k):
        return jnp.broadcast_to(x[:, k : k + 1], (NODES, 128))

    def turned(x):
        return neg * pltpu.roll(x, 64, axis=1)

    for k in range(0, RANK, 2):
        top = k // NODES
        for gs, ws in state:
            gt, wt = turned(gs[top]), turned(ws[top])
            cols = [[column(gs[i], c) for c in (k, 64 + k, k + 1, 65 + k)] for i in range(top, groups)]
            a = row(cols[0][0], k)
            br, bi = row(cols[0][2], k), row(cols[0][3], k)
            d = row(cols[0][2], k + 1)
            ia = 1.0 / a
            lr, li = br * ia, -bi * ia
            second = 1.0 / (d - (br * br + bi * bi) * ia)
            g0, g0i, w0, w0i = row(gs[top], k), row(gt, k), row(ws[top], k), row(wt, k)
            g1 = row(gs[top], k + 1) - (lr * g0 + li * g0i)
            g1i = row(gt, k + 1) - (lr * g0i - li * g0)
            w1 = row(ws[top], k + 1) - (lr * w0 + li * w0i)
            w1i = row(wt, k + 1) - (lr * w0i - li * w0)
            for i in range(top, groups):
                c0r, c0i, c1r, c1i = cols[i - top]
                f0r, f0i = c0r * ia, c0i * ia
                f1r = (c1r - (f0r * br - f0i * bi)) * second
                f1i = (c1i - (f0r * bi + f0i * br)) * second
                if i == top:
                    f0r, f0i = jnp.where(row_i > k % NODES, f0r, 0.0), jnp.where(row_i > k % NODES, f0i, 0.0)
                    f1r, f1i = jnp.where(row_i > k % NODES + 1, f1r, 0.0), jnp.where(row_i > k % NODES + 1, f1i, 0.0)
                gs[i] = gs[i] - ((f0r * g0 + f0i * g0i) + (f1r * g1 + f1i * g1i))
                ws[i] = ws[i] - ((f0r * w0 + f0i * w0i) + (f1r * w1 + f1i * w1i))
    systems = [[jnp.concatenate(gs, 0), jnp.concatenate(ws, 0)] for gs, ws in state]

    def two(left, right):
        lh, ll = split(left)
        rh, rl = split(right)
        return dot(jnp.concatenate([lh, ll], 1), jnp.concatenate([rh, rh], 0)) + dot(lh, rl)

    stores = []
    for j in range(2):
        g, w = systems[j]
        d = jnp.sum(jnp.where(diagonal[:RANK], g, 0.0), axis=1, keepdims=True)
        w = w * lax.rsqrt(d)
        w = jnp.concatenate([w, jnp.zeros((16, 128), f32)], 0)
        left = jnp.concatenate([flip * w, pltpu.roll(w, 64, axis=1)], 0)
        x = two(left.T, two(left, rights[j]))
        x = jnp.concatenate(
            [jnp.concatenate([x[:64], -x[64:]], 0), jnp.concatenate([x[64:], x[:64]], 0)], 1
        )
        xh, xl = split(x)
        yh, yl = basis[j]
        low = dot(jnp.concatenate([yh, yl], 1), jnp.concatenate([xh, xh], 0)) + dot(yh, xl)
        out_ref[2 * j] = low[:, :384]
        out_ref[2 * j + 1] = low[:, 384:]
        stores.append(
            pltpu.make_async_copy(out_ref.at[pl.ds(2 * j, 2)], out_hbm.at[pl.ds(2 * j, 2)], out_sem.at[j])
        )
        stores[-1].start()
    for store in stores:
        store.wait()


def rank_reduce(recv, est, w):
    vmem = pl.BlockSpec(memory_space=pltpu.VMEM)
    hbm = pl.BlockSpec(memory_space=pltpu.HBM)
    return pl.pallas_call(
        rank_kernel,
        in_specs=[vmem, hbm, hbm],
        out_specs=hbm,
        out_shape=pltpu.HBM((4, 256, 384), f32),
        scratch_shapes=[
            pltpu.VMEM((2, 256, 768), bf16),
            pltpu.VMEM((2, 256, 768), bf16),
            pltpu.VMEM((4, 256, 384), f32),
            pltpu.VMEM((4, 256, 384), f32),
            pltpu.VMEM((768, 256), bf16),
            pltpu.SemaphoreType.DMA((4,)),
            pltpu.SemaphoreType.DMA((2,)),
            pltpu.SemaphoreType.DMA,
        ],
        compiler_params=pltpu.CompilerParams(vmem_limit_bytes=20 << 20),
        name="rank",
    )(recv, keep(est), keep(w))


def table(rows_first):
    half = FRAME // 2
    fine = 128 if rows_first else 64
    row = lax.iota(jnp.int32, 256)
    k = 2 * (row % 128) + row // 128 + 1
    near = 2 * lax.iota(jnp.int32, fine) + 1
    far = 2 * fine * lax.iota(jnp.int32, half // fine)
    if rows_first:
        phases = k[:, None] * near[None, :], k[:, None] * far[None, :]
    else:
        phases = near[:, None] * k[None, :], far[:, None] * k[None, :]
    angles = [math.pi / SPAN * (p % (2 * SPAN)).astype(f32) for p in phases]
    scale = 1.0 / math.sqrt(SPAN)
    cn, sn = jnp.cos(angles[0]) * scale, jnp.sin(angles[0]) * scale
    cf, sf = jnp.cos(angles[1]), jnp.sin(angles[1])
    cn, sn, cf, sf = lax.optimization_barrier((cn, sn, cf, sf))
    if rows_first:
        pieces = [
            (cn * cf[:, i : i + 1] - sn * sf[:, i : i + 1], -(sn * cf[:, i : i + 1] + cn * sf[:, i : i + 1]))
            for i in range(half // fine)
        ]
        value = jnp.stack([jnp.concatenate([p[j] for p in pieces], 1) for j in range(2)])
    else:
        cn, sn, cf, sf = cn[None], sn[None], cf[:, None], sf[:, None]
        value = jnp.stack([cn * cf - sn * sf, -(sn * cf + cn * sf)]).reshape(2, half, 256)
    hi = lax.reduce_precision(value, 8, 7)
    return hi.astype(bf16), (value - hi).astype(bf16)


def shards(receiver_gathers, fourier_estimate, random_projector, release_sample):
    q = lax.axis_index("freq")
    est = fourier_estimate.reshape(4, 32, NODES, 4 * SHOTS)
    send = pack(est).reshape(GROUP, ROWS // 2, 2, 128)
    recv = lax.all_to_all(send, ("node", "freq"), split_axis=0, concat_axis=0, tiled=True)

    up = [(0, 1), (1, 2), (2, 3)]
    down = [(1, 0), (2, 1), (3, 2)]
    starts = jnp.broadcast_to(jnp.pad(release_sample[:HALO].astype(f32), (0, 124))[None], (NODES, 128))
    head = lax.ppermute(
        jnp.concatenate([receiver_gathers[:, : HALO * FRAME], starts], 1), "freq", down
    )
    release_before = lax.ppermute(release_sample[SHOTS - HALO :], "freq", up)
    release_after = head[0, HALO * FRAME : HALO * FRAME + HALO].astype(jnp.int32)
    dither = jnp.concatenate([release_before, release_sample, release_after]) % FRAME
    src = lax.iota(jnp.int32, 256)
    k = 2 * (src % 128) + src // 128 + 1
    angle = math.pi / SPAN * (k[None, :] * (2 * dither - FRAME + 1)[:, None] % (2 * SPAN)).astype(f32)
    cos_t, sin_t = jnp.cos(angle), jnp.sin(angle)
    tables = table(True) + table(False)
    last = (q == 3).astype(jnp.int32).reshape(1)
    misfit, back = signal(dither, last, recv.reshape(GROUP * ROWS, 128), cos_t, sin_t, tables, head, receiver_gathers)

    arrived = lax.all_to_all(
        back.reshape(GROUP, 24, 128), ("node", "freq"), split_axis=0, concat_axis=0, tiled=True
    )
    omega = jnp.pad(random_projector, ((0, 0), (0, 16)))
    zero = jnp.zeros_like(omega)
    w = jnp.concatenate([jnp.concatenate([omega, zero], 1), jnp.concatenate([zero, omega], 1)], 0)
    hi = lax.reduce_precision(w, 8, 7)
    w = jnp.concatenate([hi.astype(bf16), (w - hi).astype(bf16)], 1)
    low = rank_reduce(arrived.reshape(GROUP * 24, 128), fourier_estimate.reshape(4, 256, 384), w)
    return low.reshape(2, 2, 256, 384), misfit


def solution(mesh):
    return jax.shard_map(
        shards,
        mesh=mesh,
        in_specs=(P("node", "freq"), P(("node", "freq"), None, None, None), P(), P("freq")),
        out_specs=(P(("node", "freq"), None, None, None), P("node", "freq")),
        check_vma=False,
    )
```

```python
import functools
import math

import jax
import jax.numpy as jnp
from jax import lax
from jax.experimental import pallas as pl
from jax.experimental.pallas import tpu as pltpu
from jax.sharding import PartitionSpec as P


SPAN = 4096
FRAME = 1024
RANK = 48
HALO = 4
SHOTS = 96
NODES = 8
EXT = SHOTS + 2 * HALO
FRAMES = SHOTS + HALO
GROUP = 128
ROWS = 26
PACK_CHUNKS = 8
ORDER = (0, 2, 1, 3)
RELAX = 0.25
RIDGE = 0.001
highest = lax.Precision.HIGHEST
f32 = jnp.float32
bf16 = jnp.bfloat16


def keep(x):
    return pltpu.with_memory_space_constraint(x, pltpu.HBM)


def aligned(x, n):
    return x if isinstance(x, int) else pl.multiple_of(x, n)


def split(x):
    hi = x.astype(bf16)
    lo = (x - hi.astype(f32)).astype(bf16)
    return hi, lo


def pack_kernel(x_hbm, o_hbm, x_ref, o_ref, in_sem, out_sem):
    chunks = PACK_CHUNKS
    count = 32 // chunks
    size = count * 4 * ROWS
    lane = lax.broadcasted_iota(jnp.int32, (1, NODES, 128), 2)
    node = lax.broadcasted_iota(jnp.int32, (1, NODES, 128), 1)
    slot = lane // 32
    own = slot == node % 4
    shape = (count, NODES, 128)

    def load(i):
        part = pl.ds(i * count, count)
        return pltpu.make_async_copy(x_hbm.at[:, part], x_ref.at[:, part], in_sem.at[i])

    def store(i):
        part = pl.ds(aligned(i * size, 8), size)
        return pltpu.make_async_copy(o_ref.at[part], o_hbm.at[part], out_sem.at[i])

    def pick(mask, x, y):
        return jnp.where(jnp.broadcast_to(mask, shape), x, y)

    def turn(v, by):
        return pltpu.roll(v, by % 128, axis=2) if by % 128 else v

    for i in range(chunks):
        load(i).start()

    @pl.loop(0, chunks)
    def _(step):
        load(step).wait()
        blocks = pl.ds(step * count, count)
        x = [[x_ref[a, blocks, :, i * 128 : (i + 1) * 128] for i in range(3)] for a in range(4)]
        zero = jnp.zeros(shape, f32)
        edges = zero
        for k in range(3):
            for a in range(4):
                moved = turn(x[a][k], 32 * k + 8 * a - (92 - 32 * k))
                edges = pick(lane // 8 == 4 * k + a, moved, edges)
        turned = [turn(edges, 32 * r) for r in range(4)]

        def spread(k):
            v = turned[(0 - k) % 4]
            for m in range(1, 4):
                v = pick(slot == m, turned[(m - k) % 4], v)
            return pick(own, v, zero)

        spreads = [spread(k) for k in range(3)]

        def put(row, value, size):
            for p in range(count):
                o_ref[pl.ds(aligned(step * chunk_rows, 8) + p * 4 * ROWS + row, size), :] = value[p]

        chunk_rows = size
        for q in range(4):
            for a in range(3):
                if q == 0:
                    main = x[a][0]
                elif q == 3:
                    main = turn(x[a][2], 96)
                else:
                    main = pick(lane < 32 * q, turn(x[a][q - 1], 32 * q), turn(x[a][q], 32 * q))
                m = 3 * q + a
                rest = turn(x[3][m // 4], 32 * (3 - m % 4))
                put(q * ROWS + NODES * a, pick(lane < SHOTS, main, rest), NODES)
            before = spreads[q - 1] if q > 0 else zero
            after = spreads[q] if q < 3 else zero
            halo = pick(lane % 8 < 4, before, after)
            halo = halo + pltpu.roll(halo, 1, axis=1)
            halo = halo + pltpu.roll(halo, 2, axis=1)
            put(q * ROWS + 24, halo[:, 3:4], 1)
            put(q * ROWS + 25, halo[:, 7:8], 1)
        store(step).start()

    for i in range(chunks):
        store(i).wait()


def pack(x):
    hbm = pl.BlockSpec(memory_space=pltpu.HBM)
    return pl.pallas_call(
        pack_kernel,
        in_specs=[hbm],
        out_specs=hbm,
        out_shape=pltpu.HBM((GROUP * ROWS, 128), f32),
        scratch_shapes=[
            pltpu.VMEM((4, 32, NODES, 4 * SHOTS), f32),
            pltpu.VMEM((GROUP * ROWS, 128), f32),
            pltpu.SemaphoreType.DMA((PACK_CHUNKS,)),
            pltpu.SemaphoreType.DMA((PACK_CHUNKS,)),
        ],
        name="pack",
    )(keep(x))


def product(hi, lo, th, tl):
    return jnp.dot(
        jnp.concatenate([hi, lo, hi], 1), jnp.concatenate([th, th, tl], 0), preferred_element_type=f32
    )


def signal_kernel(
    d_ref, last_ref, recv_ref, cos_ref, sin_ref, fh_hbm, fl_hbm, ah_hbm, al_hbm, head_ref, gath_ref,
    mis_ref, send_hbm,
    c_ref, g_ref, q_ref, h_ref, lh_ref, ll_ref, mh_ref, ml_ref, sp_ref, w_ref, send_ref,
    fh_ref, fl_ref, ah_ref, al_ref, in_sem, head_sem, out_sem, send_sem, table_sem,
):
    rows_ext = EXT * NODES
    rows_frames = FRAMES * NODES
    rows_local = SHOTS * NODES
    local = SHOTS * FRAME
    loads = [
        pltpu.make_async_copy(src, dst, table_sem.at[i])
        for i, (src, dst) in enumerate(
            [(fh_hbm, fh_ref), (fl_hbm, fl_ref), (ah_hbm, ah_ref), (al_hbm, al_ref)]
        )
    ]
    loads[0].start()
    loads[1].start()
    fetch = pltpu.make_async_copy(gath_ref, g_ref.at[:, pl.ds(0, local)], in_sem)
    fetch.start()
    fetch_head = pltpu.make_async_copy(head_ref.at[:, pl.ds(0, HALO * FRAME)], g_ref.at[:, pl.ds(local, HALO * FRAME)], head_sem)
    fetch_head.start()
    loads[2].start()
    loads[3].start()

    for i in range(2):
        h_ref[i * 128 : (i + 1) * 128, :] = recv_ref[pl.ds(24 + i, GROUP, stride=ROWS), :].T

    for n in range(NODES):
        blocks = [recv_ref[pl.ds(a * NODES + n, GROUP, stride=ROWS), :].T for a in range(3)]
        planes = [b[:SHOTS] for b in blocks] + [jnp.concatenate([b[SHOTS:] for b in blocks], 0)]
        halo = aligned(n * 32, 32)
        pieces = [
            (HALO, SHOTS, planes),
            (0, HALO, [h_ref[pl.ds(halo + 8 * a, HALO), :] for a in range(4)]),
            (HALO + SHOTS, HALO, [h_ref[pl.ds(halo + 8 * a + HALO, HALO), :] for a in range(4)]),
        ]
        for first, size, values in pieces:
            for j in range(2):
                re, im = values[2 * j], values[2 * j + 1]
                co = cos_ref[first : first + size, j * 128 : (j + 1) * 128]
                si = sin_ref[first : first + size, j * 128 : (j + 1) * 128]
                place = 2 * j * rows_ext + first * NODES + n
                c_ref[pl.ds(place, size, stride=NODES), :] = 2.0 * (re * co + im * si)
                c_ref[pl.ds(place + rows_ext, size, stride=NODES), :] = 2.0 * (im * co - re * si)

    step = 80
    parity = 1.0 - 2.0 * (lax.broadcasted_iota(jnp.int32, (step, 128), 1) & 1).astype(f32)

    def build(i):
        base = aligned(i * step, NODES)

        def shot(m, a):
            return c_ref[pl.ds(aligned(a * rows_ext + base + (HALO - m) * NODES, NODES), step), :]

        parts = [
            (shot(0, 0) - shot(2, 0)) - parity * (shot(1, 1) - shot(3, 1)),
            (shot(0, 1) - shot(2, 1)) + parity * (shot(1, 0) - shot(3, 0)),
            (shot(0, 2) + shot(2, 2)) - parity * (shot(1, 2) + shot(3, 2)),
            (shot(0, 3) + shot(2, 3)) - parity * (shot(1, 3) + shot(3, 3)),
        ]
        for a in range(4):
            hi, lo = split(parts[a])
            lh_ref[pl.ds(base, step), ORDER[a] * 128 : (ORDER[a] + 1) * 128] = hi
            ll_ref[pl.ds(base, step), ORDER[a] * 128 : (ORDER[a] + 1) * 128] = lo

    for i in range(rows_ext // 64):
        base = aligned(i * 64, 64)
        target = aligned(rows_frames + base, 32)
        for a in range(4):
            hi, lo = split(c_ref[pl.ds(aligned(a * rows_ext + base, 64), 64), :])
            lh_ref[pl.ds(target, 64), ORDER[a] * 128 : (ORDER[a] + 1) * 128] = hi
            ll_ref[pl.ds(target, 64), ORDER[a] * 128 : (ORDER[a] + 1) * 128] = lo

    width = 256
    lane = lax.broadcasted_iota(jnp.int32, (NODES, width), 1)
    mirror = 127 - lax.broadcasted_iota(jnp.int32, (NODES, 128), 1)

    def reverse(x):
        tiles = [x[:, i : i + 128] for i in range(0, x.shape[1], 128)]
        return jnp.concatenate([jnp.take_along_axis(t, mirror, axis=1) for t in tiles[::-1]], 1)

    def pair(row, size, c):
        cols = pl.ds(aligned(c * width, width), width)
        rows = pl.ds(row, size)
        return (
            product(lh_ref[rows, :256], ll_ref[rows, :256], fh_ref[0, :, cols], fl_ref[0, :, cols]),
            product(lh_ref[rows, 256:], ll_ref[rows, 256:], fh_ref[1, :, cols], fl_ref[1, :, cols]),
        )

    def columns(c):
        return aligned(512 + c * width, width), aligned(256 - c * width, width)

    loads[0].wait()
    loads[1].wait()
    half_ext = rows_ext // 2

    for i in range(4):
        m, c = i // 2, i % 2
        even, odd = pair(aligned(rows_frames + m * half_ext, 16), half_ext, c)
        upper, lower = columns(c)
        for s in range(EXT // 2):
            rows = slice(s * NODES, (s + 1) * NODES)
            place = pl.ds(aligned(m * half_ext + s * NODES, NODES), NODES)
            d = d_ref[m * (EXT // 2) + s]
            q_ref[place, pl.ds(upper, width)] = jnp.where(lane < d - upper, even[rows] + odd[rows], 0.0)
            q_ref[place, pl.ds(lower, width)] = jnp.where(lane < d - lower, reverse(even[rows] - odd[rows]), 0.0)

    for i in range(rows_frames // step):
        build(i)

    fetch.wait()
    fetch_head.wait()
    half_frames = rows_frames // 2

    for i in range(4):
        m, c = i // 2, i % 2
        even, odd = pair(aligned(m * half_frames, 16), half_frames, c)
        upper, lower = columns(c)
        for f in range(FRAMES // 2):
            rows = slice(f * NODES, (f + 1) * NODES)
            first = m * half_frames + f * NODES
            now = pl.ds(aligned(first, NODES), NODES)
            ahead = pl.ds(aligned(first + HALO * NODES, NODES), NODES)
            start = (m * (FRAMES // 2) + f) * FRAME
            for col, out in ((upper, even[rows] + odd[rows]), (lower, reverse(even[rows] - odd[rows]))):
                cols = pl.ds(col, width)
                place = pl.ds(aligned(start + col, width), width)
                g_ref[:, place] = g_ref[:, place] - out + (q_ref[ahead, cols] - q_ref[now, cols])

    store = pltpu.make_async_copy(g_ref.at[:, pl.ds(0, local)], mis_ref, out_sem)
    store.start()

    wide = lax.broadcasted_iota(jnp.int32, (NODES, FRAME), 1)

    def put(row, first, second):
        folded = []
        for x in (first, second):
            back = reverse(x[:, :512])
            folded.append(jnp.concatenate([x[:, 512:] + back, x[:, 512:] - back], 1))
        hi, lo = split(jnp.concatenate(folded, 0))
        mh_ref[pl.ds(row, 16), :] = hi
        ml_ref[pl.ds(row, 16), :] = lo

    def frame_at(f):
        return g_ref[:, pl.ds(aligned(f * FRAME, FRAME), FRAME)]

    inside = last_ref[0] == 0

    def residual(f):
        x = frame_at(f)
        return x if f < SHOTS else jnp.where(inside, x, 0.0)

    total = rows_frames + rows_local
    half = total // 2

    def adjoint(i):
        rows = slice(i * half, (i + 1) * half)
        for part in range(2):
            cols = slice(part * 512, (part + 1) * 512)
            out = product(mh_ref[rows, cols], ml_ref[rows, cols], ah_ref[part], al_ref[part])
            for k in range(2):
                place = (2 * k + part) * total + i * half
                sp_ref[place : place + half, :] = out[:, k * 128 : (k + 1) * 128]

    def edge_of(f):
        return jnp.where(wide < d_ref[f + HALO], residual(f + HALO) - residual(f), 0.0)

    for f in range(0, FRAMES, 2):
        put(f * NODES, residual(f), residual(f + 1))
    loads[2].wait()
    loads[3].wait()
    adjoint(0)
    for f in range(0, SHOTS, 2):
        put(rows_frames + f * NODES, edge_of(f), edge_of(f + 1))
    adjoint(1)

    band = 48
    sign = 1.0 - 2.0 * (lax.broadcasted_iota(jnp.int32, (band, 128), 1) & 1).astype(f32)

    for i in range(rows_local // band):
        base = aligned(i * band, NODES)

        def frame(m, a):
            return sp_ref[pl.ds(aligned(a * total + base + m * NODES, NODES), band), :]

        def edge(a):
            return sp_ref[pl.ds(aligned(a * total + rows_frames + base, NODES), band), :]

        parts = [
            (frame(0, 0) - frame(2, 0)) + sign * (frame(1, 1) - frame(3, 1)) + edge(0),
            (frame(0, 1) - frame(2, 1)) - sign * (frame(1, 0) - frame(3, 0)) + edge(1),
            (frame(0, 2) + frame(2, 2)) - sign * (frame(1, 2) + frame(3, 2)) + edge(2),
            (frame(0, 3) + frame(2, 3)) - sign * (frame(1, 3) + frame(3, 3)) + edge(3),
        ]
        for a in range(4):
            w_ref[pl.ds(aligned(a * rows_local + base, NODES), band), :] = parts[a]

    def emit(n):
        parts = [w_ref[pl.ds(a * rows_local + n, SHOTS, stride=NODES), :] for a in range(4)]
        outs = []
        for j in range(2):
            co = RELAX * cos_ref[HALO : HALO + SHOTS, j * 128 : (j + 1) * 128]
            si = RELAX * sin_ref[HALO : HALO + SHOTS, j * 128 : (j + 1) * 128]
            re, im = parts[2 * j], parts[2 * j + 1]
            outs += [re * co - im * si, im * co + re * si]
        for a in range(3):
            block = jnp.concatenate([outs[a], outs[3][32 * a : 32 * a + 32]], 0).T
            send_ref[pl.ds(a * NODES + n, GROUP, stride=24), :] = block

    for n in range(NODES):
        emit(n)

    send = pltpu.make_async_copy(send_ref, send_hbm, send_sem)
    send.start()
    store.wait()
    send.wait()


def signal(dither, last, recv, cos_t, sin_t, tables, head, gathers):
    vmem = pl.BlockSpec(memory_space=pltpu.VMEM)
    smem = pl.BlockSpec(memory_space=pltpu.SMEM)
    hbm = pl.BlockSpec(memory_space=pltpu.HBM)
    rows_ext, rows_frames, rows_local = EXT * NODES, FRAMES * NODES, SHOTS * NODES
    return pl.pallas_call(
        signal_kernel,
        in_specs=[smem, smem, vmem, vmem, vmem, hbm, hbm, hbm, hbm, hbm, hbm],
        out_specs=[hbm, hbm],
        out_shape=[
            pltpu.HBM((NODES, SHOTS * FRAME), f32),
            pltpu.HBM((GROUP * 24, 128), f32),
        ],
        scratch_shapes=[
            pltpu.VMEM((4 * rows_ext, 128), f32),
            pltpu.VMEM((NODES, FRAMES * FRAME), f32),
            pltpu.VMEM((rows_ext, FRAME), f32),
            pltpu.VMEM((256, 128), f32),
            pltpu.VMEM((rows_frames + rows_ext, 512), bf16),
            pltpu.VMEM((rows_frames + rows_ext, 512), bf16),
            pltpu.VMEM((rows_frames + rows_local, FRAME), bf16),
            pltpu.VMEM((rows_frames + rows_local, FRAME), bf16),
            pltpu.VMEM((4 * (rows_frames + rows_local), 128), f32),
            pltpu.VMEM((4 * rows_local, 128), f32),
            pltpu.VMEM((GROUP * 24, 128), f32),
            pltpu.VMEM((2, 256, 512), bf16),
            pltpu.VMEM((2, 256, 512), bf16),
            pltpu.VMEM((2, 512, 256), bf16),
            pltpu.VMEM((2, 512, 256), bf16),
            pltpu.SemaphoreType.DMA,
            pltpu.SemaphoreType.DMA,
            pltpu.SemaphoreType.DMA,
            pltpu.SemaphoreType.DMA,
            pltpu.SemaphoreType.DMA((4,)),
        ],
        compiler_params=pltpu.CompilerParams(vmem_limit_bytes=40 << 20),
        name="signal",
    )(dither, last, recv, cos_t, sin_t, *[keep(t) for t in tables], keep(head), keep(gathers))


def rank_kernel(recv_ref, est_ref, w_hbm, out_hbm, ah_ref, al_ref, out_ref, w_ref, out_sem, w_sem):
    load_w = pltpu.make_async_copy(w_hbm, w_ref, w_sem)
    load_w.start()
    lane = lax.broadcasted_iota(jnp.int32, (NODES, 128), 1)
    chunk = lane // 32

    def planes(p):
        rows = pl.ds(aligned(p * NODES, NODES), NODES)
        values, extras = [], []
        for a in range(3):
            t = []
            for q in range(4):
                tile = recv_ref[pl.ds(aligned((p * 4 + q) * 24 + a * NODES, NODES), NODES), :]
                t.append(pltpu.roll(tile, (96 * q) % 128, axis=1) if q else tile)
            values.append([
                jnp.where(lane < 96, t[0], t[1]),
                jnp.where(lane < 64, t[1], t[2]),
                jnp.where(lane < 32, t[2], t[3]),
            ])
            e = jnp.where(chunk == 0, t[3], jnp.where(chunk == 1, t[2], jnp.where(chunk == 2, t[1], t[0])))
            extras.append(pltpu.roll(e, 32 * (a + 1), axis=1) if a < 3 else e)
        values.append([])
        for i in range(3):
            x = extras[(4 * i) % 3]
            for k in range(1, 4):
                x = jnp.where(chunk == k, extras[(4 * i + k) % 3], x)
            values[3].append(x)
        return [
            [est_ref[a, rows, i * 128 : (i + 1) * 128] + values[a][i] for i in range(3)] for a in range(4)
        ]

    def unpack(p):
        upper, lower = planes(2 * p), planes(2 * p + 1)
        rows = pl.ds(aligned(p * 16, 16), 16)
        for a in range(4):
            for i in range(3):
                hi, lo = split(jnp.concatenate([upper[a][i], lower[a][i]], 0))
                cols = slice((a % 2) * 384 + i * 128, (a % 2) * 384 + (i + 1) * 128)
                ah_ref[a // 2, rows, cols] = hi
                al_ref[a // 2, rows, cols] = lo

    @pl.loop(0, 4)
    def _(p):
        for i in range(4):
            unpack(4 * p + i)

    load_w.wait()

    dot = functools.partial(jnp.dot, preferred_element_type=f32)
    lane_r = lax.broadcasted_iota(jnp.int32, (64, 128), 1)
    row_r = lax.broadcasted_iota(jnp.int32, (64, 128), 0)
    flip = jnp.where(lane_r < 64, 1.0, -1.0).astype(f32)
    diagonal = (lane_r == row_r) & (row_r < RANK)
    systems = []
    rights = []
    basis = []
    for j in range(2):
        yy = dot(ah_ref[j], w_ref[...])
        y = yy[:, :128] + yy[:, 128:] + dot(al_ref[j], w_ref[:, :128])
        basis.append(split(y))
        yt = y.T
        g = jnp.dot(yt, y, precision=highest, preferred_element_type=f32)
        g = g[:64] + flip * pltpu.roll(g[64:], 64, axis=1)
        trace = jnp.sum(jnp.where(diagonal, g, 0.0))
        g = jnp.where(diagonal, g + RIDGE * trace / RANK, g)
        eye = jnp.where(diagonal, 1.0, 0.0).astype(f32)
        systems.append([g[:RANK], eye[:RANK]])
        yh, yl = split(yt)
        c = dot(jnp.concatenate([yh, yl], 0), ah_ref[j])
        c = c[:128] + c[128:] + dot(yh, al_ref[j])
        rights.append(jnp.concatenate([c[:64, :384] + c[64:, 384:], c[:64, 384:] - c[64:, :384]], 0))

    neg = jnp.where(lax.broadcasted_iota(jnp.int32, (NODES, 128), 1) < 64, -1.0, 1.0).astype(f32)
    row_i = lax.broadcasted_iota(jnp.int32, (NODES, 128), 0)
    groups = RANK // NODES
    state = [
        ([g[i * NODES : (i + 1) * NODES] for i in range(groups)], [w[i * NODES : (i + 1) * NODES] for i in range(groups)])
        for g, w in systems
    ]

    def row(x, k):
        return jnp.broadcast_to(x[k % NODES : k % NODES + 1], (NODES, 128))

    def column(x, k):
        return jnp.broadcast_to(x[:, k : k + 1], (NODES, 128))

    def gathered(x, k):
        return jnp.take_along_axis(x, jnp.full((NODES, 128), k, jnp.int32), axis=1)

    def turned(x):
        return neg * pltpu.roll(x, 64, axis=1)

    for k in range(0, RANK, 2):
        top = k // NODES
        for gs, ws in state:
            gt, wt = turned(gs[top]), turned(ws[top])
            cols = [
                [(gathered if i == top else column)(gs[i], c) for c in (k, 64 + k, k + 1, 65 + k)]
                for i in range(top, groups)
            ]
            a = row(cols[0][0], k)
            br, bi = row(cols[0][2], k), row(cols[0][3], k)
            d = row(cols[0][2], k + 1)
            ia = 1.0 / a
            lr, li = br * ia, -bi * ia
            second = 1.0 / (d - (br * br + bi * bi) * ia)
            g0, g0i, w0, w0i = row(gs[top], k), row(gt, k), row(ws[top], k), row(wt, k)
            g1 = row(gs[top], k + 1) - (lr * g0 + li * g0i)
            g1i = row(gt, k + 1) - (lr * g0i - li * g0)
            w1 = row(ws[top], k + 1) - (lr * w0 + li * w0i)
            w1i = row(wt, k + 1) - (lr * w0i - li * w0)
            for i in range(top, groups):
                c0r, c0i, c1r, c1i = cols[i - top]
                f0r, f0i = c0r * ia, c0i * ia
                f1r = (c1r - (f0r * br - f0i * bi)) * second
                f1i = (c1i - (f0r * bi + f0i * br)) * second
                if i == top:
                    f0r, f0i = jnp.where(row_i > k % NODES, f0r, 0.0), jnp.where(row_i > k % NODES, f0i, 0.0)
                    f1r, f1i = jnp.where(row_i > k % NODES + 1, f1r, 0.0), jnp.where(row_i > k % NODES + 1, f1i, 0.0)
                gs[i] = gs[i] - ((f0r * g0 + f0i * g0i) + (f1r * g1 + f1i * g1i))
                ws[i] = ws[i] - ((f0r * w0 + f0i * w0i) + (f1r * w1 + f1i * w1i))
    systems = [[jnp.concatenate(gs, 0), jnp.concatenate(ws, 0)] for gs, ws in state]

    def two(left, right):
        lh, ll = split(left)
        rh, rl = split(right)
        return dot(jnp.concatenate([lh, ll], 1), jnp.concatenate([rh, rh], 0)) + dot(lh, rl)

    stores = []
    for j in range(2):
        g, w = systems[j]
        d = jnp.sum(jnp.where(diagonal[:RANK], g, 0.0), axis=1, keepdims=True)
        w = w * lax.rsqrt(d)
        w = jnp.concatenate([w, jnp.zeros((16, 128), f32)], 0)
        left = jnp.concatenate([flip * w, pltpu.roll(w, 64, axis=1)], 0)
        x = two(left.T, two(left, rights[j]))
        x = jnp.concatenate(
            [jnp.concatenate([x[:64], -x[64:]], 0), jnp.concatenate([x[64:], x[:64]], 0)], 1
        )
        xh, xl = split(x)
        yh, yl = basis[j]
        low = dot(jnp.concatenate([yh, yl], 1), jnp.concatenate([xh, xh], 0)) + dot(yh, xl)
        out_ref[2 * j] = low[:, :384]
        out_ref[2 * j + 1] = low[:, 384:]
        stores.append(
            pltpu.make_async_copy(out_ref.at[pl.ds(2 * j, 2)], out_hbm.at[pl.ds(2 * j, 2)], out_sem.at[j])
        )
        stores[-1].start()
    for store in stores:
        store.wait()


def rank_reduce(recv, est, w):
    vmem = pl.BlockSpec(memory_space=pltpu.VMEM)
    hbm = pl.BlockSpec(memory_space=pltpu.HBM)
    return pl.pallas_call(
        rank_kernel,
        in_specs=[vmem, vmem, hbm],
        out_specs=hbm,
        out_shape=pltpu.HBM((4, 256, 384), f32),
        scratch_shapes=[
            pltpu.VMEM((2, 256, 768), bf16),
            pltpu.VMEM((2, 256, 768), bf16),
            pltpu.VMEM((4, 256, 384), f32),
            pltpu.VMEM((768, 256), bf16),
            pltpu.SemaphoreType.DMA((2,)),
            pltpu.SemaphoreType.DMA,
        ],
        compiler_params=pltpu.CompilerParams(vmem_limit_bytes=20 << 20),
        name="rank",
    )(recv, est, keep(w))


def table(rows_first):
    half = FRAME // 2
    fine = 128 if rows_first else 64
    row = lax.iota(jnp.int32, 256)
    k = 2 * (row % 128) + row // 128 + 1
    near = 2 * lax.iota(jnp.int32, fine) + 1
    far = 2 * fine * lax.iota(jnp.int32, half // fine)
    if rows_first:
        phases = k[:, None] * near[None, :], k[:, None] * far[None, :]
    else:
        phases = near[:, None] * k[None, :], far[:, None] * k[None, :]
    angles = [math.pi / SPAN * (p % (2 * SPAN)).astype(f32) for p in phases]
    scale = 1.0 / math.sqrt(SPAN)
    cn, sn = jnp.cos(angles[0]) * scale, jnp.sin(angles[0]) * scale
    cf, sf = jnp.cos(angles[1]), jnp.sin(angles[1])
    cn, sn, cf, sf = lax.optimization_barrier((cn, sn, cf, sf))
    if rows_first:
        pieces = [
            (cn * cf[:, i : i + 1] - sn * sf[:, i : i + 1], -(sn * cf[:, i : i + 1] + cn * sf[:, i : i + 1]))
            for i in range(half // fine)
        ]
        value = jnp.stack([jnp.concatenate([p[j] for p in pieces], 1) for j in range(2)])
    else:
        cn, sn, cf, sf = cn[None], sn[None], cf[:, None], sf[:, None]
        value = jnp.stack([cn * cf - sn * sf, -(sn * cf + cn * sf)]).reshape(2, half, 256)
    hi = lax.reduce_precision(value, 8, 7)
    return hi.astype(bf16), (value - hi).astype(bf16)


def shards(receiver_gathers, fourier_estimate, random_projector, release_sample):
    q = lax.axis_index("freq")
    est = fourier_estimate.reshape(4, 32, NODES, 4 * SHOTS)
    send = pack(est).reshape(GROUP, ROWS // 2, 2, 128)
    recv = lax.all_to_all(send, ("node", "freq"), split_axis=0, concat_axis=0, tiled=True)

    up = [(0, 1), (1, 2), (2, 3)]
    down = [(1, 0), (2, 1), (3, 2)]
    starts = jnp.broadcast_to(jnp.pad(release_sample[:HALO].astype(f32), (0, 124))[None], (NODES, 128))
    head = lax.ppermute(
        jnp.concatenate([receiver_gathers[:, : HALO * FRAME], starts], 1), "freq", down
    )
    release_before = lax.ppermute(release_sample[SHOTS - HALO :], "freq", up)
    release_after = head[0, HALO * FRAME : HALO * FRAME + HALO].astype(jnp.int32)
    dither = jnp.concatenate([release_before, release_sample, release_after]) % FRAME
    src = lax.iota(jnp.int32, 256)
    k = 2 * (src % 128) + src // 128 + 1
    angle = math.pi / SPAN * (k[None, :] * (2 * dither - FRAME + 1)[:, None] % (2 * SPAN)).astype(f32)
    cos_t, sin_t = jnp.cos(angle), jnp.sin(angle)
    tables = table(True) + table(False)
    last = (q == 3).astype(jnp.int32).reshape(1)
    misfit, back = signal(dither, last, recv.reshape(GROUP * ROWS, 128), cos_t, sin_t, tables, head, receiver_gathers)

    arrived = lax.all_to_all(
        back.reshape(GROUP, 24, 128), ("node", "freq"), split_axis=0, concat_axis=0, tiled=True
    )
    omega = jnp.pad(random_projector, ((0, 0), (0, 16)))
    zero = jnp.zeros_like(omega)
    w = jnp.concatenate([jnp.concatenate([omega, zero], 1), jnp.concatenate([zero, omega], 1)], 0)
    hi = lax.reduce_precision(w, 8, 7)
    w = jnp.concatenate([hi.astype(bf16), (w - hi).astype(bf16)], 1)
    low = rank_reduce(arrived.reshape(GROUP * 24, 128), fourier_estimate.reshape(4, 256, 384), w)
    return low.reshape(2, 2, 256, 384), misfit


def solution(mesh):
    return jax.shard_map(
        shards,
        mesh=mesh,
        in_specs=(P("node", "freq"), P(("node", "freq"), None, None, None), P(), P("freq")),
        out_specs=(P(("node", "freq"), None, None, None), P("node", "freq")),
        check_vma=False,
    )
```

```python
import functools
import math

import jax
import jax.numpy as jnp
from jax import lax
from jax.experimental import pallas as pl
from jax.experimental.pallas import tpu as pltpu
from jax.sharding import PartitionSpec as P


SPAN = 4096
FRAME = 1024
RANK = 48
HALO = 4
SHOTS = 96
NODES = 8
EXT = SHOTS + 2 * HALO
FRAMES = SHOTS + HALO
GROUP = 128
ROWS = 26
PACK_CHUNKS = 4
ORDER = (0, 2, 1, 3)
RELAX = 0.25
RIDGE = 0.001
highest = lax.Precision.HIGHEST
f32 = jnp.float32
bf16 = jnp.bfloat16


def keep(x):
    return pltpu.with_memory_space_constraint(x, pltpu.HBM)


def aligned(x, n):
    return x if isinstance(x, int) else pl.multiple_of(x, n)


def split(x):
    hi = x.astype(bf16)
    lo = (x - hi.astype(f32)).astype(bf16)
    return hi, lo


def pack_kernel(x_hbm, o_hbm, x_ref, o_ref, in_sem, out_sem):
    chunks = PACK_CHUNKS
    count = 32 // chunks
    size = count * 4 * ROWS
    lane = lax.broadcasted_iota(jnp.int32, (1, NODES, 128), 2)
    node = lax.broadcasted_iota(jnp.int32, (1, NODES, 128), 1)
    slot = lane // 32
    own = slot == node % 4
    shape = (count, NODES, 128)

    def load(i):
        part = pl.ds(i * count, count)
        return pltpu.make_async_copy(x_hbm.at[:, part], x_ref.at[:, part], in_sem.at[i])

    def store(i):
        part = pl.ds(aligned(i * size, 8), size)
        return pltpu.make_async_copy(o_ref.at[part], o_hbm.at[part], out_sem.at[i])

    def pick(mask, x, y):
        return jnp.where(jnp.broadcast_to(mask, shape), x, y)

    def turn(v, by):
        return pltpu.roll(v, by % 128, axis=2) if by % 128 else v

    for i in range(chunks):
        load(i).start()

    @pl.loop(0, chunks)
    def _(step):
        load(step).wait()
        blocks = pl.ds(step * count, count)
        x = [[x_ref[a, blocks, :, i * 128 : (i + 1) * 128] for i in range(3)] for a in range(4)]
        zero = jnp.zeros(shape, f32)
        edges = zero
        for k in range(3):
            for a in range(4):
                moved = turn(x[a][k], 32 * k + 8 * a - (92 - 32 * k))
                edges = pick(lane // 8 == 4 * k + a, moved, edges)
        turned = [turn(edges, 32 * r) for r in range(4)]

        def spread(k):
            v = turned[(0 - k) % 4]
            for m in range(1, 4):
                v = pick(slot == m, turned[(m - k) % 4], v)
            return pick(own, v, zero)

        spreads = [spread(k) for k in range(3)]

        def put(row, value, size):
            for p in range(count):
                o_ref[pl.ds(aligned(step * chunk_rows, 8) + p * 4 * ROWS + row, size), :] = value[p]

        chunk_rows = size
        for q in range(4):
            for a in range(3):
                if q == 0:
                    main = x[a][0]
                elif q == 3:
                    main = turn(x[a][2], 96)
                else:
                    main = pick(lane < 32 * q, turn(x[a][q - 1], 32 * q), turn(x[a][q], 32 * q))
                m = 3 * q + a
                rest = turn(x[3][m // 4], 32 * (3 - m % 4))
                put(q * ROWS + NODES * a, pick(lane < SHOTS, main, rest), NODES)
            before = spreads[q - 1] if q > 0 else zero
            after = spreads[q] if q < 3 else zero
            halo = pick(lane % 8 < 4, before, after)
            halo = halo + pltpu.roll(halo, 1, axis=1)
            halo = halo + pltpu.roll(halo, 2, axis=1)
            put(q * ROWS + 24, halo[:, 3:4], 1)
            put(q * ROWS + 25, halo[:, 7:8], 1)
        store(step).start()

    for i in range(chunks):
        store(i).wait()


def pack(x):
    hbm = pl.BlockSpec(memory_space=pltpu.HBM)
    return pl.pallas_call(
        pack_kernel,
        in_specs=[hbm],
        out_specs=hbm,
        out_shape=pltpu.HBM((GROUP * ROWS, 128), f32),
        scratch_shapes=[
            pltpu.VMEM((4, 32, NODES, 4 * SHOTS), f32),
            pltpu.VMEM((GROUP * ROWS, 128), f32),
            pltpu.SemaphoreType.DMA((PACK_CHUNKS,)),
            pltpu.SemaphoreType.DMA((PACK_CHUNKS,)),
        ],
        name="pack",
    )(keep(x))


def product(hi, lo, th, tl):
    return jnp.dot(
        jnp.concatenate([hi, lo, hi], 1), jnp.concatenate([th, th, tl], 0), preferred_element_type=f32
    )


def signal_kernel(
    d_ref, last_ref, recv_ref, cos_ref, sin_ref, fh_hbm, fl_hbm, ah_hbm, al_hbm, head_ref, gath_ref,
    mis_ref, send_hbm,
    c_ref, g_ref, q_ref, h_ref, lh_ref, ll_ref, mh_ref, ml_ref, sp_ref, w_ref, send_ref,
    fh_ref, fl_ref, ah_ref, al_ref, in_sem, head_sem, out_sem, send_sem, table_sem,
):
    rows_ext = EXT * NODES
    rows_frames = FRAMES * NODES
    rows_local = SHOTS * NODES
    local = SHOTS * FRAME
    loads = [
        pltpu.make_async_copy(src, dst, table_sem.at[i])
        for i, (src, dst) in enumerate(
            [(fh_hbm, fh_ref), (fl_hbm, fl_ref), (ah_hbm, ah_ref), (al_hbm, al_ref)]
        )
    ]
    loads[0].start()
    loads[1].start()
    fetch = pltpu.make_async_copy(gath_ref, g_ref.at[:, pl.ds(0, local)], in_sem)
    fetch.start()
    fetch_head = pltpu.make_async_copy(head_ref.at[:, pl.ds(0, HALO * FRAME)], g_ref.at[:, pl.ds(local, HALO * FRAME)], head_sem)
    fetch_head.start()
    loads[2].start()
    loads[3].start()

    for i in range(2):
        h_ref[i * 128 : (i + 1) * 128, :] = recv_ref[pl.ds(24 + i, GROUP, stride=ROWS), :].T

    for n in range(NODES):
        blocks = [recv_ref[pl.ds(a * NODES + n, GROUP, stride=ROWS), :].T for a in range(3)]
        planes = [b[:SHOTS] for b in blocks] + [jnp.concatenate([b[SHOTS:] for b in blocks], 0)]
        halo = aligned(n * 32, 32)
        pieces = [
            (HALO, SHOTS, planes),
            (0, HALO, [h_ref[pl.ds(halo + 8 * a, HALO), :] for a in range(4)]),
            (HALO + SHOTS, HALO, [h_ref[pl.ds(halo + 8 * a + HALO, HALO), :] for a in range(4)]),
        ]
        for first, size, values in pieces:
            for j in range(2):
                re, im = values[2 * j], values[2 * j + 1]
                co = cos_ref[first : first + size, j * 128 : (j + 1) * 128]
                si = sin_ref[first : first + size, j * 128 : (j + 1) * 128]
                place = 2 * j * rows_ext + first * NODES + n
                c_ref[pl.ds(place, size, stride=NODES), :] = 2.0 * (re * co + im * si)
                c_ref[pl.ds(place + rows_ext, size, stride=NODES), :] = 2.0 * (im * co - re * si)

    step = 80
    parity = 1.0 - 2.0 * (lax.broadcasted_iota(jnp.int32, (step, 128), 1) & 1).astype(f32)

    def build(i):
        base = aligned(i * step, NODES)

        def shot(m, a):
            return c_ref[pl.ds(aligned(a * rows_ext + base + (HALO - m) * NODES, NODES), step), :]

        parts = [
            (shot(0, 0) - shot(2, 0)) - parity * (shot(1, 1) - shot(3, 1)),
            (shot(0, 1) - shot(2, 1)) + parity * (shot(1, 0) - shot(3, 0)),
            (shot(0, 2) + shot(2, 2)) - parity * (shot(1, 2) + shot(3, 2)),
            (shot(0, 3) + shot(2, 3)) - parity * (shot(1, 3) + shot(3, 3)),
        ]
        for a in range(4):
            hi, lo = split(parts[a])
            lh_ref[pl.ds(base, step), ORDER[a] * 128 : (ORDER[a] + 1) * 128] = hi
            ll_ref[pl.ds(base, step), ORDER[a] * 128 : (ORDER[a] + 1) * 128] = lo

    for i in range(rows_ext // 64):
        base = aligned(i * 64, 64)
        target = aligned(rows_frames + base, 32)
        for a in range(4):
            hi, lo = split(c_ref[pl.ds(aligned(a * rows_ext + base, 64), 64), :])
            lh_ref[pl.ds(target, 64), ORDER[a] * 128 : (ORDER[a] + 1) * 128] = hi
            ll_ref[pl.ds(target, 64), ORDER[a] * 128 : (ORDER[a] + 1) * 128] = lo

    width = 256
    lane = lax.broadcasted_iota(jnp.int32, (NODES, width), 1)
    mirror = 127 - lax.broadcasted_iota(jnp.int32, (NODES, 128), 1)

    def reverse(x):
        tiles = [x[:, i : i + 128] for i in range(0, x.shape[1], 128)]
        return jnp.concatenate([jnp.take_along_axis(t, mirror, axis=1) for t in tiles[::-1]], 1)

    def pair(row, size, c):
        cols = pl.ds(aligned(c * width, width), width)
        rows = pl.ds(row, size)
        return (
            product(lh_ref[rows, :256], ll_ref[rows, :256], fh_ref[0, :, cols], fl_ref[0, :, cols]),
            product(lh_ref[rows, 256:], ll_ref[rows, 256:], fh_ref[1, :, cols], fl_ref[1, :, cols]),
        )

    def columns(c):
        return aligned(512 + c * width, width), aligned(256 - c * width, width)

    loads[0].wait()
    loads[1].wait()
    half_ext = rows_ext // 2

    for i in range(4):
        m, c = i // 2, i % 2
        even, odd = pair(aligned(rows_frames + m * half_ext, 16), half_ext, c)
        upper, lower = columns(c)
        for s in range(EXT // 2):
            rows = slice(s * NODES, (s + 1) * NODES)
            place = pl.ds(aligned(m * half_ext + s * NODES, NODES), NODES)
            d = d_ref[m * (EXT // 2) + s]
            q_ref[place, pl.ds(upper, width)] = jnp.where(lane < d - upper, even[rows] + odd[rows], 0.0)
            q_ref[place, pl.ds(lower, width)] = jnp.where(lane < d - lower, reverse(even[rows] - odd[rows]), 0.0)

    for i in range(rows_frames // step):
        build(i)

    fetch.wait()
    fetch_head.wait()
    half_frames = rows_frames // 2

    for i in range(4):
        m, c = i // 2, i % 2
        even, odd = pair(aligned(m * half_frames, 16), half_frames, c)
        upper, lower = columns(c)
        for f in range(FRAMES // 2):
            rows = slice(f * NODES, (f + 1) * NODES)
            first = m * half_frames + f * NODES
            now = pl.ds(aligned(first, NODES), NODES)
            ahead = pl.ds(aligned(first + HALO * NODES, NODES), NODES)
            start = (m * (FRAMES // 2) + f) * FRAME
            for col, out in ((upper, even[rows] + odd[rows]), (lower, reverse(even[rows] - odd[rows]))):
                cols = pl.ds(col, width)
                place = pl.ds(aligned(start + col, width), width)
                g_ref[:, place] = g_ref[:, place] - out + (q_ref[ahead, cols] - q_ref[now, cols])

    store = pltpu.make_async_copy(g_ref.at[:, pl.ds(0, local)], mis_ref, out_sem)
    store.start()

    wide = lax.broadcasted_iota(jnp.int32, (NODES, FRAME), 1)

    def put(row, first, second):
        folded = []
        for x in (first, second):
            back = reverse(x[:, :512])
            folded.append(jnp.concatenate([x[:, 512:] + back, x[:, 512:] - back], 1))
        hi, lo = split(jnp.concatenate(folded, 0))
        mh_ref[pl.ds(row, 16), :] = hi
        ml_ref[pl.ds(row, 16), :] = lo

    def frame_at(f):
        return g_ref[:, pl.ds(aligned(f * FRAME, FRAME), FRAME)]

    inside = last_ref[0] == 0

    def residual(f):
        x = frame_at(f)
        return x if f < SHOTS else jnp.where(inside, x, 0.0)

    total = rows_frames + rows_local
    half = total // 2

    def adjoint(i):
        rows = slice(i * half, (i + 1) * half)
        for part in range(2):
            cols = slice(part * 512, (part + 1) * 512)
            out = product(mh_ref[rows, cols], ml_ref[rows, cols], ah_ref[part], al_ref[part])
            for k in range(2):
                place = (2 * k + part) * total + i * half
                sp_ref[place : place + half, :] = out[:, k * 128 : (k + 1) * 128]

    def edge_of(f):
        return jnp.where(wide < d_ref[f + HALO], residual(f + HALO) - residual(f), 0.0)

    for f in range(0, FRAMES, 2):
        put(f * NODES, residual(f), residual(f + 1))
    loads[2].wait()
    loads[3].wait()
    adjoint(0)
    for f in range(0, SHOTS, 2):
        put(rows_frames + f * NODES, edge_of(f), edge_of(f + 1))
    adjoint(1)

    band = 48
    sign = 1.0 - 2.0 * (lax.broadcasted_iota(jnp.int32, (band, 128), 1) & 1).astype(f32)

    for i in range(rows_local // band):
        base = aligned(i * band, NODES)

        def frame(m, a):
            return sp_ref[pl.ds(aligned(a * total + base + m * NODES, NODES), band), :]

        def edge(a):
            return sp_ref[pl.ds(aligned(a * total + rows_frames + base, NODES), band), :]

        parts = [
            (frame(0, 0) - frame(2, 0)) + sign * (frame(1, 1) - frame(3, 1)) + edge(0),
            (frame(0, 1) - frame(2, 1)) - sign * (frame(1, 0) - frame(3, 0)) + edge(1),
            (frame(0, 2) + frame(2, 2)) - sign * (frame(1, 2) + frame(3, 2)) + edge(2),
            (frame(0, 3) + frame(2, 3)) - sign * (frame(1, 3) + frame(3, 3)) + edge(3),
        ]
        for a in range(4):
            w_ref[pl.ds(aligned(a * rows_local + base, NODES), band), :] = parts[a]

    def spectrum(n, a, first, size):
        j = a // 2
        re, im = w_ref[pl.ds(2 * j * rows_local + n + first * NODES, size, stride=NODES), :], w_ref[
            pl.ds((2 * j + 1) * rows_local + n + first * NODES, size, stride=NODES), :
        ]
        shots = slice(HALO + first, HALO + first + size)
        co = RELAX * cos_ref[shots, j * 128 : (j + 1) * 128]
        si = RELAX * sin_ref[shots, j * 128 : (j + 1) * 128]
        return re * co - im * si if a % 2 == 0 else im * co + re * si

    sends = []
    for a in range(3):
        for n in range(NODES):
            block = jnp.concatenate([spectrum(n, a, 0, SHOTS), spectrum(n, 3, 32 * a, 32)], 0).T
            send_ref[pl.ds(a * NODES + n, GROUP, stride=24), :] = block
        part = pl.ds(a * NODES, NODES)
        sends.append(
            pltpu.make_async_copy(
                send_ref.reshape(GROUP, 24, 128).at[:, part], send_hbm.reshape(GROUP, 24, 128).at[:, part], send_sem.at[a]
            )
        )
        sends[-1].start()
    store.wait()
    for send in sends:
        send.wait()


def signal(dither, last, recv, cos_t, sin_t, tables, head, gathers):
    vmem = pl.BlockSpec(memory_space=pltpu.VMEM)
    smem = pl.BlockSpec(memory_space=pltpu.SMEM)
    hbm = pl.BlockSpec(memory_space=pltpu.HBM)
    rows_ext, rows_frames, rows_local = EXT * NODES, FRAMES * NODES, SHOTS * NODES
    return pl.pallas_call(
        signal_kernel,
        in_specs=[smem, smem, vmem, vmem, vmem, hbm, hbm, hbm, hbm, hbm, hbm],
        out_specs=[hbm, hbm],
        out_shape=[
            pltpu.HBM((NODES, SHOTS * FRAME), f32),
            pltpu.HBM((GROUP * 24, 128), f32),
        ],
        scratch_shapes=[
            pltpu.VMEM((4 * rows_ext, 128), f32),
            pltpu.VMEM((NODES, FRAMES * FRAME), f32),
            pltpu.VMEM((rows_ext, FRAME), f32),
            pltpu.VMEM((256, 128), f32),
            pltpu.VMEM((rows_frames + rows_ext, 512), bf16),
            pltpu.VMEM((rows_frames + rows_ext, 512), bf16),
            pltpu.VMEM((rows_frames + rows_local, FRAME), bf16),
            pltpu.VMEM((rows_frames + rows_local, FRAME), bf16),
            pltpu.VMEM((4 * (rows_frames + rows_local), 128), f32),
            pltpu.VMEM((4 * rows_local, 128), f32),
            pltpu.VMEM((GROUP * 24, 128), f32),
            pltpu.VMEM((2, 256, 512), bf16),
            pltpu.VMEM((2, 256, 512), bf16),
            pltpu.VMEM((2, 512, 256), bf16),
            pltpu.VMEM((2, 512, 256), bf16),
            pltpu.SemaphoreType.DMA,
            pltpu.SemaphoreType.DMA,
            pltpu.SemaphoreType.DMA,
            pltpu.SemaphoreType.DMA((3,)),
            pltpu.SemaphoreType.DMA((4,)),
        ],
        compiler_params=pltpu.CompilerParams(vmem_limit_bytes=40 << 20),
        name="signal",
    )(dither, last, recv, cos_t, sin_t, *[keep(t) for t in tables], keep(head), keep(gathers))


def rank_kernel(recv_ref, est_ref, w_hbm, out_hbm, ah_ref, al_ref, out_ref, w_ref, out_sem, w_sem):
    load_w = pltpu.make_async_copy(w_hbm, w_ref, w_sem)
    load_w.start()
    lane = lax.broadcasted_iota(jnp.int32, (NODES, 128), 1)
    chunk = lane // 32

    def planes(p):
        rows = pl.ds(aligned(p * NODES, NODES), NODES)
        values, extras = [], []
        for a in range(3):
            t = []
            for q in range(4):
                tile = recv_ref[pl.ds(aligned((p * 4 + q) * 24 + a * NODES, NODES), NODES), :]
                t.append(pltpu.roll(tile, (96 * q) % 128, axis=1) if q else tile)
            values.append([
                jnp.where(lane < 96, t[0], t[1]),
                jnp.where(lane < 64, t[1], t[2]),
                jnp.where(lane < 32, t[2], t[3]),
            ])
            e = jnp.where(chunk == 0, t[3], jnp.where(chunk == 1, t[2], jnp.where(chunk == 2, t[1], t[0])))
            extras.append(pltpu.roll(e, 32 * (a + 1), axis=1) if a < 3 else e)
        values.append([])
        for i in range(3):
            x = extras[(4 * i) % 3]
            for k in range(1, 4):
                x = jnp.where(chunk == k, extras[(4 * i + k) % 3], x)
            values[3].append(x)
        return [
            [est_ref[a, rows, i * 128 : (i + 1) * 128] + values[a][i] for i in range(3)] for a in range(4)
        ]

    def unpack(p):
        upper, lower = planes(2 * p), planes(2 * p + 1)
        rows = pl.ds(aligned(p * 16, 16), 16)
        for a in range(4):
            for i in range(3):
                hi, lo = split(jnp.concatenate([upper[a][i], lower[a][i]], 0))
                cols = slice((a % 2) * 384 + i * 128, (a % 2) * 384 + (i + 1) * 128)
                ah_ref[a // 2, rows, cols] = hi
                al_ref[a // 2, rows, cols] = lo

    @pl.loop(0, 4)
    def _(p):
        for i in range(4):
            unpack(4 * p + i)

    load_w.wait()

    dot = functools.partial(jnp.dot, preferred_element_type=f32)
    lane_r = lax.broadcasted_iota(jnp.int32, (64, 128), 1)
    row_r = lax.broadcasted_iota(jnp.int32, (64, 128), 0)
    flip = jnp.where(lane_r < 64, 1.0, -1.0).astype(f32)
    diagonal = (lane_r == row_r) & (row_r < RANK)
    systems = []
    rights = []
    basis = []
    for j in range(2):
        yy = dot(ah_ref[j], w_ref[...])
        y = yy[:, :128] + yy[:, 128:] + dot(al_ref[j], w_ref[:, :128])
        basis.append(split(y))
        yt = y.T
        g = jnp.dot(yt, y, precision=highest, preferred_element_type=f32)
        g = g[:64] + flip * pltpu.roll(g[64:], 64, axis=1)
        trace = jnp.sum(jnp.where(diagonal, g, 0.0))
        g = jnp.where(diagonal, g + RIDGE * trace / RANK, g)
        eye = jnp.where(diagonal, 1.0, 0.0).astype(f32)
        systems.append([g[:RANK], eye[:RANK]])
        yh, yl = split(yt)
        c = dot(jnp.concatenate([yh, yl], 0), ah_ref[j])
        c = c[:128] + c[128:] + dot(yh, al_ref[j])
        rights.append(jnp.concatenate([c[:64, :384] + c[64:, 384:], c[:64, 384:] - c[64:, :384]], 0))

    neg = jnp.where(lax.broadcasted_iota(jnp.int32, (NODES, 128), 1) < 64, -1.0, 1.0).astype(f32)
    row_i = lax.broadcasted_iota(jnp.int32, (NODES, 128), 0)
    groups = RANK // NODES
    state = [
        ([g[i * NODES : (i + 1) * NODES] for i in range(groups)], [w[i * NODES : (i + 1) * NODES] for i in range(groups)])
        for g, w in systems
    ]

    def row(x, k):
        return jnp.broadcast_to(x[k % NODES : k % NODES + 1], (NODES, 128))

    def column(x, k):
        return jnp.broadcast_to(x[:, k : k + 1], (NODES, 128))

    def gathered(x, k):
        return jnp.take_along_axis(x, jnp.full((NODES, 128), k, jnp.int32), axis=1)

    def turned(x):
        return neg * pltpu.roll(x, 64, axis=1)

    for k in range(0, RANK, 2):
        top = k // NODES
        for gs, ws in state:
            gt, wt = turned(gs[top]), turned(ws[top])
            cols = [
                [(gathered if i == top else column)(gs[i], c) for c in (k, 64 + k, k + 1, 65 + k)]
                for i in range(top, groups)
            ]
            a = row(cols[0][0], k)
            br, bi = row(cols[0][2], k), row(cols[0][3], k)
            d = row(cols[0][2], k + 1)
            ia = 1.0 / a
            lr, li = br * ia, -bi * ia
            second = 1.0 / (d - (br * br + bi * bi) * ia)
            g0, g0i, w0, w0i = row(gs[top], k), row(gt, k), row(ws[top], k), row(wt, k)
            g1 = row(gs[top], k + 1) - (lr * g0 + li * g0i)
            g1i = row(gt, k + 1) - (lr * g0i - li * g0)
            w1 = row(ws[top], k + 1) - (lr * w0 + li * w0i)
            w1i = row(wt, k + 1) - (lr * w0i - li * w0)
            for i in range(top, groups):
                c0r, c0i, c1r, c1i = cols[i - top]
                f0r, f0i = c0r * ia, c0i * ia
                f1r = (c1r - (f0r * br - f0i * bi)) * second
                f1i = (c1i - (f0r * bi + f0i * br)) * second
                if i == top:
                    f0r, f0i = jnp.where(row_i > k % NODES, f0r, 0.0), jnp.where(row_i > k % NODES, f0i, 0.0)
                    f1r, f1i = jnp.where(row_i > k % NODES + 1, f1r, 0.0), jnp.where(row_i > k % NODES + 1, f1i, 0.0)
                gs[i] = gs[i] - ((f0r * g0 + f0i * g0i) + (f1r * g1 + f1i * g1i))
                ws[i] = ws[i] - ((f0r * w0 + f0i * w0i) + (f1r * w1 + f1i * w1i))
    systems = [[jnp.concatenate(gs, 0), jnp.concatenate(ws, 0)] for gs, ws in state]

    def two(left, right):
        lh, ll = split(left)
        rh, rl = split(right)
        return dot(jnp.concatenate([lh, ll], 1), jnp.concatenate([rh, rh], 0)) + dot(lh, rl)

    stores = []
    for j in range(2):
        g, w = systems[j]
        d = jnp.sum(jnp.where(diagonal[:RANK], g, 0.0), axis=1, keepdims=True)
        w = w * lax.rsqrt(d)
        w = jnp.concatenate([w, jnp.zeros((16, 128), f32)], 0)
        left = jnp.concatenate([flip * w, pltpu.roll(w, 64, axis=1)], 0)
        x = two(left.T, two(left, rights[j]))
        x = jnp.concatenate(
            [jnp.concatenate([x[:64], -x[64:]], 0), jnp.concatenate([x[64:], x[:64]], 0)], 1
        )
        xh, xl = split(x)
        yh, yl = basis[j]
        low = dot(jnp.concatenate([yh, yl], 1), jnp.concatenate([xh, xh], 0)) + dot(yh, xl)
        for c in range(2):
            i = 2 * j + c
            out_ref[i] = low[:, 384 * c : 384 * (c + 1)]
            stores.append(pltpu.make_async_copy(out_ref.at[i], out_hbm.at[i], out_sem.at[i]))
            stores[-1].start()
    for store in stores:
        store.wait()


def rank_reduce(recv, est, w):
    vmem = pl.BlockSpec(memory_space=pltpu.VMEM)
    hbm = pl.BlockSpec(memory_space=pltpu.HBM)
    return pl.pallas_call(
        rank_kernel,
        in_specs=[vmem, vmem, hbm],
        out_specs=hbm,
        out_shape=pltpu.HBM((4, 256, 384), f32),
        scratch_shapes=[
            pltpu.VMEM((2, 256, 768), bf16),
            pltpu.VMEM((2, 256, 768), bf16),
            pltpu.VMEM((4, 256, 384), f32),
            pltpu.VMEM((768, 256), bf16),
            pltpu.SemaphoreType.DMA((4,)),
            pltpu.SemaphoreType.DMA,
        ],
        compiler_params=pltpu.CompilerParams(vmem_limit_bytes=20 << 20),
        name="rank",
    )(recv, est, keep(w))


def table(rows_first):
    half = FRAME // 2
    fine = 128 if rows_first else 64
    row = lax.iota(jnp.int32, 256)
    k = 2 * (row % 128) + row // 128 + 1
    near = 2 * lax.iota(jnp.int32, fine) + 1
    far = 2 * fine * lax.iota(jnp.int32, half // fine)
    if rows_first:
        phases = k[:, None] * near[None, :], k[:, None] * far[None, :]
    else:
        phases = near[:, None] * k[None, :], far[:, None] * k[None, :]
    angles = [math.pi / SPAN * (p % (2 * SPAN)).astype(f32) for p in phases]
    scale = 1.0 / math.sqrt(SPAN)
    cn, sn = jnp.cos(angles[0]) * scale, jnp.sin(angles[0]) * scale
    cf, sf = jnp.cos(angles[1]), jnp.sin(angles[1])
    cn, sn, cf, sf = lax.optimization_barrier((cn, sn, cf, sf))
    if rows_first:
        pieces = [
            (cn * cf[:, i : i + 1] - sn * sf[:, i : i + 1], -(sn * cf[:, i : i + 1] + cn * sf[:, i : i + 1]))
            for i in range(half // fine)
        ]
        value = jnp.stack([jnp.concatenate([p[j] for p in pieces], 1) for j in range(2)])
    else:
        cn, sn, cf, sf = cn[None], sn[None], cf[:, None], sf[:, None]
        value = jnp.stack([cn * cf - sn * sf, -(sn * cf + cn * sf)]).reshape(2, half, 256)
    hi = lax.reduce_precision(value, 8, 7)
    return hi.astype(bf16), (value - hi).astype(bf16)


def shards(receiver_gathers, fourier_estimate, random_projector, release_sample):
    q = lax.axis_index("freq")
    est = fourier_estimate.reshape(4, 32, NODES, 4 * SHOTS)
    send = pack(est).reshape(GROUP, ROWS // 2, 2, 128)
    recv = lax.all_to_all(send, ("node", "freq"), split_axis=0, concat_axis=0, tiled=True)

    up = [(0, 1), (1, 2), (2, 3)]
    down = [(1, 0), (2, 1), (3, 2)]
    starts = jnp.broadcast_to(jnp.pad(release_sample[:HALO].astype(f32), (0, 124))[None], (NODES, 128))
    head = lax.ppermute(
        jnp.concatenate([receiver_gathers[:, : HALO * FRAME], starts], 1), "freq", down
    )
    release_before = lax.ppermute(release_sample[SHOTS - HALO :], "freq", up)
    release_after = head[0, HALO * FRAME : HALO * FRAME + HALO].astype(jnp.int32)
    dither = jnp.concatenate([release_before, release_sample, release_after]) % FRAME
    src = lax.iota(jnp.int32, 256)
    k = 2 * (src % 128) + src // 128 + 1
    angle = math.pi / SPAN * (k[None, :] * (2 * dither - FRAME + 1)[:, None] % (2 * SPAN)).astype(f32)
    cos_t, sin_t = jnp.cos(angle), jnp.sin(angle)
    tables = table(True) + table(False)
    last = (q == 3).astype(jnp.int32).reshape(1)
    misfit, back = signal(dither, last, recv.reshape(GROUP * ROWS, 128), cos_t, sin_t, tables, head, receiver_gathers)

    arrived = lax.all_to_all(
        back.reshape(GROUP, 24, 128), ("node", "freq"), split_axis=0, concat_axis=0, tiled=True
    )
    omega = jnp.pad(random_projector, ((0, 0), (0, 16)))
    zero = jnp.zeros_like(omega)
    w = jnp.concatenate([jnp.concatenate([omega, zero], 1), jnp.concatenate([zero, omega], 1)], 0)
    hi = lax.reduce_precision(w, 8, 7)
    w = jnp.concatenate([hi.astype(bf16), (w - hi).astype(bf16)], 1)
    low = rank_reduce(arrived.reshape(GROUP * 24, 128), fourier_estimate.reshape(4, 256, 384), w)
    return low.reshape(2, 2, 256, 384), misfit


def solution(mesh):
    return jax.shard_map(
        shards,
        mesh=mesh,
        in_specs=(P("node", "freq"), P(("node", "freq"), None, None, None), P(), P("freq")),
        out_specs=(P(("node", "freq"), None, None, None), P("node", "freq")),
        check_vma=False,
    )
```

```python
import functools
import math

import jax
import jax.numpy as jnp
from jax import lax
from jax.experimental import pallas as pl
from jax.experimental.pallas import tpu as pltpu
from jax.sharding import PartitionSpec as P


SPAN = 4096
FRAME = 1024
RANK = 48
HALO = 4
SHOTS = 96
NODES = 8
EXT = SHOTS + 2 * HALO
FRAMES = SHOTS + HALO
GROUP = 128
ROWS = 26
PACK_CHUNKS = 4
ORDER = (0, 2, 1, 3)
RELAX = 0.25
RIDGE = 0.001
highest = lax.Precision.HIGHEST
f32 = jnp.float32
bf16 = jnp.bfloat16


def keep(x):
    return pltpu.with_memory_space_constraint(x, pltpu.HBM)


def aligned(x, n):
    return x if isinstance(x, int) else pl.multiple_of(x, n)


def split(x):
    hi = x.astype(bf16)
    lo = (x - hi.astype(f32)).astype(bf16)
    return hi, lo


def pack_kernel(x_hbm, o_hbm, x_ref, o_ref, in_sem, out_sem):
    chunks = PACK_CHUNKS
    count = 32 // chunks
    size = count * 4 * ROWS
    lane = lax.broadcasted_iota(jnp.int32, (1, NODES, 128), 2)
    node = lax.broadcasted_iota(jnp.int32, (1, NODES, 128), 1)
    slot = lane // 32
    own = slot == node % 4
    shape = (count, NODES, 128)

    def load(i):
        part = pl.ds(i * count, count)
        return pltpu.make_async_copy(x_hbm.at[:, part], x_ref.at[:, part], in_sem.at[i])

    def store(i):
        part = pl.ds(aligned(i * size, 8), size)
        return pltpu.make_async_copy(o_ref.at[part], o_hbm.at[part], out_sem.at[i])

    def pick(mask, x, y):
        return jnp.where(jnp.broadcast_to(mask, shape), x, y)

    def turn(v, by):
        return pltpu.roll(v, by % 128, axis=2) if by % 128 else v

    for i in range(chunks):
        load(i).start()

    @pl.loop(0, chunks)
    def _(step):
        load(step).wait()
        blocks = pl.ds(step * count, count)
        x = [[x_ref[a, blocks, :, i * 128 : (i + 1) * 128] for i in range(3)] for a in range(4)]
        zero = jnp.zeros(shape, f32)
        edges = zero
        for k in range(3):
            for a in range(4):
                moved = turn(x[a][k], 32 * k + 8 * a - (92 - 32 * k))
                edges = pick(lane // 8 == 4 * k + a, moved, edges)
        turned = [turn(edges, 32 * r) for r in range(4)]

        def spread(k):
            v = turned[(0 - k) % 4]
            for m in range(1, 4):
                v = pick(slot == m, turned[(m - k) % 4], v)
            return pick(own, v, zero)

        spreads = [spread(k) for k in range(3)]

        def put(row, value, size):
            for p in range(count):
                o_ref[pl.ds(aligned(step * chunk_rows, 8) + p * 4 * ROWS + row, size), :] = value[p]

        chunk_rows = size
        for q in range(4):
            for a in range(3):
                if q == 0:
                    main = x[a][0]
                elif q == 3:
                    main = turn(x[a][2], 96)
                else:
                    main = pick(lane < 32 * q, turn(x[a][q - 1], 32 * q), turn(x[a][q], 32 * q))
                m = 3 * q + a
                rest = turn(x[3][m // 4], 32 * (3 - m % 4))
                put(q * ROWS + NODES * a, pick(lane < SHOTS, main, rest), NODES)
            before = spreads[q - 1] if q > 0 else zero
            after = spreads[q] if q < 3 else zero
            halo = pick(lane % 8 < 4, before, after)
            halo = halo + pltpu.roll(halo, 1, axis=1)
            halo = halo + pltpu.roll(halo, 2, axis=1)
            put(q * ROWS + 24, halo[:, 3:4], 1)
            put(q * ROWS + 25, halo[:, 7:8], 1)
        store(step).start()

    for i in range(chunks):
        store(i).wait()


def pack(x):
    hbm = pl.BlockSpec(memory_space=pltpu.HBM)
    return pl.pallas_call(
        pack_kernel,
        in_specs=[hbm],
        out_specs=hbm,
        out_shape=pltpu.HBM((GROUP * ROWS, 128), f32),
        scratch_shapes=[
            pltpu.VMEM((4, 32, NODES, 4 * SHOTS), f32),
            pltpu.VMEM((GROUP * ROWS, 128), f32),
            pltpu.SemaphoreType.DMA((PACK_CHUNKS,)),
            pltpu.SemaphoreType.DMA((PACK_CHUNKS,)),
        ],
        name="pack",
    )(keep(x))


def product(hi, lo, th, tl):
    return jnp.dot(
        jnp.concatenate([hi, lo, hi], 1), jnp.concatenate([th, th, tl], 0), preferred_element_type=f32
    )


def signal_kernel(
    d_ref, last_ref, recv_ref, cos_ref, sin_ref, fh_hbm, fl_hbm, ah_hbm, al_hbm, head_ref, gath_ref,
    mis_ref, send_hbm,
    c_ref, g_ref, q_ref, h_ref, lh_ref, ll_ref, mh_ref, ml_ref, sp_ref, w_ref, send_ref,
    fh_ref, fl_ref, ah_ref, al_ref, in_sem, head_sem, out_sem, send_sem, table_sem,
):
    rows_ext = EXT * NODES
    rows_frames = FRAMES * NODES
    rows_local = SHOTS * NODES
    local = SHOTS * FRAME
    loads = [
        pltpu.make_async_copy(src, dst, table_sem.at[i])
        for i, (src, dst) in enumerate(
            [(fh_hbm, fh_ref), (fl_hbm, fl_ref), (ah_hbm, ah_ref), (al_hbm, al_ref)]
        )
    ]
    loads[0].start()
    loads[1].start()
    fetch = pltpu.make_async_copy(gath_ref, g_ref.at[:, pl.ds(0, local)], in_sem)
    fetch.start()
    fetch_head = pltpu.make_async_copy(head_ref.at[:, pl.ds(0, HALO * FRAME)], g_ref.at[:, pl.ds(local, HALO * FRAME)], head_sem)
    fetch_head.start()
    loads[2].start()
    loads[3].start()

    for i in range(2):
        h_ref[i * 128 : (i + 1) * 128, :] = recv_ref[pl.ds(24 + i, GROUP, stride=ROWS), :].T

    for n in range(NODES):
        blocks = [recv_ref[pl.ds(a * NODES + n, GROUP, stride=ROWS), :].T for a in range(3)]
        planes = [b[:SHOTS] for b in blocks] + [jnp.concatenate([b[SHOTS:] for b in blocks], 0)]
        halo = aligned(n * 32, 32)
        pieces = [
            (HALO, SHOTS, planes),
            (0, HALO, [h_ref[pl.ds(halo + 8 * a, HALO), :] for a in range(4)]),
            (HALO + SHOTS, HALO, [h_ref[pl.ds(halo + 8 * a + HALO, HALO), :] for a in range(4)]),
        ]
        for first, size, values in pieces:
            for j in range(2):
                re, im = values[2 * j], values[2 * j + 1]
                co = cos_ref[first : first + size, j * 128 : (j + 1) * 128]
                si = sin_ref[first : first + size, j * 128 : (j + 1) * 128]
                place = 2 * j * rows_ext + first * NODES + n
                c_ref[pl.ds(place, size, stride=NODES), :] = 2.0 * (re * co + im * si)
                c_ref[pl.ds(place + rows_ext, size, stride=NODES), :] = 2.0 * (im * co - re * si)

    step = 80
    parity = 1.0 - 2.0 * (lax.broadcasted_iota(jnp.int32, (step, 128), 1) & 1).astype(f32)

    def build(i):
        base = aligned(i * step, NODES)

        def shot(m, a):
            return c_ref[pl.ds(aligned(a * rows_ext + base + (HALO - m) * NODES, NODES), step), :]

        parts = [
            (shot(0, 0) - shot(2, 0)) - parity * (shot(1, 1) - shot(3, 1)),
            (shot(0, 1) - shot(2, 1)) + parity * (shot(1, 0) - shot(3, 0)),
            (shot(0, 2) + shot(2, 2)) - parity * (shot(1, 2) + shot(3, 2)),
            (shot(0, 3) + shot(2, 3)) - parity * (shot(1, 3) + shot(3, 3)),
        ]
        for a in range(4):
            hi, lo = split(parts[a])
            lh_ref[pl.ds(base, step), ORDER[a] * 128 : (ORDER[a] + 1) * 128] = hi
            ll_ref[pl.ds(base, step), ORDER[a] * 128 : (ORDER[a] + 1) * 128] = lo

    for i in range(rows_ext // 64):
        base = aligned(i * 64, 64)
        target = aligned(rows_frames + base, 32)
        for a in range(4):
            hi, lo = split(c_ref[pl.ds(aligned(a * rows_ext + base, 64), 64), :])
            lh_ref[pl.ds(target, 64), ORDER[a] * 128 : (ORDER[a] + 1) * 128] = hi
            ll_ref[pl.ds(target, 64), ORDER[a] * 128 : (ORDER[a] + 1) * 128] = lo

    width = 256
    lane = lax.broadcasted_iota(jnp.int32, (NODES, width), 1)
    mirror = 127 - lax.broadcasted_iota(jnp.int32, (NODES, 128), 1)

    def reverse(x):
        tiles = [x[:, i : i + 128] for i in range(0, x.shape[1], 128)]
        return jnp.concatenate([jnp.take_along_axis(t, mirror, axis=1) for t in tiles[::-1]], 1)

    def pair(row, size, c):
        cols = pl.ds(aligned(c * width, width), width)
        rows = pl.ds(row, size)
        return (
            product(lh_ref[rows, :256], ll_ref[rows, :256], fh_ref[0, :, cols], fl_ref[0, :, cols]),
            product(lh_ref[rows, 256:], ll_ref[rows, 256:], fh_ref[1, :, cols], fl_ref[1, :, cols]),
        )

    def columns(c):
        return aligned(512 + c * width, width), aligned(256 - c * width, width)

    loads[0].wait()
    loads[1].wait()
    half_ext = rows_ext // 2

    for i in range(4):
        m, c = i // 2, i % 2
        even, odd = pair(aligned(rows_frames + m * half_ext, 16), half_ext, c)
        upper, lower = columns(c)
        for s in range(EXT // 2):
            rows = slice(s * NODES, (s + 1) * NODES)
            place = pl.ds(aligned(m * half_ext + s * NODES, NODES), NODES)
            d = d_ref[m * (EXT // 2) + s]
            q_ref[place, pl.ds(upper, width)] = jnp.where(lane < d - upper, even[rows] + odd[rows], 0.0)
            q_ref[place, pl.ds(lower, width)] = jnp.where(lane < d - lower, reverse(even[rows] - odd[rows]), 0.0)

    for i in range(rows_frames // step):
        build(i)

    fetch.wait()
    fetch_head.wait()
    half_frames = rows_frames // 2

    for i in range(4):
        m, c = i // 2, i % 2
        even, odd = pair(aligned(m * half_frames, 16), half_frames, c)
        upper, lower = columns(c)
        for f in range(FRAMES // 2):
            rows = slice(f * NODES, (f + 1) * NODES)
            first = m * half_frames + f * NODES
            now = pl.ds(aligned(first, NODES), NODES)
            ahead = pl.ds(aligned(first + HALO * NODES, NODES), NODES)
            start = (m * (FRAMES // 2) + f) * FRAME
            for col, out in ((upper, even[rows] + odd[rows]), (lower, reverse(even[rows] - odd[rows]))):
                cols = pl.ds(col, width)
                place = pl.ds(aligned(start + col, width), width)
                g_ref[:, place] = g_ref[:, place] - out + (q_ref[ahead, cols] - q_ref[now, cols])

    store = pltpu.make_async_copy(g_ref.at[:, pl.ds(0, local)], mis_ref, out_sem)
    store.start()

    wide = lax.broadcasted_iota(jnp.int32, (NODES, FRAME), 1)

    def put(row, first, second):
        folded = []
        for x in (first, second):
            back = reverse(x[:, :512])
            folded.append(jnp.concatenate([x[:, 512:] + back, x[:, 512:] - back], 1))
        hi, lo = split(jnp.concatenate(folded, 0))
        mh_ref[pl.ds(row, 16), :] = hi
        ml_ref[pl.ds(row, 16), :] = lo

    def frame_at(f):
        return g_ref[:, pl.ds(aligned(f * FRAME, FRAME), FRAME)]

    inside = last_ref[0] == 0

    def residual(f):
        x = frame_at(f)
        return x if f < SHOTS else jnp.where(inside, x, 0.0)

    total = rows_frames + rows_local
    half = total // 2

    def adjoint(i):
        rows = slice(i * half, (i + 1) * half)
        for part in range(2):
            cols = slice(part * 512, (part + 1) * 512)
            out = product(mh_ref[rows, cols], ml_ref[rows, cols], ah_ref[part], al_ref[part])
            for k in range(2):
                place = (2 * k + part) * total + i * half
                sp_ref[place : place + half, :] = out[:, k * 128 : (k + 1) * 128]

    def edge_of(f):
        return jnp.where(wide < d_ref[f + HALO], residual(f + HALO) - residual(f), 0.0)

    for f in range(0, FRAMES, 2):
        put(f * NODES, residual(f), residual(f + 1))
    loads[2].wait()
    loads[3].wait()
    adjoint(0)
    for f in range(0, SHOTS, 2):
        put(rows_frames + f * NODES, edge_of(f), edge_of(f + 1))
    adjoint(1)

    band = 48
    sign = 1.0 - 2.0 * (lax.broadcasted_iota(jnp.int32, (band, 128), 1) & 1).astype(f32)

    for i in range(rows_local // band):
        base = aligned(i * band, NODES)

        def frame(m, a):
            return sp_ref[pl.ds(aligned(a * total + base + m * NODES, NODES), band), :]

        def edge(a):
            return sp_ref[pl.ds(aligned(a * total + rows_frames + base, NODES), band), :]

        parts = [
            (frame(0, 0) - frame(2, 0)) + sign * (frame(1, 1) - frame(3, 1)) + edge(0),
            (frame(0, 1) - frame(2, 1)) - sign * (frame(1, 0) - frame(3, 0)) + edge(1),
            (frame(0, 2) + frame(2, 2)) - sign * (frame(1, 2) + frame(3, 2)) + edge(2),
            (frame(0, 3) + frame(2, 3)) - sign * (frame(1, 3) + frame(3, 3)) + edge(3),
        ]
        for a in range(4):
            w_ref[pl.ds(aligned(a * rows_local + base, NODES), band), :] = parts[a]

    def spectrum(n, a, first, size):
        j = a // 2
        re, im = w_ref[pl.ds(2 * j * rows_local + n + first * NODES, size, stride=NODES), :], w_ref[
            pl.ds((2 * j + 1) * rows_local + n + first * NODES, size, stride=NODES), :
        ]
        shots = slice(HALO + first, HALO + first + size)
        co = RELAX * cos_ref[shots, j * 128 : (j + 1) * 128]
        si = RELAX * sin_ref[shots, j * 128 : (j + 1) * 128]
        return re * co - im * si if a % 2 == 0 else im * co + re * si

    sends = []
    for a in range(3):
        for n in range(NODES):
            block = jnp.concatenate([spectrum(n, a, 0, SHOTS), spectrum(n, 3, 32 * a, 32)], 0).T
            send_ref[pl.ds(a * NODES + n, GROUP, stride=24), :] = block
        part = pl.ds(a * NODES, NODES)
        sends.append(
            pltpu.make_async_copy(
                send_ref.reshape(GROUP, 24, 128).at[:, part], send_hbm.reshape(GROUP, 24, 128).at[:, part], send_sem.at[a]
            )
        )
        sends[-1].start()
    store.wait()
    for send in sends:
        send.wait()


def signal(dither, last, recv, cos_t, sin_t, tables, head, gathers):
    vmem = pl.BlockSpec(memory_space=pltpu.VMEM)
    smem = pl.BlockSpec(memory_space=pltpu.SMEM)
    hbm = pl.BlockSpec(memory_space=pltpu.HBM)
    rows_ext, rows_frames, rows_local = EXT * NODES, FRAMES * NODES, SHOTS * NODES
    return pl.pallas_call(
        signal_kernel,
        in_specs=[smem, smem, vmem, vmem, vmem, hbm, hbm, hbm, hbm, hbm, hbm],
        out_specs=[hbm, hbm],
        out_shape=[
            pltpu.HBM((NODES, SHOTS * FRAME), f32),
            pltpu.HBM((GROUP * 24, 128), f32),
        ],
        scratch_shapes=[
            pltpu.VMEM((4 * rows_ext, 128), f32),
            pltpu.VMEM((NODES, FRAMES * FRAME), f32),
            pltpu.VMEM((rows_ext, FRAME), f32),
            pltpu.VMEM((256, 128), f32),
            pltpu.VMEM((rows_frames + rows_ext, 512), bf16),
            pltpu.VMEM((rows_frames + rows_ext, 512), bf16),
            pltpu.VMEM((rows_frames + rows_local, FRAME), bf16),
            pltpu.VMEM((rows_frames + rows_local, FRAME), bf16),
            pltpu.VMEM((4 * (rows_frames + rows_local), 128), f32),
            pltpu.VMEM((4 * rows_local, 128), f32),
            pltpu.VMEM((GROUP * 24, 128), f32),
            pltpu.VMEM((2, 256, 512), bf16),
            pltpu.VMEM((2, 256, 512), bf16),
            pltpu.VMEM((2, 512, 256), bf16),
            pltpu.VMEM((2, 512, 256), bf16),
            pltpu.SemaphoreType.DMA,
            pltpu.SemaphoreType.DMA,
            pltpu.SemaphoreType.DMA,
            pltpu.SemaphoreType.DMA((3,)),
            pltpu.SemaphoreType.DMA((4,)),
        ],
        compiler_params=pltpu.CompilerParams(vmem_limit_bytes=40 << 20),
        name="signal",
    )(dither, last, recv, cos_t, sin_t, *[keep(t) for t in tables], keep(head), keep(gathers))


def rank_kernel(recv_ref, est_ref, w_hbm, out_hbm, ah_ref, al_ref, out_ref, w_ref, out_sem, w_sem):
    load_w = pltpu.make_async_copy(w_hbm, w_ref, w_sem)
    load_w.start()
    lane = lax.broadcasted_iota(jnp.int32, (NODES, 128), 1)
    chunk = lane // 32

    def planes(p):
        rows = pl.ds(aligned(p * NODES, NODES), NODES)
        values, extras = [], []
        for a in range(3):
            t = []
            for q in range(4):
                tile = recv_ref[pl.ds(aligned((p * 4 + q) * 24 + a * NODES, NODES), NODES), :]
                t.append(pltpu.roll(tile, (96 * q) % 128, axis=1) if q else tile)
            values.append([
                jnp.where(lane < 96, t[0], t[1]),
                jnp.where(lane < 64, t[1], t[2]),
                jnp.where(lane < 32, t[2], t[3]),
            ])
            e = jnp.where(chunk == 0, t[3], jnp.where(chunk == 1, t[2], jnp.where(chunk == 2, t[1], t[0])))
            extras.append(pltpu.roll(e, 32 * (a + 1), axis=1) if a < 3 else e)
        values.append([])
        for i in range(3):
            x = extras[(4 * i) % 3]
            for k in range(1, 4):
                x = jnp.where(chunk == k, extras[(4 * i + k) % 3], x)
            values[3].append(x)
        return [
            [est_ref[a, rows, i * 128 : (i + 1) * 128] + values[a][i] for i in range(3)] for a in range(4)
        ]

    def unpack(p):
        upper, lower = planes(2 * p), planes(2 * p + 1)
        rows = pl.ds(aligned(p * 16, 16), 16)
        for a in range(4):
            for i in range(3):
                hi, lo = split(jnp.concatenate([upper[a][i], lower[a][i]], 0))
                cols = slice((a % 2) * 384 + i * 128, (a % 2) * 384 + (i + 1) * 128)
                ah_ref[a // 2, rows, cols] = hi
                al_ref[a // 2, rows, cols] = lo

    @pl.loop(0, 4)
    def _(p):
        for i in range(4):
            unpack(4 * p + i)

    load_w.wait()

    dot = functools.partial(jnp.dot, preferred_element_type=f32)
    lane_r = lax.broadcasted_iota(jnp.int32, (64, 128), 1)
    row_r = lax.broadcasted_iota(jnp.int32, (64, 128), 0)
    flip = jnp.where(lane_r < 64, 1.0, -1.0).astype(f32)
    diagonal = (lane_r == row_r) & (row_r < RANK)
    systems = []
    rights = []
    basis = []
    for j in range(2):
        yy = dot(ah_ref[j], w_ref[...])
        y = yy[:, :128] + yy[:, 128:] + dot(al_ref[j], w_ref[:, :128])
        basis.append(y)
        yt = y.T
        g = jnp.dot(yt, y, precision=highest, preferred_element_type=f32)
        g = g[:64] + flip * pltpu.roll(g[64:], 64, axis=1)
        trace = jnp.sum(jnp.where(diagonal, g, 0.0))
        g = jnp.where(diagonal, g + RIDGE * trace / RANK, g)
        eye = jnp.where(diagonal, 1.0, 0.0).astype(f32)
        systems.append([g[:RANK], eye[:RANK]])
        yh, ym = split(yt)
        yl = (yt - yh.astype(f32) - ym.astype(f32)).astype(bf16)
        c = dot(jnp.concatenate([yh, ym, yl], 0), ah_ref[j])
        rest = dot(jnp.concatenate([yh, ym], 0), al_ref[j])
        c = c[:128] + ((c[128:256] + rest[:128]) + (c[256:] + rest[128:]))
        rights.append(jnp.concatenate([c[:64, :384] + c[64:, 384:], c[:64, 384:] - c[64:, :384]], 0))

    neg = jnp.where(lax.broadcasted_iota(jnp.int32, (NODES, 128), 1) < 64, -1.0, 1.0).astype(f32)
    row_i = lax.broadcasted_iota(jnp.int32, (NODES, 128), 0)
    groups = RANK // NODES
    state = [
        ([g[i * NODES : (i + 1) * NODES] for i in range(groups)], [w[i * NODES : (i + 1) * NODES] for i in range(groups)])
        for g, w in systems
    ]

    def row(x, k):
        return jnp.broadcast_to(x[k % NODES : k % NODES + 1], (NODES, 128))

    def column(x, k):
        return jnp.broadcast_to(x[:, k : k + 1], (NODES, 128))

    def gathered(x, k):
        return jnp.take_along_axis(x, jnp.full((NODES, 128), k, jnp.int32), axis=1)

    def turned(x):
        return neg * pltpu.roll(x, 64, axis=1)

    for k in range(0, RANK, 2):
        top = k // NODES
        for gs, ws in state:
            gt, wt = turned(gs[top]), turned(ws[top])
            cols = [
                [(gathered if i == top else column)(gs[i], c) for c in (k, 64 + k, k + 1, 65 + k)]
                for i in range(top, groups)
            ]
            a = row(cols[0][0], k)
            br, bi = row(cols[0][2], k), row(cols[0][3], k)
            d = row(cols[0][2], k + 1)
            ia = 1.0 / a
            lr, li = br * ia, -bi * ia
            second = 1.0 / (d - (br * br + bi * bi) * ia)
            g0, g0i, w0, w0i = row(gs[top], k), row(gt, k), row(ws[top], k), row(wt, k)
            g1 = row(gs[top], k + 1) - (lr * g0 + li * g0i)
            g1i = row(gt, k + 1) - (lr * g0i - li * g0)
            w1 = row(ws[top], k + 1) - (lr * w0 + li * w0i)
            w1i = row(wt, k + 1) - (lr * w0i - li * w0)
            for i in range(top, groups):
                c0r, c0i, c1r, c1i = cols[i - top]
                f0r, f0i = c0r * ia, c0i * ia
                f1r = (c1r - (f0r * br - f0i * bi)) * second
                f1i = (c1i - (f0r * bi + f0i * br)) * second
                if i == top:
                    f0r, f0i = jnp.where(row_i > k % NODES, f0r, 0.0), jnp.where(row_i > k % NODES, f0i, 0.0)
                    f1r, f1i = jnp.where(row_i > k % NODES + 1, f1r, 0.0), jnp.where(row_i > k % NODES + 1, f1i, 0.0)
                gs[i] = gs[i] - ((f0r * g0 + f0i * g0i) + (f1r * g1 + f1i * g1i))
                ws[i] = ws[i] - ((f0r * w0 + f0i * w0i) + (f1r * w1 + f1i * w1i))
    systems = [[jnp.concatenate(gs, 0), jnp.concatenate(ws, 0)] for gs, ws in state]

    stores = []
    for j in range(2):
        g, w = systems[j]
        d = jnp.sum(jnp.where(diagonal[:RANK], g, 0.0), axis=1, keepdims=True)
        w = w * lax.rsqrt(d)
        w = jnp.concatenate([w, jnp.zeros((16, 128), f32)], 0)
        left = jnp.concatenate([flip * w, pltpu.roll(w, 64, axis=1)], 0)
        v = jnp.dot(left, rights[j], precision=highest, preferred_element_type=f32)
        conj = jnp.concatenate([w, -flip * pltpu.roll(w, 64, axis=1)], 0)
        z = jnp.dot(basis[j], conj.T, precision=highest, preferred_element_type=f32)
        v = jnp.concatenate(
            [jnp.concatenate([v[:64], v[64:]], 1), jnp.concatenate([-v[64:], v[:64]], 1)], 0
        )
        vh, vl = split(v)
        zh, zl = split(z)
        low = dot(jnp.concatenate([zh, zl], 1), jnp.concatenate([vh, vh], 0)) + dot(zh, vl)
        for c in range(2):
            i = 2 * j + c
            out_ref[i] = low[:, 384 * c : 384 * (c + 1)]
            stores.append(pltpu.make_async_copy(out_ref.at[i], out_hbm.at[i], out_sem.at[i]))
            stores[-1].start()
    for store in stores:
        store.wait()


def rank_reduce(recv, est, w):
    vmem = pl.BlockSpec(memory_space=pltpu.VMEM)
    hbm = pl.BlockSpec(memory_space=pltpu.HBM)
    return pl.pallas_call(
        rank_kernel,
        in_specs=[vmem, vmem, hbm],
        out_specs=hbm,
        out_shape=pltpu.HBM((4, 256, 384), f32),
        scratch_shapes=[
            pltpu.VMEM((2, 256, 768), bf16),
            pltpu.VMEM((2, 256, 768), bf16),
            pltpu.VMEM((4, 256, 384), f32),
            pltpu.VMEM((768, 256), bf16),
            pltpu.SemaphoreType.DMA((4,)),
            pltpu.SemaphoreType.DMA,
        ],
        compiler_params=pltpu.CompilerParams(vmem_limit_bytes=20 << 20),
        name="rank",
    )(recv, est, keep(w))


def table(rows_first):
    half = FRAME // 2
    fine = 128 if rows_first else 64
    row = lax.iota(jnp.int32, 256)
    k = 2 * (row % 128) + row // 128 + 1
    near = 2 * lax.iota(jnp.int32, fine) + 1
    far = 2 * fine * lax.iota(jnp.int32, half // fine)
    if rows_first:
        phases = k[:, None] * near[None, :], k[:, None] * far[None, :]
    else:
        phases = near[:, None] * k[None, :], far[:, None] * k[None, :]
    angles = [math.pi / SPAN * (p % (2 * SPAN)).astype(f32) for p in phases]
    scale = 1.0 / math.sqrt(SPAN)
    cn, sn = jnp.cos(angles[0]) * scale, jnp.sin(angles[0]) * scale
    cf, sf = jnp.cos(angles[1]), jnp.sin(angles[1])
    cn, sn, cf, sf = lax.optimization_barrier((cn, sn, cf, sf))
    if rows_first:
        pieces = [
            (cn * cf[:, i : i + 1] - sn * sf[:, i : i + 1], -(sn * cf[:, i : i + 1] + cn * sf[:, i : i + 1]))
            for i in range(half // fine)
        ]
        value = jnp.stack([jnp.concatenate([p[j] for p in pieces], 1) for j in range(2)])
    else:
        cn, sn, cf, sf = cn[None], sn[None], cf[:, None], sf[:, None]
        value = jnp.stack([cn * cf - sn * sf, -(sn * cf + cn * sf)]).reshape(2, half, 256)
    hi = lax.reduce_precision(value, 8, 7)
    return hi.astype(bf16), (value - hi).astype(bf16)


def shards(receiver_gathers, fourier_estimate, random_projector, release_sample):
    q = lax.axis_index("freq")
    est = fourier_estimate.reshape(4, 32, NODES, 4 * SHOTS)
    send = pack(est).reshape(GROUP, ROWS // 2, 2, 128)
    recv = lax.all_to_all(send, ("node", "freq"), split_axis=0, concat_axis=0, tiled=True)

    up = [(0, 1), (1, 2), (2, 3)]
    down = [(1, 0), (2, 1), (3, 2)]
    starts = jnp.broadcast_to(jnp.pad(release_sample[:HALO].astype(f32), (0, 124))[None], (NODES, 128))
    head = lax.ppermute(
        jnp.concatenate([receiver_gathers[:, : HALO * FRAME], starts], 1), "freq", down
    )
    release_before = lax.ppermute(release_sample[SHOTS - HALO :], "freq", up)
    release_after = head[0, HALO * FRAME : HALO * FRAME + HALO].astype(jnp.int32)
    dither = jnp.concatenate([release_before, release_sample, release_after]) % FRAME
    src = lax.iota(jnp.int32, 256)
    k = 2 * (src % 128) + src // 128 + 1
    angle = math.pi / SPAN * (k[None, :] * (2 * dither - FRAME + 1)[:, None] % (2 * SPAN)).astype(f32)
    cos_t, sin_t = jnp.cos(angle), jnp.sin(angle)
    tables = table(True) + table(False)
    last = (q == 3).astype(jnp.int32).reshape(1)
    misfit, back = signal(dither, last, recv.reshape(GROUP * ROWS, 128), cos_t, sin_t, tables, head, receiver_gathers)

    arrived = lax.all_to_all(
        back.reshape(GROUP, 24, 128), ("node", "freq"), split_axis=0, concat_axis=0, tiled=True
    )
    omega = jnp.pad(random_projector, ((0, 0), (0, 16)))
    zero = jnp.zeros_like(omega)
    w = jnp.concatenate([jnp.concatenate([omega, zero], 1), jnp.concatenate([zero, omega], 1)], 0)
    hi = lax.reduce_precision(w, 8, 7)
    w = jnp.concatenate([hi.astype(bf16), (w - hi).astype(bf16)], 1)
    low = rank_reduce(arrived.reshape(GROUP * 24, 128), fourier_estimate.reshape(4, 256, 384), w)
    return low.reshape(2, 2, 256, 384), misfit


def solution(mesh):
    return jax.shard_map(
        shards,
        mesh=mesh,
        in_specs=(P("node", "freq"), P(("node", "freq"), None, None, None), P(), P("freq")),
        out_specs=(P(("node", "freq"), None, None, None), P("node", "freq")),
        check_vma=False,
    )
```

```python
import functools
import math

import jax
import jax.numpy as jnp
from jax import lax
from jax.experimental import pallas as pl
from jax.experimental.pallas import tpu as pltpu
from jax.sharding import PartitionSpec as P


SPAN = 4096
FRAME = 1024
RANK = 48
HALO = 4
SHOTS = 96
NODES = 8
EXT = SHOTS + 2 * HALO
FRAMES = SHOTS + HALO
GROUP = 128
ROWS = 26
PACK_CHUNKS = 4
ORDER = (0, 2, 1, 3)
RELAX = 0.25
RIDGE = 0.001
highest = lax.Precision.HIGHEST
f32 = jnp.float32
bf16 = jnp.bfloat16


def keep(x):
    return pltpu.with_memory_space_constraint(x, pltpu.HBM)


def aligned(x, n):
    return x if isinstance(x, int) else pl.multiple_of(x, n)


def split(x):
    hi = x.astype(bf16)
    lo = (x - hi.astype(f32)).astype(bf16)
    return hi, lo


def pack_kernel(x_hbm, o_hbm, x_ref, o_ref, in_sem, out_sem):
    chunks = PACK_CHUNKS
    count = 32 // chunks
    size = count * 4 * ROWS
    lane = lax.broadcasted_iota(jnp.int32, (1, NODES, 128), 2)
    node = lax.broadcasted_iota(jnp.int32, (1, NODES, 128), 1)
    slot = lane // 32
    own = slot == node % 4
    shape = (count, NODES, 128)

    def load(i):
        part = pl.ds(i * count, count)
        return pltpu.make_async_copy(x_hbm.at[:, part], x_ref.at[:, part], in_sem.at[i])

    def store(i):
        part = pl.ds(aligned(i * size, 8), size)
        return pltpu.make_async_copy(o_ref.at[part], o_hbm.at[part], out_sem.at[i])

    def pick(mask, x, y):
        return jnp.where(jnp.broadcast_to(mask, shape), x, y)

    def turn(v, by):
        return pltpu.roll(v, by % 128, axis=2) if by % 128 else v

    for i in range(chunks):
        load(i).start()

    @pl.loop(0, chunks)
    def _(step):
        load(step).wait()
        blocks = pl.ds(step * count, count)
        x = [[x_ref[a, blocks, :, i * 128 : (i + 1) * 128] for i in range(3)] for a in range(4)]
        zero = jnp.zeros(shape, f32)
        edges = zero
        for k in range(3):
            for a in range(4):
                moved = turn(x[a][k], 32 * k + 8 * a - (92 - 32 * k))
                edges = pick(lane // 8 == 4 * k + a, moved, edges)
        turned = [turn(edges, 32 * r) for r in range(4)]

        def spread(k):
            v = turned[(0 - k) % 4]
            for m in range(1, 4):
                v = pick(slot == m, turned[(m - k) % 4], v)
            return pick(own, v, zero)

        spreads = [spread(k) for k in range(3)]

        def put(row, value, size):
            for p in range(count):
                o_ref[pl.ds(aligned(step * chunk_rows, 8) + p * 4 * ROWS + row, size), :] = value[p]

        chunk_rows = size
        for q in range(4):
            for a in range(3):
                if q == 0:
                    main = x[a][0]
                elif q == 3:
                    main = turn(x[a][2], 96)
                else:
                    main = pick(lane < 32 * q, turn(x[a][q - 1], 32 * q), turn(x[a][q], 32 * q))
                m = 3 * q + a
                rest = turn(x[3][m // 4], 32 * (3 - m % 4))
                put(q * ROWS + NODES * a, pick(lane < SHOTS, main, rest), NODES)
            before = spreads[q - 1] if q > 0 else zero
            after = spreads[q] if q < 3 else zero
            halo = pick(lane % 8 < 4, before, after)
            halo = halo + pltpu.roll(halo, 1, axis=1)
            halo = halo + pltpu.roll(halo, 2, axis=1)
            put(q * ROWS + 24, halo[:, 3:4], 1)
            put(q * ROWS + 25, halo[:, 7:8], 1)
        store(step).start()

    for i in range(chunks):
        store(i).wait()


def pack(x):
    hbm = pl.BlockSpec(memory_space=pltpu.HBM)
    return pl.pallas_call(
        pack_kernel,
        in_specs=[hbm],
        out_specs=hbm,
        out_shape=pltpu.HBM((GROUP * ROWS, 128), f32),
        scratch_shapes=[
            pltpu.VMEM((4, 32, NODES, 4 * SHOTS), f32),
            pltpu.VMEM((GROUP * ROWS, 128), f32),
            pltpu.SemaphoreType.DMA((PACK_CHUNKS,)),
            pltpu.SemaphoreType.DMA((PACK_CHUNKS,)),
        ],
        name="pack",
    )(keep(x))


def product(hi, lo, th, tl):
    return jnp.dot(
        jnp.concatenate([hi, lo, hi], 1), jnp.concatenate([th, th, tl], 0), preferred_element_type=f32
    )


def signal_kernel(
    d_ref, last_ref, recv_ref, cos_ref, sin_ref, fh_hbm, fl_hbm, ah_hbm, al_hbm, head_ref, gath_ref,
    mis_ref, send_hbm,
    c_ref, g_ref, q_ref, h_ref, lh_ref, ll_ref, mh_ref, ml_ref, sp_ref, w_ref, send_ref,
    fh_ref, fl_ref, ah_ref, al_ref, in_sem, head_sem, out_sem, send_sem, table_sem,
):
    rows_ext = EXT * NODES
    rows_frames = FRAMES * NODES
    rows_local = SHOTS * NODES
    local = SHOTS * FRAME
    loads = [
        pltpu.make_async_copy(src, dst, table_sem.at[i])
        for i, (src, dst) in enumerate(
            [(fh_hbm, fh_ref), (fl_hbm, fl_ref), (ah_hbm, ah_ref), (al_hbm, al_ref)]
        )
    ]
    loads[0].start()
    loads[1].start()
    middle = FRAMES // 2 * FRAME
    fetches = [
        pltpu.make_async_copy(gath_ref.at[:, pl.ds(x, n)], g_ref.at[:, pl.ds(x, n)], in_sem.at[i])
        for i, (x, n) in enumerate([(0, middle), (middle, local - middle)])
    ]
    for fetch in fetches:
        fetch.start()
    fetch_head = pltpu.make_async_copy(head_ref.at[:, pl.ds(0, HALO * FRAME)], g_ref.at[:, pl.ds(local, HALO * FRAME)], head_sem)
    fetch_head.start()
    loads[2].start()
    loads[3].start()

    for i in range(2):
        h_ref[i * 128 : (i + 1) * 128, :] = recv_ref[pl.ds(24 + i, GROUP, stride=ROWS), :].T

    for n in range(NODES):
        blocks = [recv_ref[pl.ds(a * NODES + n, GROUP, stride=ROWS), :].T for a in range(3)]
        planes = [b[:SHOTS] for b in blocks] + [jnp.concatenate([b[SHOTS:] for b in blocks], 0)]
        halo = aligned(n * 32, 32)
        pieces = [
            (HALO, SHOTS, planes),
            (0, HALO, [h_ref[pl.ds(halo + 8 * a, HALO), :] for a in range(4)]),
            (HALO + SHOTS, HALO, [h_ref[pl.ds(halo + 8 * a + HALO, HALO), :] for a in range(4)]),
        ]
        for first, size, values in pieces:
            for j in range(2):
                re, im = values[2 * j], values[2 * j + 1]
                co = cos_ref[first : first + size, j * 128 : (j + 1) * 128]
                si = sin_ref[first : first + size, j * 128 : (j + 1) * 128]
                place = 2 * j * rows_ext + first * NODES + n
                c_ref[pl.ds(place, size, stride=NODES), :] = 2.0 * (re * co + im * si)
                c_ref[pl.ds(place + rows_ext, size, stride=NODES), :] = 2.0 * (im * co - re * si)

    step = 80
    parity = 1.0 - 2.0 * (lax.broadcasted_iota(jnp.int32, (step, 128), 1) & 1).astype(f32)

    def build(i):
        base = aligned(i * step, NODES)

        def shot(m, a):
            return c_ref[pl.ds(aligned(a * rows_ext + base + (HALO - m) * NODES, NODES), step), :]

        parts = [
            (shot(0, 0) - shot(2, 0)) - parity * (shot(1, 1) - shot(3, 1)),
            (shot(0, 1) - shot(2, 1)) + parity * (shot(1, 0) - shot(3, 0)),
            (shot(0, 2) + shot(2, 2)) - parity * (shot(1, 2) + shot(3, 2)),
            (shot(0, 3) + shot(2, 3)) - parity * (shot(1, 3) + shot(3, 3)),
        ]
        for a in range(4):
            hi, lo = split(parts[a])
            lh_ref[pl.ds(base, step), ORDER[a] * 128 : (ORDER[a] + 1) * 128] = hi
            ll_ref[pl.ds(base, step), ORDER[a] * 128 : (ORDER[a] + 1) * 128] = lo

    for i in range(rows_ext // 64):
        base = aligned(i * 64, 64)
        target = aligned(rows_frames + base, 32)
        for a in range(4):
            hi, lo = split(c_ref[pl.ds(aligned(a * rows_ext + base, 64), 64), :])
            lh_ref[pl.ds(target, 64), ORDER[a] * 128 : (ORDER[a] + 1) * 128] = hi
            ll_ref[pl.ds(target, 64), ORDER[a] * 128 : (ORDER[a] + 1) * 128] = lo

    width = 256
    lane = lax.broadcasted_iota(jnp.int32, (NODES, width), 1)
    mirror = 127 - lax.broadcasted_iota(jnp.int32, (NODES, 128), 1)

    def reverse(x):
        tiles = [x[:, i : i + 128] for i in range(0, x.shape[1], 128)]
        return jnp.concatenate([jnp.take_along_axis(t, mirror, axis=1) for t in tiles[::-1]], 1)

    def pair(row, size, c):
        cols = pl.ds(aligned(c * width, width), width)
        rows = pl.ds(row, size)
        return (
            product(lh_ref[rows, :256], ll_ref[rows, :256], fh_ref[0, :, cols], fl_ref[0, :, cols]),
            product(lh_ref[rows, 256:], ll_ref[rows, 256:], fh_ref[1, :, cols], fl_ref[1, :, cols]),
        )

    def columns(c):
        return aligned(512 + c * width, width), aligned(256 - c * width, width)

    loads[0].wait()
    loads[1].wait()
    half_ext = rows_ext // 2

    for i in range(4):
        m, c = i // 2, i % 2
        even, odd = pair(aligned(rows_frames + m * half_ext, 16), half_ext, c)
        upper, lower = columns(c)
        for s in range(EXT // 2):
            rows = slice(s * NODES, (s + 1) * NODES)
            place = pl.ds(aligned(m * half_ext + s * NODES, NODES), NODES)
            d = d_ref[m * (EXT // 2) + s]
            q_ref[place, pl.ds(upper, width)] = jnp.where(lane < d - upper, even[rows] + odd[rows], 0.0)
            q_ref[place, pl.ds(lower, width)] = jnp.where(lane < d - lower, reverse(even[rows] - odd[rows]), 0.0)

    for i in range(rows_frames // step):
        build(i)

    half_frames = rows_frames // 2

    for i in range(4):
        m, c = i // 2, i % 2
        if c == 0:
            fetches[m].wait()
        if i == 2:
            fetch_head.wait()
        even, odd = pair(aligned(m * half_frames, 16), half_frames, c)
        upper, lower = columns(c)
        for f in range(FRAMES // 2):
            rows = slice(f * NODES, (f + 1) * NODES)
            first = m * half_frames + f * NODES
            now = pl.ds(aligned(first, NODES), NODES)
            ahead = pl.ds(aligned(first + HALO * NODES, NODES), NODES)
            start = (m * (FRAMES // 2) + f) * FRAME
            for col, out in ((upper, even[rows] + odd[rows]), (lower, reverse(even[rows] - odd[rows]))):
                cols = pl.ds(col, width)
                place = pl.ds(aligned(start + col, width), width)
                g_ref[:, place] = g_ref[:, place] - out + (q_ref[ahead, cols] - q_ref[now, cols])

    store = pltpu.make_async_copy(g_ref.at[:, pl.ds(0, local)], mis_ref, out_sem)
    store.start()

    wide = lax.broadcasted_iota(jnp.int32, (NODES, FRAME), 1)

    def put(row, first, second):
        folded = []
        for x in (first, second):
            back = reverse(x[:, :512])
            folded.append(jnp.concatenate([x[:, 512:] + back, x[:, 512:] - back], 1))
        hi, lo = split(jnp.concatenate(folded, 0))
        mh_ref[pl.ds(row, 16), :] = hi
        ml_ref[pl.ds(row, 16), :] = lo

    def frame_at(f):
        return g_ref[:, pl.ds(aligned(f * FRAME, FRAME), FRAME)]

    inside = last_ref[0] == 0

    def residual(f):
        x = frame_at(f)
        return x if f < SHOTS else jnp.where(inside, x, 0.0)

    total = rows_frames + rows_local
    half = total // 2

    def adjoint(i):
        rows = slice(i * half, (i + 1) * half)
        for part in range(2):
            cols = slice(part * 512, (part + 1) * 512)
            out = product(mh_ref[rows, cols], ml_ref[rows, cols], ah_ref[part], al_ref[part])
            for k in range(2):
                place = (2 * k + part) * total + i * half
                sp_ref[place : place + half, :] = out[:, k * 128 : (k + 1) * 128]

    def edge_of(f):
        return jnp.where(wide < d_ref[f + HALO], residual(f + HALO) - residual(f), 0.0)

    for f in range(0, FRAMES, 2):
        put(f * NODES, residual(f), residual(f + 1))
    loads[2].wait()
    loads[3].wait()
    adjoint(0)
    for f in range(0, SHOTS, 2):
        put(rows_frames + f * NODES, edge_of(f), edge_of(f + 1))
    adjoint(1)

    band = 48
    sign = 1.0 - 2.0 * (lax.broadcasted_iota(jnp.int32, (band, 128), 1) & 1).astype(f32)

    for i in range(rows_local // band):
        base = aligned(i * band, NODES)

        def frame(m, a):
            return sp_ref[pl.ds(aligned(a * total + base + m * NODES, NODES), band), :]

        def edge(a):
            return sp_ref[pl.ds(aligned(a * total + rows_frames + base, NODES), band), :]

        parts = [
            (frame(0, 0) - frame(2, 0)) + sign * (frame(1, 1) - frame(3, 1)) + edge(0),
            (frame(0, 1) - frame(2, 1)) - sign * (frame(1, 0) - frame(3, 0)) + edge(1),
            (frame(0, 2) + frame(2, 2)) - sign * (frame(1, 2) + frame(3, 2)) + edge(2),
            (frame(0, 3) + frame(2, 3)) - sign * (frame(1, 3) + frame(3, 3)) + edge(3),
        ]
        for a in range(4):
            w_ref[pl.ds(aligned(a * rows_local + base, NODES), band), :] = parts[a]

    def spectrum(n, a, first, size):
        j = a // 2
        re, im = w_ref[pl.ds(2 * j * rows_local + n + first * NODES, size, stride=NODES), :], w_ref[
            pl.ds((2 * j + 1) * rows_local + n + first * NODES, size, stride=NODES), :
        ]
        shots = slice(HALO + first, HALO + first + size)
        co = RELAX * cos_ref[shots, j * 128 : (j + 1) * 128]
        si = RELAX * sin_ref[shots, j * 128 : (j + 1) * 128]
        return re * co - im * si if a % 2 == 0 else im * co + re * si

    sends = []
    for a in range(3):
        for n in range(NODES):
            block = jnp.concatenate([spectrum(n, a, 0, SHOTS), spectrum(n, 3, 32 * a, 32)], 0).T
            send_ref[pl.ds(a * NODES + n, GROUP, stride=24), :] = block
        part = pl.ds(a * NODES, NODES)
        sends.append(
            pltpu.make_async_copy(
                send_ref.reshape(GROUP, 24, 128).at[:, part], send_hbm.reshape(GROUP, 24, 128).at[:, part], send_sem.at[a]
            )
        )
        sends[-1].start()
    store.wait()
    for send in sends:
        send.wait()


def signal(dither, last, recv, cos_t, sin_t, tables, head, gathers):
    vmem = pl.BlockSpec(memory_space=pltpu.VMEM)
    smem = pl.BlockSpec(memory_space=pltpu.SMEM)
    hbm = pl.BlockSpec(memory_space=pltpu.HBM)
    rows_ext, rows_frames, rows_local = EXT * NODES, FRAMES * NODES, SHOTS * NODES
    return pl.pallas_call(
        signal_kernel,
        in_specs=[smem, smem, vmem, vmem, vmem, hbm, hbm, hbm, hbm, hbm, hbm],
        out_specs=[hbm, hbm],
        out_shape=[
            pltpu.HBM((NODES, SHOTS * FRAME), f32),
            pltpu.HBM((GROUP * 24, 128), f32),
        ],
        scratch_shapes=[
            pltpu.VMEM((4 * rows_ext, 128), f32),
            pltpu.VMEM((NODES, FRAMES * FRAME), f32),
            pltpu.VMEM((rows_ext, FRAME), f32),
            pltpu.VMEM((256, 128), f32),
            pltpu.VMEM((rows_frames + rows_ext, 512), bf16),
            pltpu.VMEM((rows_frames + rows_ext, 512), bf16),
            pltpu.VMEM((rows_frames + rows_local, FRAME), bf16),
            pltpu.VMEM((rows_frames + rows_local, FRAME), bf16),
            pltpu.VMEM((4 * (rows_frames + rows_local), 128), f32),
            pltpu.VMEM((4 * rows_local, 128), f32),
            pltpu.VMEM((GROUP * 24, 128), f32),
            pltpu.VMEM((2, 256, 512), bf16),
            pltpu.VMEM((2, 256, 512), bf16),
            pltpu.VMEM((2, 512, 256), bf16),
            pltpu.VMEM((2, 512, 256), bf16),
            pltpu.SemaphoreType.DMA((2,)),
            pltpu.SemaphoreType.DMA,
            pltpu.SemaphoreType.DMA,
            pltpu.SemaphoreType.DMA((3,)),
            pltpu.SemaphoreType.DMA((4,)),
        ],
        compiler_params=pltpu.CompilerParams(vmem_limit_bytes=40 << 20),
        name="signal",
    )(dither, last, recv, cos_t, sin_t, *[keep(t) for t in tables], keep(head), keep(gathers))


def rank_kernel(recv_ref, est_ref, w_hbm, out_hbm, ah_ref, al_ref, out_ref, w_ref, out_sem, w_sem):
    load_w = pltpu.make_async_copy(w_hbm, w_ref, w_sem)
    load_w.start()
    lane = lax.broadcasted_iota(jnp.int32, (NODES, 128), 1)
    chunk = lane // 32

    def planes(p):
        rows = pl.ds(aligned(p * NODES, NODES), NODES)
        values, extras = [], []
        for a in range(3):
            t = []
            for q in range(4):
                tile = recv_ref[pl.ds(aligned((p * 4 + q) * 24 + a * NODES, NODES), NODES), :]
                t.append(pltpu.roll(tile, (96 * q) % 128, axis=1) if q else tile)
            values.append([
                jnp.where(lane < 96, t[0], t[1]),
                jnp.where(lane < 64, t[1], t[2]),
                jnp.where(lane < 32, t[2], t[3]),
            ])
            e = jnp.where(chunk == 0, t[3], jnp.where(chunk == 1, t[2], jnp.where(chunk == 2, t[1], t[0])))
            extras.append(pltpu.roll(e, 32 * (a + 1), axis=1) if a < 3 else e)
        values.append([])
        for i in range(3):
            x = extras[(4 * i) % 3]
            for k in range(1, 4):
                x = jnp.where(chunk == k, extras[(4 * i + k) % 3], x)
            values[3].append(x)
        return [
            [est_ref[a, rows, i * 128 : (i + 1) * 128] + values[a][i] for i in range(3)] for a in range(4)
        ]

    def unpack(p):
        upper, lower = planes(2 * p), planes(2 * p + 1)
        rows = pl.ds(aligned(p * 16, 16), 16)
        for a in range(4):
            for i in range(3):
                hi, lo = split(jnp.concatenate([upper[a][i], lower[a][i]], 0))
                cols = slice((a % 2) * 384 + i * 128, (a % 2) * 384 + (i + 1) * 128)
                ah_ref[a // 2, rows, cols] = hi
                al_ref[a // 2, rows, cols] = lo

    @pl.loop(0, 4)
    def _(p):
        for i in range(4):
            unpack(4 * p + i)

    load_w.wait()

    dot = functools.partial(jnp.dot, preferred_element_type=f32)
    lane_r = lax.broadcasted_iota(jnp.int32, (64, 128), 1)
    row_r = lax.broadcasted_iota(jnp.int32, (64, 128), 0)
    flip = jnp.where(lane_r < 64, 1.0, -1.0).astype(f32)
    diagonal = (lane_r == row_r) & (row_r < RANK)
    systems = []
    rights = []
    basis = []
    for j in range(2):
        yy = dot(ah_ref[j], w_ref[...])
        y = yy[:, :128] + yy[:, 128:] + dot(al_ref[j], w_ref[:, :128])
        basis.append(y)
        yt = y.T
        g = jnp.dot(yt, y, precision=highest, preferred_element_type=f32)
        g = g[:64] + flip * pltpu.roll(g[64:], 64, axis=1)
        trace = jnp.sum(jnp.where(diagonal, g, 0.0))
        g = jnp.where(diagonal, g + RIDGE * trace / RANK, g)
        eye = jnp.where(diagonal, 1.0, 0.0).astype(f32)
        systems.append([g[:RANK], eye[:RANK]])
        yh, ym = split(yt)
        yl = (yt - yh.astype(f32) - ym.astype(f32)).astype(bf16)
        c = dot(jnp.concatenate([yh, ym, yl], 0), ah_ref[j])
        rest = dot(jnp.concatenate([yh, ym], 0), al_ref[j])
        c = c[:128] + ((c[128:256] + rest[:128]) + (c[256:] + rest[128:]))
        rights.append(jnp.concatenate([c[:64, :384] + c[64:, 384:], c[:64, 384:] - c[64:, :384]], 0))

    neg = jnp.where(lax.broadcasted_iota(jnp.int32, (NODES, 128), 1) < 64, -1.0, 1.0).astype(f32)
    row_i = lax.broadcasted_iota(jnp.int32, (NODES, 128), 0)
    groups = RANK // NODES
    state = [
        ([g[i * NODES : (i + 1) * NODES] for i in range(groups)], [w[i * NODES : (i + 1) * NODES] for i in range(groups)])
        for g, w in systems
    ]

    def row(x, k):
        return jnp.broadcast_to(x[k % NODES : k % NODES + 1], (NODES, 128))

    def column(x, k):
        return jnp.broadcast_to(x[:, k : k + 1], (NODES, 128))

    def gathered(x, k):
        return jnp.take_along_axis(x, jnp.full((NODES, 128), k, jnp.int32), axis=1)

    def turned(x):
        return neg * pltpu.roll(x, 64, axis=1)

    for k in range(0, RANK, 2):
        top = k // NODES
        for gs, ws in state:
            gt, wt = turned(gs[top]), turned(ws[top])
            cols = [
                [(gathered if i == top else column)(gs[i], c) for c in (k, 64 + k, k + 1, 65 + k)]
                for i in range(top, groups)
            ]
            a = row(cols[0][0], k)
            br, bi = row(cols[0][2], k), row(cols[0][3], k)
            d = row(cols[0][2], k + 1)
            ia = 1.0 / a
            lr, li = br * ia, -bi * ia
            second = 1.0 / (d - (br * br + bi * bi) * ia)
            g0, g0i, w0, w0i = row(gs[top], k), row(gt, k), row(ws[top], k), row(wt, k)
            g1 = row(gs[top], k + 1) - (lr * g0 + li * g0i)
            g1i = row(gt, k + 1) - (lr * g0i - li * g0)
            w1 = row(ws[top], k + 1) - (lr * w0 + li * w0i)
            w1i = row(wt, k + 1) - (lr * w0i - li * w0)
            for i in range(top, groups):
                c0r, c0i, c1r, c1i = cols[i - top]
                f0r, f0i = c0r * ia, c0i * ia
                f1r = (c1r - (f0r * br - f0i * bi)) * second
                f1i = (c1i - (f0r * bi + f0i * br)) * second
                if i == top:
                    f0r, f0i = jnp.where(row_i > k % NODES, f0r, 0.0), jnp.where(row_i > k % NODES, f0i, 0.0)
                    f1r, f1i = jnp.where(row_i > k % NODES + 1, f1r, 0.0), jnp.where(row_i > k % NODES + 1, f1i, 0.0)
                gs[i] = gs[i] - ((f0r * g0 + f0i * g0i) + (f1r * g1 + f1i * g1i))
                ws[i] = ws[i] - ((f0r * w0 + f0i * w0i) + (f1r * w1 + f1i * w1i))
    systems = [[jnp.concatenate(gs, 0), jnp.concatenate(ws, 0)] for gs, ws in state]

    stores = []
    for j in range(2):
        g, w = systems[j]
        d = jnp.sum(jnp.where(diagonal[:RANK], g, 0.0), axis=1, keepdims=True)
        w = w * lax.rsqrt(d)
        w = jnp.concatenate([w, jnp.zeros((16, 128), f32)], 0)
        left = jnp.concatenate([flip * w, pltpu.roll(w, 64, axis=1)], 0)
        v = jnp.dot(left, rights[j], precision=highest, preferred_element_type=f32)
        conj = jnp.concatenate([w, -flip * pltpu.roll(w, 64, axis=1)], 0)
        z = jnp.dot(basis[j], conj.T, precision=highest, preferred_element_type=f32)
        v = jnp.concatenate(
            [jnp.concatenate([v[:64], v[64:]], 1), jnp.concatenate([-v[64:], v[:64]], 1)], 0
        )
        vh, vl = split(v)
        zh, zl = split(z)
        low = dot(jnp.concatenate([zh, zl], 1), jnp.concatenate([vh, vh], 0)) + dot(zh, vl)
        for c in range(2):
            i = 2 * j + c
            out_ref[i] = low[:, 384 * c : 384 * (c + 1)]
            stores.append(pltpu.make_async_copy(out_ref.at[i], out_hbm.at[i], out_sem.at[i]))
            stores[-1].start()
    for store in stores:
        store.wait()


def rank_reduce(recv, est, w):
    vmem = pl.BlockSpec(memory_space=pltpu.VMEM)
    hbm = pl.BlockSpec(memory_space=pltpu.HBM)
    return pl.pallas_call(
        rank_kernel,
        in_specs=[vmem, vmem, hbm],
        out_specs=hbm,
        out_shape=pltpu.HBM((4, 256, 384), f32),
        scratch_shapes=[
            pltpu.VMEM((2, 256, 768), bf16),
            pltpu.VMEM((2, 256, 768), bf16),
            pltpu.VMEM((4, 256, 384), f32),
            pltpu.VMEM((768, 256), bf16),
            pltpu.SemaphoreType.DMA((4,)),
            pltpu.SemaphoreType.DMA,
        ],
        compiler_params=pltpu.CompilerParams(vmem_limit_bytes=20 << 20),
        name="rank",
    )(recv, est, keep(w))


def table(rows_first):
    half = FRAME // 2
    fine = 128 if rows_first else 64
    row = lax.iota(jnp.int32, 256)
    k = 2 * (row % 128) + row // 128 + 1
    near = 2 * lax.iota(jnp.int32, fine) + 1
    far = 2 * fine * lax.iota(jnp.int32, half // fine)
    if rows_first:
        phases = k[:, None] * near[None, :], k[:, None] * far[None, :]
    else:
        phases = near[:, None] * k[None, :], far[:, None] * k[None, :]
    angles = [math.pi / SPAN * (p % (2 * SPAN)).astype(f32) for p in phases]
    scale = 1.0 / math.sqrt(SPAN)
    cn, sn = jnp.cos(angles[0]) * scale, jnp.sin(angles[0]) * scale
    cf, sf = jnp.cos(angles[1]), jnp.sin(angles[1])
    cn, sn, cf, sf = lax.optimization_barrier((cn, sn, cf, sf))
    if rows_first:
        pieces = [
            (cn * cf[:, i : i + 1] - sn * sf[:, i : i + 1], -(sn * cf[:, i : i + 1] + cn * sf[:, i : i + 1]))
            for i in range(half // fine)
        ]
        value = jnp.stack([jnp.concatenate([p[j] for p in pieces], 1) for j in range(2)])
    else:
        cn, sn, cf, sf = cn[None], sn[None], cf[:, None], sf[:, None]
        value = jnp.stack([cn * cf - sn * sf, -(sn * cf + cn * sf)]).reshape(2, half, 256)
    hi = lax.reduce_precision(value, 8, 7)
    return hi.astype(bf16), (value - hi).astype(bf16)


def shards(receiver_gathers, fourier_estimate, random_projector, release_sample):
    q = lax.axis_index("freq")
    est = fourier_estimate.reshape(4, 32, NODES, 4 * SHOTS)
    send = pack(est).reshape(GROUP, ROWS // 2, 2, 128)
    recv = lax.all_to_all(send, ("node", "freq"), split_axis=0, concat_axis=0, tiled=True)

    up = [(0, 1), (1, 2), (2, 3)]
    down = [(1, 0), (2, 1), (3, 2)]
    starts = jnp.broadcast_to(jnp.pad(release_sample[:HALO].astype(f32), (0, 124))[None], (NODES, 128))
    head = lax.ppermute(
        jnp.concatenate([receiver_gathers[:, : HALO * FRAME], starts], 1), "freq", down
    )
    release_before = lax.ppermute(release_sample[SHOTS - HALO :], "freq", up)
    release_after = head[0, HALO * FRAME : HALO * FRAME + HALO].astype(jnp.int32)
    dither = jnp.concatenate([release_before, release_sample, release_after]) % FRAME
    src = lax.iota(jnp.int32, 256)
    k = 2 * (src % 128) + src // 128 + 1
    angle = math.pi / SPAN * (k[None, :] * (2 * dither - FRAME + 1)[:, None] % (2 * SPAN)).astype(f32)
    cos_t, sin_t = jnp.cos(angle), jnp.sin(angle)
    tables = table(True) + table(False)
    last = (q == 3).astype(jnp.int32).reshape(1)
    misfit, back = signal(dither, last, recv.reshape(GROUP * ROWS, 128), cos_t, sin_t, tables, head, receiver_gathers)

    arrived = lax.all_to_all(
        back.reshape(GROUP, 24, 128), ("node", "freq"), split_axis=0, concat_axis=0, tiled=True
    )
    omega = jnp.pad(random_projector, ((0, 0), (0, 16)))
    zero = jnp.zeros_like(omega)
    w = jnp.concatenate([jnp.concatenate([omega, zero], 1), jnp.concatenate([zero, omega], 1)], 0)
    hi = lax.reduce_precision(w, 8, 7)
    w = jnp.concatenate([hi.astype(bf16), (w - hi).astype(bf16)], 1)
    low = rank_reduce(arrived.reshape(GROUP * 24, 128), fourier_estimate.reshape(4, 256, 384), w)
    return low.reshape(2, 2, 256, 384), misfit


def solution(mesh):
    return jax.shard_map(
        shards,
        mesh=mesh,
        in_specs=(P("node", "freq"), P(("node", "freq"), None, None, None), P(), P("freq")),
        out_specs=(P(("node", "freq"), None, None, None), P("node", "freq")),
        check_vma=False,
    )
```
